128 devices in a mesh: dp: 4 (over z_hi, core), expert: 32 (over z_lo, y, x).
Axes of the slice: x: 4, y: 4, z: 4 (z_hi: 2, z_lo: 2; z = z_hi * 2 + z_lo), core: 2. Of those that a mesh axis runs over, the one named last changes fastest.
Arguments:
- queries: bfloat16 [1024, 4096], P(('dp', 'expert')), may hold values from -9 to 9
- kv_pool: bfloat16 [16384, 16, 1024], P(('dp', 'expert')), may hold values from -9 to 9
- page_table: int32 [1024, 4, 16], P(('dp', 'expert')), may hold values from 0 to 127
- held_tokens: int32 [1024, 4], P(('dp', 'expert')), may hold values from 1 to 256, as said below
- sinks: float32 [64], replicated, may hold values from 2 to 8
- residual: bfloat16 [1024, 2880], P(('dp', 'expert')), may hold values from -100 to 100
- route_ids: int32 [1024, 4], P(('dp', 'expert')), may hold values from 0 to 31, all different within a row; in each aligned block of 8 rows (0 to 7, 8 to 15, ...) at most 2 rows name the same one
- route_weights: float32 [1024, 4], P(('dp', 'expert')), may hold values from 0.1 to 1
- moe_gain: float32 [2880], replicated, may hold values from 0.25 to 1.75
- w_gate: bfloat16 [32, 2880, 1536], P('expert', None, 'dp')
- w_up: bfloat16 [32, 2880, 1536], P('expert', None, 'dp')
- w_down: bfloat16 [32, 1536, 2880], P('expert', 'dp'), may hold values from -0.078125 to 0.078125
- o_weight: bfloat16 [4096, 2880], P(None, 'dp'), may hold values from -0.09375 to 0.09375
- attn_gain: float32 [2880], replicated, may hold values from 0.25 to 1.75
- qkv_weight: bfloat16 [2880, 5120], P(None, 'dp'), may hold values from -0.109375 to 0.109375
Outputs:
- next_stream: bfloat16 [1024, 2880], P(('dp', 'expert'))
- next_qkv: bfloat16 [1024, 5120], P(('dp', 'expert'))
The draws below stay inside these ranges and needn't reach their ends.
Inputs may be any that keep to these rules, and one draw needn't show every extreme that they name: `route_ids`: each row names 4 different experts; among the 8 rows of one device no expert is named more than 2 times, a bound that some block reaches. `page_table`: pages may be shared between requests. `held_tokens`: the largest value is reached in every draw.
All inputs are finite; a program needn't handle non-finite values.
Results may differ from the reference program's by a relative error of at most 0.0145.
Values may be sent and summed in bfloat16 or wider, within the bound.
A program may use at most 128 MiB of HBM per device.

```python
import math
import jax
import jax.numpy as jnp
import numpy as np
from jax import lax

D = 2880
HEADS = 64
KVH = 8
HD = 64
TOP = 4
FF = 1536
PAGE = 16
PPH = 16
ROWS_DEV = 8
POOL_DEV = 128
EXPERTS = 32
CAP = 2
QKV = 5120
ROWS = 1024
POOL = 16384
N_DP = 4


def draw_queries(key, part):
    noise = jnp.clip(jax.random.normal(jax.random.fold_in(key, 1), (ROWS, HEADS * HD), jnp.float32), -4.0, 4.0)
    return noise.astype(jnp.bfloat16)


def draw_kv_pool(key, part):
    noise = jnp.clip(jax.random.normal(jax.random.fold_in(key, 2), (POOL, PAGE, 2 * KVH * HD), jnp.float32), -4.0, 4.0)
    return noise.astype(jnp.bfloat16)


def draw_held_tokens(key, part):
    limit = PPH * PAGE
    first_key, second_key = jax.random.split(jax.random.fold_in(key, 4))
    base = jax.random.randint(first_key, (ROWS, N_DP), 1, limit + 1)
    shifts = jax.random.randint(second_key, (ROWS, N_DP), 0, 4)
    held = jnp.maximum(base // jnp.power(2, shifts), 1)
    return held.at[0, 0].set(limit).astype(jnp.int32)


def draw_residual(key, part):
    keys = jax.random.split(jax.random.fold_in(key, 5), 3)
    row_scale = jnp.exp(jax.random.uniform(keys[0], (ROWS, 1), jnp.float32, 0.0, math.log(10.0)))
    column_scale = jnp.exp(jax.random.uniform(keys[1], (1, D), jnp.float32, -math.log(2.0), math.log(2.0)))
    base = jnp.clip(jax.random.normal(keys[2], (ROWS, D), jnp.float32), -5.0, 5.0)
    return (base * row_scale * column_scale).astype(jnp.bfloat16)


def expert_weight(key, salt):
    noise_key, scale_key = jax.random.split(jax.random.fold_in(key, salt))
    noise = jnp.clip(jax.random.normal(noise_key, (EXPERTS, D, FF), jnp.float32), -4.0, 4.0)
    column_scale = jnp.exp(jax.random.uniform(scale_key, (EXPERTS, 1, FF), jnp.float32, 0.0, math.log(8.0)))
    return (noise * column_scale * (1.0 / math.sqrt(D))).astype(jnp.bfloat16)


def draw_w_gate(key, part):
    return expert_weight(key, 21)


def draw_w_up(key, part):
    return expert_weight(key, 22)


def set_ends(values, key, smallest, largest):
    place = [jax.random.randint(jax.random.fold_in(key, axis), (), 0, length) for axis, length in enumerate(values.shape)]
    main_axis = values.shape.index(max(values.shape))
    next_to = place[:main_axis] + [(place[main_axis] + 1) % values.shape[main_axis]] + place[main_axis + 1:]
    return values.at[tuple(place)].set(smallest).at[tuple(next_to)].set(largest)


def steps_of(key, extent, shards, low, largest):
    level, own = 1.0, jax.random.fold_in(key, 6)
    for dim, blocks in shards:
        steps = jnp.exp(jax.random.uniform(jax.random.fold_in(own, dim), (blocks,), jnp.float32, low / len(shards), largest / len(shards)))
        level = level * jnp.repeat(steps, extent[dim] // blocks).reshape([-1 if axis == dim else 1 for axis in range(len(extent))])
    return level


def routed_block(key, own, number, rows, count, top, bound, slope):
    order = jax.random.permutation(key, count)
    crowded, usual = portions_of(count, rows * top, bound, slope, True), portions_of(count, rows * top, bound, slope, False)
    places = jnp.arange(count)

    def named(lengths, offset_by):
        used = int((lengths > 0).sum())
        fixed = max(1, used // 4)
        passed = fixed + (places - fixed + offset_by * (used - fixed)) % max(1, count - fixed)
        return jnp.zeros((count,), jnp.int32).at[order[jnp.where(places < fixed, places, passed)]].set(jnp.asarray(lengths, jnp.int32))

    lengths = jnp.where(number % 4 == 0, named(crowded, number // 4), named(usual, number - number // 4 - 1))
    mixed = jax.random.permutation(jax.random.fold_in(own, 3), count)
    giver, receiver = mixed[0:count // 2 * 2:2], mixed[1:count // 2 * 2:2]
    slack = jnp.minimum(lengths[giver] - 1, bound - lengths[receiver]) // 2
    slack = jnp.where((giver == order[0]) | (receiver == order[0]) | (lengths[receiver] == 0), 0, jnp.maximum(slack, 0))
    passed = jax.random.randint(jax.random.fold_in(own, 4), (count // 2,), 0, 1 << 20) % (slack + 1)
    lengths = lengths.at[giver].add(-passed).at[receiver].add(passed)
    labels = jnp.searchsorted(jnp.cumsum(lengths), jnp.arange(rows * top), side="right").astype(jnp.int32)
    listing = labels.reshape(top, rows).T
    listing = listing[jax.random.permutation(jax.random.fold_in(own, 1), rows)]
    offset_by = jax.random.randint(jax.random.fold_in(own, 2), (rows, 1), 0, top)
    return jnp.take_along_axis(listing, (jnp.arange(top)[None, :] + offset_by) % top, axis=1)


def portions_of(count, total, bound, skew, full):
    portions = [(1 << 20) // math.isqrt(rank ** skew) + 1 for rank in range(1, count + 1)]
    largest = bound if full else min(bound, max(-(-total // count), total * portions[0] // sum(portions)))
    least = 1 if total - largest >= count - 1 else 0
    given, rest = [largest] + [least] * (count - 1), total - largest - least * (count - 1)
    while rest > 0:
        movable = [i for i in range(1, count) if given[i] < largest] or [i for i in range(1, count) if given[i] < bound]
        mass, remaining = sum([portions[i] for i in movable]), rest
        for i in movable:
            addition = min(bound - given[i], max(1, remaining * portions[i] // mass), rest)
            given[i] = given[i] + addition
            rest = rest - addition
    return np.array(given)


def scatter_about(own_key, dims, width, most, shards=(), kind=jnp.bfloat16):
    drawn = jax.random.normal(own_key, dims, jnp.float32) * width
    if len(shards) > 0:
        drawn = steps_of(own_key, dims, shards, -0.22, 0.18) * drawn
    return jnp.clip(drawn, min=-most, max=most).astype(kind)


def setup_inputs(seed: int = 0) -> dict:
    streams_of = jax.random.split(jax.random.key(seed), 16)
    queries = draw_queries(jax.random.fold_in(streams_of[15], 71), 0)
    kv_pool = draw_kv_pool(jax.random.fold_in(streams_of[15], 71), 0)
    page_table = set_ends(jax.random.randint(streams_of[2], (ROWS, N_DP, PPH), 0, POOL_DEV), jax.random.fold_in(streams_of[2], 1), 0, POOL_DEV - 1).astype(jnp.int32)
    held_tokens = draw_held_tokens(jax.random.fold_in(streams_of[15], 71), 0)
    sinks = jnp.clip(jax.random.uniform(streams_of[4], (HEADS,), jnp.float32, 2.0, 8.0), 2.0, 8.0)
    residual = draw_residual(jax.random.fold_in(streams_of[15], 71), 0)
    route_ids_keys = jax.random.split(jax.random.fold_in(streams_of[6], 1), ROWS // ROWS_DEV)
    route_ids_turns = jax.random.permutation(jax.random.fold_in(streams_of[6], 3), ROWS // ROWS_DEV)
    route_ids = jax.vmap(lambda own, number: routed_block(jax.random.fold_in(streams_of[6], 2), own, number, ROWS_DEV, EXPERTS, TOP, CAP, 2))(route_ids_keys, route_ids_turns).reshape((ROWS, TOP))
    route_weights = jnp.clip(jnp.exp(math.log(1.0) - 2.3025851 * jax.random.uniform(streams_of[7], (ROWS, TOP), jnp.float32) ** steps_of(streams_of[7], (ROWS, TOP), ((0, 128),), -0.2, 0.2)), 0.1, 1.0)
    moe_gain = jnp.clip(1.0 + 0.15 * jax.random.normal(streams_of[8], (D,), jnp.float32), 0.25, 1.75)
    w_gate = draw_w_gate(jax.random.fold_in(streams_of[15], 71), 0)
    w_up = draw_w_up(jax.random.fold_in(streams_of[15], 71), 0)
    w_down = scatter_about(streams_of[11], (EXPERTS, FF, D), (4 * FF) ** -0.5, 0.078125, ((0, 32), (1, 4)))
    o_weight = scatter_about(streams_of[12], (HEADS * HD, D), (HEADS * HD) ** -0.5, 0.09375, ((1, 4),))
    attn_gain = jnp.clip(1.0 + 0.15 * jax.random.normal(streams_of[13], (D,), jnp.float32), 0.25, 1.75)
    qkv_weight = scatter_about(streams_of[14], (D, QKV), D ** -0.5, 0.109375, ((1, 4),))
    return {"queries": queries, "kv_pool": kv_pool, "page_table": page_table, "held_tokens": held_tokens, "sinks": sinks, "residual": residual, "route_ids": route_ids, "route_weights": route_weights, "moe_gain": moe_gain, "w_gate": w_gate, "w_up": w_up, "w_down": w_down, "o_weight": o_weight, "attn_gain": attn_gain, "qkv_weight": qkv_weight}


EPSILON = 1e-05
LIMIT = 7.0

def rms_scale(values, gain):
    wide = values.astype(jnp.float32)
    scale = lax.rsqrt(lax.optimization_barrier(jnp.mean(wide * wide, axis=-1, keepdims=True)) + EPSILON)
    return (wide * scale * gain).astype(jnp.bfloat16)

def holder_block(query_rows, fetched, count_rows):
    blocks = query_rows.shape[0]
    groups = HEADS // KVH
    token_span = PPH * PAGE
    fetched = fetched.reshape(blocks, token_span, 2, KVH, HD)
    keys_part = fetched[:, :, 0].astype(jnp.float32)
    values_part = fetched[:, :, 1].astype(jnp.float32)
    query_heads = query_rows.reshape(blocks, KVH, groups, HD).astype(jnp.float32)
    scores = jnp.einsum('bgjd,blgd->bgjl', query_heads, keys_part, precision=lax.Precision.HIGHEST) * (1.0 / math.sqrt(HD))
    usable = (jnp.arange(token_span, dtype=jnp.int32)[None, :] < count_rows[:, None])[:, None, None, :]
    highest = lax.optimization_barrier(jnp.max(jnp.where(usable, scores, -1e+30), axis=-1))
    weights = jnp.where(usable, jnp.exp(scores - highest[..., None]), 0.0)
    totals = lax.optimization_barrier(jnp.sum(weights, axis=-1))
    rounded = lax.optimization_barrier(weights.astype(jnp.bfloat16)).astype(jnp.float32)
    numerator = jnp.einsum('bgjl,blgd->bgjd', rounded, values_part, precision=lax.Precision.HIGHEST)
    return (highest.reshape(blocks, HEADS), totals.reshape(blocks, HEADS), numerator.reshape(blocks, HEADS, HD))

def expert_apply(rows, gate_w, up_w, down_w):
    gate_proj = jnp.minimum(jnp.dot(rows, gate_w, preferred_element_type=jnp.float32), LIMIT)
    up_proj = jnp.clip(jnp.dot(rows, up_w, preferred_element_type=jnp.float32), -LIMIT, LIMIT)
    activated = (gate_proj * jax.nn.sigmoid(1.702 * gate_proj) * (up_proj + 1.0)).astype(jnp.bfloat16)
    return jnp.dot(activated, down_w, preferred_element_type=jnp.float32)

def reference(queries, kv_pool, page_table, held_tokens, sinks, residual, route_ids, route_weights, moe_gain, w_gate, w_up, w_down, o_weight, attn_gain, qkv_weight):
    block_rows = 32
    block_total = ROWS // block_rows

    def attention_block(items):
        query_rows, table_rows, held_rows, index = items
        row_ids = index * block_rows + jnp.arange(block_rows, dtype=jnp.int32)
        group = row_ids // ROWS_DEV % EXPERTS
        parts = []
        for holder in range(N_DP):
            pages = (holder * EXPERTS + group)[:, None] * POOL_DEV + table_rows[:, holder, :]
            fetched = kv_pool[pages.astype(jnp.int32)]
            parts.append(holder_block(query_rows, fetched, held_rows[:, holder]))
        ceiling = sinks[None, :].astype(jnp.float32)
        for part_item in parts:
            ceiling = jnp.maximum(ceiling, part_item[0])
        denominator = jnp.exp(sinks[None, :] - ceiling)
        numerator = jnp.zeros((block_rows, HEADS, HD), jnp.float32)
        for part_item in parts:
            kept = jnp.exp(part_item[0] - ceiling)
            denominator = denominator + part_item[1] * kept
            numerator = numerator + part_item[2] * kept[..., None]
        return (numerator / denominator[..., None]).reshape(block_rows, HEADS * HD).astype(jnp.bfloat16)
    attention = lax.map(attention_block, (queries.reshape(block_total, block_rows, HEADS * HD), page_table.reshape(block_total, block_rows, N_DP, PPH), held_tokens.reshape(block_total, block_rows, N_DP), jnp.arange(block_total, dtype=jnp.int32)))
    attention = attention.reshape(ROWS, HEADS * HD)
    projected = jnp.dot(attention, o_weight, preferred_element_type=jnp.float32).astype(jnp.bfloat16)
    stream = (residual.astype(jnp.float32) + projected.astype(jnp.float32)).astype(jnp.bfloat16)
    moe_input = rms_scale(stream, moe_gain)
    slab_rows = 256
    assigned = ROWS * TOP
    flat_ids = route_ids.reshape(assigned)
    order = jnp.argsort(flat_ids, stable=True).astype(jnp.int32)
    counts = lax.optimization_barrier(jnp.sum((flat_ids[:, None] == jnp.arange(EXPERTS, dtype=jnp.int32)[None, :]).astype(jnp.int32), axis=0))
    offsets = jnp.cumsum(counts) - counts
    source_rows = jnp.concatenate([order // TOP, jnp.zeros((slab_rows,), jnp.int32)])

    def per_expert(expert, outputs):
        begin = offsets[expert]
        amount = counts[expert]

        def per_slab(slab, inner):
            position = (begin + slab * slab_rows).astype(jnp.int32)
            picks = lax.dynamic_slice_in_dim(source_rows, position, slab_rows, 0)
            result = expert_apply(moe_input[picks], w_gate[expert], w_up[expert], w_down[expert])
            live = jnp.arange(slab_rows, dtype=jnp.int32) + slab * slab_rows < amount
            result = jnp.where(live[:, None], result, 0.0)
            return lax.dynamic_update_slice_in_dim(inner, result, position, 0)
        return lax.fori_loop(0, (amount + slab_rows - 1) // slab_rows, per_slab, outputs)
    sorted_out = lax.fori_loop(0, EXPERTS, per_expert, jnp.zeros((assigned + slab_rows, D), jnp.float32))
    by_assignment = jnp.zeros((assigned, D), jnp.float32).at[order].set(sorted_out[:assigned])
    route_share = route_weights / lax.optimization_barrier(jnp.sum(route_weights, axis=1, keepdims=True))
    moe_out = lax.optimization_barrier(jnp.sum(by_assignment.reshape(ROWS, TOP, D) * route_share[:, :, None], axis=1))
    next_stream = (stream.astype(jnp.float32) + moe_out).astype(jnp.bfloat16)
    qkv_input = rms_scale(next_stream, attn_gain)
    next_qkv = jnp.dot(qkv_input, qkv_weight, preferred_element_type=jnp.float32).astype(jnp.bfloat16)
    return (next_stream, next_qkv)
```

```python
import math

import jax
import jax.numpy as jnp
from jax import lax
from jax.experimental import pallas as pl
from jax.experimental.pallas import tpu as pltpu
from jax.sharding import PartitionSpec as P

HEADS = 64
KVH = 8
HD = 64
TOP = 4
PAGE = 16
PPH = 16
SPAN = PPH * PAGE
WIDE = KVH * HD
PAIR = 2 * HD
ROWS = 8
NDP = 4

EPSILON = 1e-05
LIMIT = 7.0
MESH = pl.DeviceIdType.MESH
F32 = jnp.float32
BF16 = jnp.bfloat16

S_TAB, S_Q, S_RES, S_COM, S_PAIR_N, S_PAIR_ML, S_X_N, S_X_ML, S_LHS, S_PROJ = 0, 3, 6, 9, 12, 14, 16, 18, 19, 20
N_SEM_A = 23


def rms_scale(values, gain):
    wide = values.astype(jnp.float32)
    scale = lax.rsqrt(jnp.mean(wide * wide, axis=-1, keepdims=True) + EPSILON)
    return (wide * scale * gain).astype(jnp.bfloat16)


def position():
    dp = lax.axis_index("dp")
    expert = lax.axis_index("expert")
    return dp, lax.div(dp, 2), lax.rem(dp, 2), expert


def group_peer(z, c, offset):
    return lax.rem(z + offset // 2, 2) * 2 + lax.rem(c + offset % 2, 2)


def remote(src, dst, sems, sent, landed, device):
    return pltpu.make_async_remote_copy(
        src_ref=src,
        dst_ref=dst,
        send_sem=sems[0].at[sent],
        recv_sem=sems[1].at[landed],
        device_id=device,
        device_id_type=MESH,
    )


def spread_queries(query):
    wide = query.astype(F32)
    turned = pltpu.roll(wide, HD, 1)
    row = lax.broadcasted_iota(jnp.int32, (HEADS // 2, PAIR), 0)
    lane = lax.broadcasted_iota(jnp.int32, (HEADS // 2, PAIR), 1)
    odd_group = lax.rem(lax.div(row, 4), 2) == 1
    own_half = (lane >= HD) == odd_group
    even = jnp.where(own_half, jnp.where(odd_group, turned, wide), 0.0)
    odd = jnp.where(own_half, jnp.where(odd_group, wide, turned), 0.0)
    tile = lax.div(row, 8)
    parts = []
    for heads in (even, odd):
        parts.append(jnp.concatenate([jnp.where(tile == t, heads, 0.0) for t in range(4)], axis=1))
    return jnp.concatenate(parts, axis=0).astype(BF16)


def fold_values(wide):
    row = lax.broadcasted_iota(jnp.int32, (HEADS // 2, PAIR), 0)
    lane = lax.broadcasted_iota(jnp.int32, (HEADS // 2, PAIR), 1)
    odd_group = lax.rem(lax.div(row, 4), 2) == 1

    def own_tiles(base):
        return jnp.concatenate(
            [wide[base + 8 * t : base + 8 * t + 8, PAIR * t : PAIR * t + PAIR] for t in range(4)], axis=0
        )

    even, odd = own_tiles(0), own_tiles(HEADS // 2)
    even = jnp.where(odd_group, pltpu.roll(even, HD, 1), even)
    odd = jnp.where(odd_group, odd, pltpu.roll(odd, HD, 1))
    return jnp.where(lane < HD, even, odd)


def pair_columns(column):
    lane = lax.broadcasted_iota(jnp.int32, (HEADS // 2, PAIR), 1)
    return jnp.where(lane < HD, column[: HEADS // 2], column[HEADS // 2 :])


def attend(queries, tables, pool, rows, write):
    token = lax.broadcasted_iota(jnp.int32, (HEADS, SPAN), 1)
    scores, held = [], []
    for row in rows:
        keys = jnp.concatenate([pool[tables[row, page], :, :WIDE] for page in range(PPH)], axis=0)
        spread = spread_queries(queries[row])
        scores.append(
            lax.dot_general(spread, keys, (((1,), (1,)), ((), ())), preferred_element_type=F32)
            * (1.0 / math.sqrt(HD))
        )
        held.append(token < tables[row, PPH])
    weights, highs, sums = [], [], []
    for score, usable in zip(scores, held):
        high = jnp.max(jnp.where(usable, score, -1e30), axis=1, keepdims=True)
        weight = jnp.where(usable, jnp.exp(score - high), 0.0)
        highs.append(high)
        sums.append(jnp.sum(weight, axis=1, keepdims=True))
        weights.append(weight.astype(BF16))
    results = []
    for row, weight in zip(rows, weights):
        values = jnp.concatenate([pool[tables[row, page], :, WIDE:] for page in range(PPH)], axis=0)
        results.append(fold_values(jnp.dot(weight, values, preferred_element_type=F32)))
    for row, result, high, total in zip(rows, results, highs, sums):
        write(row, result, high, total)


STEP = 4


def attention_kernel(
    q_ref, tab_ref, sink_ref, res_ref, com_ref, pool_hbm, ow_hbm,
    stream_ref, com_out,
    pool, ow, qall, tabv, tabs, resall, comall, keep_n, keep_ml, send_n, send_ml, recv_n, recv_ml,
    xs_n, xs_ml, xr_n, xr_ml, att, lhs, pall, load_sem, tab_sem, send_sem, recv_sem,
):
    dp, z, c, expert = position()
    sems = (send_sem, recv_sem)
    loads = [pltpu.make_async_copy(pool_hbm, pool, load_sem.at[0]), pltpu.make_async_copy(ow_hbm, ow, load_sem.at[1])]
    for load in loads:
        load.start()

    barrier = pltpu.get_barrier_semaphore()
    for offset in (1, 2, 3):
        pl.semaphore_signal(barrier, inc=1, device_id=(group_peer(z, c, offset), expert), device_id_type=MESH)
    own_tab = pltpu.make_async_copy(tab_ref.at[dp], tabs.at[dp], tab_sem.at[0])
    own_tab.start()
    block = c * 2 + z
    qall[dp] = q_ref[...]
    resall[block] = res_ref[...]
    comall[block] = com_ref[...]
    pl.semaphore_wait(barrier, 3)

    sent = []

    def send(src, dst, number, landed, offset):
        copy = remote(src, dst, sems, number, landed, (group_peer(z, c, offset), expert))
        copy.start()
        sent.append(copy)
        return copy

    tab_in, q_in, res_in, com_in = {}, {}, {}, {}
    for offset in (2, 3, 1):
        peer = group_peer(z, c, offset)
        tab_in[offset] = send(tab_ref.at[peer], tabv.at[dp], S_TAB + offset - 1, S_TAB + offset - 1, offset)
        q_in[offset] = send(q_ref, qall.at[dp], S_Q + offset - 1, S_Q + offset - 1, offset)
    for offset in (2, 3, 1):
        res_in[offset] = send(res_ref, resall.at[block], S_RES + offset - 1, S_RES + offset - 1, offset)
        com_in[offset] = send(com_ref, comall.at[block], S_COM + offset - 1, S_COM + offset - 1, offset)

    lane = lax.broadcasted_iota(jnp.int32, (HEADS, PAIR), 1)

    def run_block(offset, number, numerators, stats):
        at = group_peer(z, c, offset)
        half = z if number == 0 else 1 - z
        stats[number] = jnp.zeros((HEADS, PAIR), F32)

        def write(row, result, high, total):
            numerators[number, row] = result.astype(numerators.dtype)
            place = half * ROWS + row
            tile = jnp.where(lane == place, high, stats[number])
            stats[number] = jnp.where(lane == place + HD, total, tile)

        def step(index, carry):
            rows = [index * STEP + i for i in range(STEP)]
            attend(qall.at[at], tabs.at[at], pool, rows, write)
            return carry

        lax.fori_loop(0, ROWS // STEP, step, 0)

    def fetch_block(offset):
        at = group_peer(z, c, offset)
        tab_in[offset].wait_recv()
        copy = pltpu.make_async_copy(tabv.at[at], tabs.at[at], tab_sem.at[offset])
        copy.start()
        q_in[offset].wait_recv()
        copy.wait()

    def send_pair(number):
        return (
            send(send_n.at[number], recv_n.at[number], S_PAIR_N + number, S_PAIR_N + number, 1),
            send(send_ml.at[number], recv_ml.at[number], S_PAIR_ML + number, S_PAIR_ML + number, 1),
        )

    def factors(tile, number):
        half = z if number == 0 else 1 - z
        return pltpu.roll(tile, lax.rem(PAIR - half * ROWS, PAIR), 1)

    def merge_pair(number, incoming):
        for copy in incoming:
            copy.wait_recv()
        mine, other = keep_ml[number], recv_ml[number]
        high = jnp.maximum(mine, other)
        left, right = jnp.exp(mine - high), jnp.exp(other - high)
        total = mine * pltpu.roll(left, HD, 1) + other * pltpu.roll(right, HD, 1)
        keep_ml[number] = jnp.where(lane < HD, high, total)
        left, right = factors(left, number), factors(right, number)
        for row in range(ROWS):
            merged = keep_n[number, row] * pair_columns(left[:, row : row + 1]) + recv_n[number, row].astype(
                F32
            ) * pair_columns(right[:, row : row + 1])
            keep_n[number, row] = merged
            xs_n[number, row] = merged.astype(BF16)
        return send(xs_n.at[number], xr_n.at[1 - number], S_X_N + number, S_X_N + 1 - number, 2)

    own_tab.wait()
    loads[0].wait()
    run_block(0, 0, keep_n, keep_ml)
    fetch_block(1)
    run_block(1, 0, send_n, send_ml)
    pair_in = [send_pair(0)]
    fetch_block(3)
    run_block(3, 1, send_n, send_ml)
    pair_in.append(send_pair(1))
    cross_in = [merge_pair(0, pair_in[0])]
    fetch_block(2)
    run_block(2, 1, keep_n, keep_ml)
    cross_in.append(merge_pair(1, pair_in[1]))
    xs_ml[...] = keep_ml[0] + keep_ml[1]
    cross_ml = send(xs_ml, xr_ml, S_X_ML, S_X_ML, 2)

    cross_ml.wait_recv()
    mine, other, sink = xs_ml[...], xr_ml[...], sink_ref[...]
    top = jnp.maximum(jnp.maximum(mine, other), sink)
    left, right = jnp.exp(mine - top), jnp.exp(other - top)
    total = mine * pltpu.roll(left, HD, 1) + other * pltpu.roll(right, HD, 1)
    below = pltpu.roll(total, HD, 1) + jnp.exp(sink - top)
    left, right = left / below, right / below
    for number in (0, 1):
        cross_in[1 - number].wait_recv()
        one, two = factors(left, number), factors(right, number)
        half = z if number == 0 else 1 - z
        for row in range(ROWS):
            attention = keep_n[number, row] * pair_columns(one[:, row : row + 1]) + xr_n[number, row].astype(
                F32
            ) * pair_columns(two[:, row : row + 1])
            start = pl.multiple_of((half * ROWS + row) * (HEADS // 2), HEADS // 2)
            att[pl.ds(start, HEADS // 2), :] = attention
    for pair in range(HEADS // 2):
        lhs[c, :, PAIR * pair : PAIR * pair + PAIR] = att[pl.ds(pair, 2 * ROWS, stride=HEADS // 2), :].astype(BF16)
    lhs_in = send(lhs.at[c], lhs.at[c], S_LHS, S_LHS, 1)
    loads[1].wait()
    lhs_in.wait_recv()
    rows = jnp.concatenate([lhs[0], lhs[1]], axis=0)
    projected = lax.dot_general(rows, ow[...], (((1,), (1,)), ((), ())), preferred_element_type=F32)
    pall[dp] = projected.astype(BF16)
    proj_in = [
        send(pall.at[dp], pall.at[dp], S_PROJ + offset - 1, S_PROJ + offset - 1, offset) for offset in (2, 3, 1)
    ]
    for offset in (1, 2, 3):
        res_in[offset].wait_recv()
        com_in[offset].wait_recv()
    com_out[...] = comall[...]
    for copy in proj_in:
        copy.wait_recv()
    for k in range(NDP):
        residual = jnp.concatenate([resall[d, k].astype(F32) for d in range(NDP)], axis=0)
        stream_ref[k] = (residual + pall[k].astype(F32)).astype(BF16)
    for copy in sent:
        copy.wait_send()


def head_order(values):
    return values.reshape(HEADS // 2, 2).T.reshape(HEADS, 1)


def attention_call(queries, kv_pool, page_table, held_tokens, sinks, residual, combine, o_weight):
    width = residual.shape[1] // NDP
    q_pairs = queries.reshape(ROWS, HEADS // 2, PAIR)
    table = jnp.concatenate([page_table, held_tokens[:, :, None]], axis=2).transpose(1, 0, 2)
    table = jnp.pad(table, ((0, 0), (0, 0), (0, 128 - PPH - 1)))
    sink_tile = jnp.broadcast_to(head_order(sinks), (HEADS, PAIR))
    residual_blocks = residual.reshape(ROWS, NDP, width).transpose(1, 0, 2)
    vmem = pl.BlockSpec(memory_space=pltpu.VMEM)
    hbm = pl.BlockSpec(memory_space=pl.ANY)
    slots = combine.shape[1]
    return pl.pallas_call(
        attention_kernel,
        out_shape=(
            jax.ShapeDtypeStruct((NDP, NDP * ROWS, width), BF16),
            jax.ShapeDtypeStruct((NDP, ROWS, slots), F32),
        ),
        in_specs=[vmem] * 5 + [hbm] * 2,
        out_specs=(vmem, vmem),
        scratch_shapes=[
            pltpu.VMEM(kv_pool.shape, BF16),
            pltpu.VMEM((width, HEADS * HD), BF16),
            pltpu.VMEM((NDP, ROWS, HEADS // 2, PAIR), BF16),
            pltpu.VMEM((NDP, ROWS, 128), jnp.int32),
            pltpu.SMEM((NDP, ROWS, 128), jnp.int32),
            pltpu.VMEM((NDP, NDP, ROWS, width), BF16),
            pltpu.VMEM((NDP, ROWS, slots), F32),
            pltpu.VMEM((2, ROWS, HEADS // 2, PAIR), F32),
            pltpu.VMEM((2, HEADS, PAIR), F32),
            pltpu.VMEM((2, ROWS, HEADS // 2, PAIR), BF16),
            pltpu.VMEM((2, HEADS, PAIR), F32),
            pltpu.VMEM((2, ROWS, HEADS // 2, PAIR), BF16),
            pltpu.VMEM((2, HEADS, PAIR), F32),
            pltpu.VMEM((2, ROWS, HEADS // 2, PAIR), BF16),
            pltpu.VMEM((HEADS, PAIR), F32),
            pltpu.VMEM((2, ROWS, HEADS // 2, PAIR), BF16),
            pltpu.VMEM((HEADS, PAIR), F32),
            pltpu.VMEM((2 * ROWS * HEADS // 2, PAIR), F32),
            pltpu.VMEM((2, 2 * ROWS, HEADS * HD), BF16),
            pltpu.VMEM((NDP, NDP * ROWS, width), BF16),
            pltpu.SemaphoreType.DMA((2,)),
            pltpu.SemaphoreType.DMA((4,)),
            pltpu.SemaphoreType.DMA((N_SEM_A,)),
            pltpu.SemaphoreType.DMA((N_SEM_A,)),
        ],
        compiler_params=pltpu.CompilerParams(collective_id=0, has_side_effects=True, vmem_limit_bytes=50 * 2**20),
        name="attention",
    )(q_pairs, table, sink_tile, residual_blocks, combine, kv_pool, o_weight.T)


def expert_apply(rows, gate_w, up_w, down_w):
    gate_proj = jnp.minimum(jnp.dot(rows, gate_w, preferred_element_type=jnp.float32), LIMIT)
    up_proj = jnp.clip(jnp.dot(rows, up_w, preferred_element_type=jnp.float32), -LIMIT, LIMIT)
    activated = (gate_proj * jax.nn.sigmoid(1.702 * gate_proj) * (up_proj + 1.0)).astype(
        jnp.bfloat16
    )
    return jnp.dot(activated, down_w, preferred_element_type=jnp.float32)


def combine_table(route_ids, route_weights, experts_count, capacity, block):
    rows = route_ids.shape[0]
    experts = jnp.arange(experts_count, dtype=jnp.int32)
    chosen = route_ids[:, :, None] == experts[None, None, :]
    share = route_weights / jnp.sum(route_weights, axis=1, keepdims=True)
    shares = jnp.sum(jnp.where(chosen, share[:, :, None], 0.0), axis=1)
    hit = jnp.any(chosen, axis=1)
    earlier = jnp.arange(rows)[:, None] > jnp.arange(rows)[None, :]
    slot = jnp.sum(jnp.where(earlier[:, :, None] & hit[None, :, :], 1, 0), axis=1)
    column = jnp.arange(NDP * capacity, dtype=jnp.int32)[None, None, :]
    table = jnp.where(hit[:, :, None] & (column == (block * capacity + slot)[:, :, None]), shares[:, :, None], 0.0)
    return table.reshape(rows, experts_count * NDP * capacity)


def body(
    queries,
    kv_pool,
    page_table,
    held_tokens,
    sinks,
    residual,
    route_ids,
    route_weights,
    moe_gain,
    w_gate,
    w_up,
    w_down,
    o_weight,
    attn_gain,
    qkv_weight,
):
    dp_count = lax.axis_size("dp")
    experts_count = lax.axis_size("expert")
    own_rows = queries.shape[0]
    holder = lax.axis_index("dp")
    block = lax.rem(holder, 2) * 2 + lax.div(holder, 2)
    capacity = 2 * own_rows * TOP // experts_count
    table = combine_table(route_ids, route_weights, experts_count, capacity, block)
    streams, tables = attention_call(
        queries, kv_pool, page_table, held_tokens, sinks, residual, table, o_weight
    )
    stream = lax.dynamic_slice_in_dim(streams, block * own_rows, own_rows, 1)
    stream = stream.transpose(1, 0, 2).reshape(own_rows, -1)
    moe_input = rms_scale(stream, moe_gain)
    own = lax.dynamic_index_in_dim(tables, block, 0, keepdims=False)
    own = own.reshape(own_rows, experts_count, NDP, capacity)
    combine = jnp.sum(own, axis=2).reshape(own_rows, experts_count * capacity)
    dispatch = (combine > 0).astype(jnp.bfloat16)
    send_rows = jnp.einsum(
        "rc,rd->cd", dispatch, moe_input, preferred_element_type=jnp.float32
    ).astype(jnp.bfloat16)
    gate_local = w_gate[0]
    up_local = w_up[0]
    down_local = w_down[0]
    copies = jnp.broadcast_to(send_rows[None], (dp_count,) + send_rows.shape).reshape(
        dp_count * send_rows.shape[0], send_rows.shape[1]
    )
    arrived = lax.all_to_all(copies, ("dp", "expert"), split_axis=0, concat_axis=0, tiled=True)
    partial_value = expert_apply(arrived, gate_local, up_local, down_local)
    came_back = lax.all_to_all(
        partial_value.astype(jnp.bfloat16),
        ("dp", "expert"),
        split_axis=0,
        concat_axis=0,
        tiled=True,
    ).astype(partial_value.dtype)
    returned = jnp.sum(came_back.reshape(dp_count, send_rows.shape[0], send_rows.shape[1]), axis=0)
    moe_out = jnp.dot(
        combine, returned, precision=lax.Precision.HIGHEST, preferred_element_type=jnp.float32
    )
    next_stream = (stream.astype(jnp.float32) + moe_out).astype(jnp.bfloat16)
    qkv_input = rms_scale(next_stream, attn_gain)
    group_qkv = jnp.dot(
        lax.all_gather(qkv_input, "dp", axis=0, tiled=True),
        qkv_weight,
        preferred_element_type=jnp.float32,
    ).astype(jnp.bfloat16)
    next_qkv = lax.all_to_all(group_qkv, "dp", split_axis=0, concat_axis=1, tiled=True)
    return (next_stream, next_qkv)


def solution(mesh):
    in_specs = (
        P(("dp", "expert"), None),
        P(("dp", "expert"), None, None),
        P(("dp", "expert"), None, None),
        P(("dp", "expert"), None),
        P(),
        P(("dp", "expert"), None),
        P(("dp", "expert"), None),
        P(("dp", "expert"), None),
        P(),
        P("expert", None, "dp"),
        P("expert", None, "dp"),
        P("expert", "dp", None),
        P(None, "dp"),
        P(),
        P(None, "dp"),
    )
    out_specs = (P(("dp", "expert"), None), P(("dp", "expert"), None))
    return jax.shard_map(body, mesh=mesh, in_specs=in_specs, out_specs=out_specs, check_vma=False)
```

```python
import math

import jax
import jax.numpy as jnp
from jax import lax
from jax.experimental import pallas as pl
from jax.experimental.pallas import tpu as pltpu
from jax.sharding import PartitionSpec as P

HEADS = 64
KVH = 8
HD = 64
TOP = 4
PAGE = 16
PPH = 16
SPAN = PPH * PAGE
WIDE = KVH * HD
PAIR = 2 * HD
ROWS = 8
NDP = 4

EPSILON = 1e-05
LIMIT = 7.0
MESH = pl.DeviceIdType.MESH
F32 = jnp.float32
BF16 = jnp.bfloat16

S_TAB, S_Q, S_RES, S_COM, S_PAIR_N, S_PAIR_ML, S_X_N, S_X_ML, S_LHS, S_PROJ = 0, 3, 6, 9, 12, 14, 16, 18, 19, 20
N_SEM_A = 23


def position():
    dp = lax.axis_index("dp")
    expert = lax.axis_index("expert")
    return dp, lax.div(dp, 2), lax.rem(dp, 2), expert


def group_peer(z, c, offset):
    return lax.rem(z + offset // 2, 2) * 2 + lax.rem(c + offset % 2, 2)


def remote(src, dst, sems, sent, landed, device):
    return pltpu.make_async_remote_copy(
        src_ref=src,
        dst_ref=dst,
        send_sem=sems[0].at[sent],
        recv_sem=sems[1].at[landed],
        device_id=device,
        device_id_type=MESH,
    )


def spread_queries(query):
    wide = query.astype(F32)
    turned = pltpu.roll(wide, HD, 1)
    row = lax.broadcasted_iota(jnp.int32, (HEADS // 2, PAIR), 0)
    lane = lax.broadcasted_iota(jnp.int32, (HEADS // 2, PAIR), 1)
    odd_group = lax.rem(lax.div(row, 4), 2) == 1
    own_half = (lane >= HD) == odd_group
    even = jnp.where(own_half, jnp.where(odd_group, turned, wide), 0.0)
    odd = jnp.where(own_half, jnp.where(odd_group, wide, turned), 0.0)
    tile = lax.div(row, 8)
    parts = []
    for heads in (even, odd):
        parts.append(jnp.concatenate([jnp.where(tile == t, heads, 0.0) for t in range(4)], axis=1))
    return jnp.concatenate(parts, axis=0).astype(BF16)


def fold_values(wide):
    row = lax.broadcasted_iota(jnp.int32, (HEADS // 2, PAIR), 0)
    lane = lax.broadcasted_iota(jnp.int32, (HEADS // 2, PAIR), 1)
    odd_group = lax.rem(lax.div(row, 4), 2) == 1

    def own_tiles(base):
        return jnp.concatenate(
            [wide[base + 8 * t : base + 8 * t + 8, PAIR * t : PAIR * t + PAIR] for t in range(4)], axis=0
        )

    even, odd = own_tiles(0), own_tiles(HEADS // 2)
    even = jnp.where(odd_group, pltpu.roll(even, HD, 1), even)
    odd = jnp.where(odd_group, odd, pltpu.roll(odd, HD, 1))
    return jnp.where(lane < HD, even, odd)


def pair_columns(column):
    lane = lax.broadcasted_iota(jnp.int32, (HEADS // 2, PAIR), 1)
    return jnp.where(lane < HD, column[: HEADS // 2], column[HEADS // 2 :])


def attend(queries, tables, pool, rows, write):
    token = lax.broadcasted_iota(jnp.int32, (HEADS, SPAN), 1)
    scores, held = [], []
    for row in rows:
        keys = jnp.concatenate([pool[tables[row, page], :, :WIDE] for page in range(PPH)], axis=0)
        spread = spread_queries(queries[row])
        scores.append(
            lax.dot_general(spread, keys, (((1,), (1,)), ((), ())), preferred_element_type=F32)
            * (1.0 / math.sqrt(HD))
        )
        held.append(token < tables[row, PPH])
    weights, highs, sums = [], [], []
    for score, usable in zip(scores, held):
        high = jnp.max(jnp.where(usable, score, -1e30), axis=1, keepdims=True)
        weight = jnp.where(usable, jnp.exp(score - high), 0.0)
        highs.append(high)
        sums.append(jnp.sum(weight, axis=1, keepdims=True))
        weights.append(weight.astype(BF16))
    results = []
    for row, weight in zip(rows, weights):
        values = jnp.concatenate([pool[tables[row, page], :, WIDE:] for page in range(PPH)], axis=0)
        results.append(fold_values(jnp.dot(weight, values, preferred_element_type=F32)))
    for row, result, high, total in zip(rows, results, highs, sums):
        write(row, result, high, total)


STEP = 4


def attention_kernel(
    q_ref, tab_ref, sink_ref, res_ref, com_ref, pool_hbm, ow_hbm,
    stream_ref, com_out,
    pool, ow, qall, tabv, tabs, resall, comall, keep_n, keep_ml, send_n, send_ml, recv_n, recv_ml,
    xs_n, xs_ml, xr_n, xr_ml, att, lhs, pall, load_sem, tab_sem, send_sem, recv_sem,
):
    dp, z, c, expert = position()
    sems = (send_sem, recv_sem)
    loads = [pltpu.make_async_copy(pool_hbm, pool, load_sem.at[0]), pltpu.make_async_copy(ow_hbm, ow, load_sem.at[1])]
    for load in loads:
        load.start()

    barrier = pltpu.get_barrier_semaphore()
    for offset in (1, 2, 3):
        pl.semaphore_signal(barrier, inc=1, device_id=(group_peer(z, c, offset), expert), device_id_type=MESH)
    own_tab = pltpu.make_async_copy(tab_ref.at[dp], tabs.at[dp], tab_sem.at[0])
    own_tab.start()
    block = c * 2 + z
    qall[dp] = q_ref[...]
    resall[block] = res_ref[...]
    comall[block] = com_ref[...]
    pl.semaphore_wait(barrier, 3)

    sent = []

    def send(src, dst, number, landed, offset):
        copy = remote(src, dst, sems, number, landed, (group_peer(z, c, offset), expert))
        copy.start()
        sent.append(copy)
        return copy

    tab_in, q_in, res_in, com_in = {}, {}, {}, {}
    for offset in (2, 3, 1):
        peer = group_peer(z, c, offset)
        tab_in[offset] = send(tab_ref.at[peer], tabv.at[dp], S_TAB + offset - 1, S_TAB + offset - 1, offset)
        q_in[offset] = send(q_ref, qall.at[dp], S_Q + offset - 1, S_Q + offset - 1, offset)
    for offset in (2, 3, 1):
        res_in[offset] = send(res_ref, resall.at[block], S_RES + offset - 1, S_RES + offset - 1, offset)
        com_in[offset] = send(com_ref, comall.at[block], S_COM + offset - 1, S_COM + offset - 1, offset)

    lane = lax.broadcasted_iota(jnp.int32, (HEADS, PAIR), 1)

    def run_block(offset, number, numerators, stats):
        at = group_peer(z, c, offset)
        half = z if number == 0 else 1 - z
        stats[number] = jnp.zeros((HEADS, PAIR), F32)

        def write(row, result, high, total):
            numerators[number, row] = result.astype(numerators.dtype)
            place = half * ROWS + row
            tile = jnp.where(lane == place, high, stats[number])
            stats[number] = jnp.where(lane == place + HD, total, tile)

        def step(index, carry):
            rows = [index * STEP + i for i in range(STEP)]
            attend(qall.at[at], tabs.at[at], pool, rows, write)
            return carry

        lax.fori_loop(0, ROWS // STEP, step, 0)

    def fetch_block(offset):
        at = group_peer(z, c, offset)
        tab_in[offset].wait_recv()
        copy = pltpu.make_async_copy(tabv.at[at], tabs.at[at], tab_sem.at[offset])
        copy.start()
        q_in[offset].wait_recv()
        copy.wait()

    def send_pair(number):
        return (
            send(send_n.at[number], recv_n.at[number], S_PAIR_N + number, S_PAIR_N + number, 1),
            send(send_ml.at[number], recv_ml.at[number], S_PAIR_ML + number, S_PAIR_ML + number, 1),
        )

    def factors(tile, number):
        half = z if number == 0 else 1 - z
        return pltpu.roll(tile, lax.rem(PAIR - half * ROWS, PAIR), 1)

    def merge_pair(number, incoming):
        for copy in incoming:
            copy.wait_recv()
        mine, other = keep_ml[number], recv_ml[number]
        high = jnp.maximum(mine, other)
        left, right = jnp.exp(mine - high), jnp.exp(other - high)
        total = mine * pltpu.roll(left, HD, 1) + other * pltpu.roll(right, HD, 1)
        keep_ml[number] = jnp.where(lane < HD, high, total)
        left, right = factors(left, number), factors(right, number)
        for row in range(ROWS):
            merged = keep_n[number, row] * pair_columns(left[:, row : row + 1]) + recv_n[number, row].astype(
                F32
            ) * pair_columns(right[:, row : row + 1])
            keep_n[number, row] = merged
            xs_n[number, row] = merged.astype(BF16)
        return send(xs_n.at[number], xr_n.at[1 - number], S_X_N + number, S_X_N + 1 - number, 2)

    own_tab.wait()
    loads[0].wait()
    run_block(0, 0, keep_n, keep_ml)
    fetch_block(1)
    run_block(1, 0, send_n, send_ml)
    pair_in = [send_pair(0)]
    fetch_block(3)
    run_block(3, 1, send_n, send_ml)
    pair_in.append(send_pair(1))
    cross_in = [merge_pair(0, pair_in[0])]
    fetch_block(2)
    run_block(2, 1, keep_n, keep_ml)
    cross_in.append(merge_pair(1, pair_in[1]))
    xs_ml[...] = keep_ml[0] + keep_ml[1]
    cross_ml = send(xs_ml, xr_ml, S_X_ML, S_X_ML, 2)

    cross_ml.wait_recv()
    mine, other, sink = xs_ml[...], xr_ml[...], sink_ref[...]
    top = jnp.maximum(jnp.maximum(mine, other), sink)
    left, right = jnp.exp(mine - top), jnp.exp(other - top)
    total = mine * pltpu.roll(left, HD, 1) + other * pltpu.roll(right, HD, 1)
    below = pltpu.roll(total, HD, 1) + jnp.exp(sink - top)
    left, right = left / below, right / below
    for number in (0, 1):
        cross_in[1 - number].wait_recv()
        one, two = factors(left, number), factors(right, number)
        half = z if number == 0 else 1 - z
        for row in range(ROWS):
            attention = keep_n[number, row] * pair_columns(one[:, row : row + 1]) + xr_n[number, row].astype(
                F32
            ) * pair_columns(two[:, row : row + 1])
            start = pl.multiple_of((half * ROWS + row) * (HEADS // 2), HEADS // 2)
            att[pl.ds(start, HEADS // 2), :] = attention
    for pair in range(HEADS // 2):
        lhs[c, :, PAIR * pair : PAIR * pair + PAIR] = att[pl.ds(pair, 2 * ROWS, stride=HEADS // 2), :].astype(BF16)
    lhs_in = send(lhs.at[c], lhs.at[c], S_LHS, S_LHS, 1)
    loads[1].wait()
    lhs_in.wait_recv()
    rows = jnp.concatenate([lhs[0], lhs[1]], axis=0)
    projected = lax.dot_general(rows, ow[...], (((1,), (1,)), ((), ())), preferred_element_type=F32)
    pall[dp] = projected.astype(BF16)
    proj_in = [
        send(pall.at[dp], pall.at[dp], S_PROJ + offset - 1, S_PROJ + offset - 1, offset) for offset in (2, 3, 1)
    ]
    for offset in (1, 2, 3):
        res_in[offset].wait_recv()
        com_in[offset].wait_recv()
    com_out[...] = comall[...]
    for copy in proj_in:
        copy.wait_recv()
    for k in range(NDP):
        residual = jnp.concatenate([resall[d, k].astype(F32) for d in range(NDP)], axis=0)
        stream_ref[k] = (residual + pall[k].astype(F32)).astype(BF16)
    for copy in sent:
        copy.wait_send()


def head_order(values):
    return values.reshape(HEADS // 2, 2).T.reshape(HEADS, 1)


def attention_call(queries, kv_pool, page_table, held_tokens, sinks, residual, combine, o_weight):
    width = residual.shape[1] // NDP
    q_pairs = queries.reshape(ROWS, HEADS // 2, PAIR)
    table = jnp.concatenate([page_table, held_tokens[:, :, None]], axis=2).transpose(1, 0, 2)
    table = jnp.pad(table, ((0, 0), (0, 0), (0, 128 - PPH - 1)))
    sink_tile = jnp.broadcast_to(head_order(sinks), (HEADS, PAIR))
    residual_blocks = residual.reshape(ROWS, NDP, width).transpose(1, 0, 2)
    vmem = pl.BlockSpec(memory_space=pltpu.VMEM)
    hbm = pl.BlockSpec(memory_space=pl.ANY)
    slots = combine.shape[1]
    return pl.pallas_call(
        attention_kernel,
        out_shape=(
            jax.ShapeDtypeStruct((NDP, NDP * ROWS, width), BF16),
            jax.ShapeDtypeStruct((NDP, ROWS, slots), F32),
        ),
        in_specs=[vmem] * 5 + [hbm] * 2,
        out_specs=(vmem, vmem),
        scratch_shapes=[
            pltpu.VMEM(kv_pool.shape, BF16),
            pltpu.VMEM((width, HEADS * HD), BF16),
            pltpu.VMEM((NDP, ROWS, HEADS // 2, PAIR), BF16),
            pltpu.VMEM((NDP, ROWS, 128), jnp.int32),
            pltpu.SMEM((NDP, ROWS, 128), jnp.int32),
            pltpu.VMEM((NDP, NDP, ROWS, width), BF16),
            pltpu.VMEM((NDP, ROWS, slots), F32),
            pltpu.VMEM((2, ROWS, HEADS // 2, PAIR), F32),
            pltpu.VMEM((2, HEADS, PAIR), F32),
            pltpu.VMEM((2, ROWS, HEADS // 2, PAIR), BF16),
            pltpu.VMEM((2, HEADS, PAIR), F32),
            pltpu.VMEM((2, ROWS, HEADS // 2, PAIR), BF16),
            pltpu.VMEM((2, HEADS, PAIR), F32),
            pltpu.VMEM((2, ROWS, HEADS // 2, PAIR), BF16),
            pltpu.VMEM((HEADS, PAIR), F32),
            pltpu.VMEM((2, ROWS, HEADS // 2, PAIR), BF16),
            pltpu.VMEM((HEADS, PAIR), F32),
            pltpu.VMEM((2 * ROWS * HEADS // 2, PAIR), F32),
            pltpu.VMEM((2, 2 * ROWS, HEADS * HD), BF16),
            pltpu.VMEM((NDP, NDP * ROWS, width), BF16),
            pltpu.SemaphoreType.DMA((2,)),
            pltpu.SemaphoreType.DMA((4,)),
            pltpu.SemaphoreType.DMA((N_SEM_A,)),
            pltpu.SemaphoreType.DMA((N_SEM_A,)),
        ],
        compiler_params=pltpu.CompilerParams(collective_id=0, has_side_effects=True, vmem_limit_bytes=50 * 2**20),
        name="attention",
    )(q_pairs, table, sink_tile, residual_blocks, combine, kv_pool, o_weight.T)


T_PAIR, T_PART, T_NEXT, T_QKV = 0, 2, 3, 4
N_SEM_B = 7


def normalized(blocks, gains):
    total = sum(jnp.sum(block * block, axis=1, keepdims=True) for block in blocks)
    width = sum(block.shape[1] for block in blocks)
    scale = lax.rsqrt(total / width + EPSILON)
    return [(block * scale * gain).astype(BF16) for block, gain in zip(blocks, gains)]


def expert_kernel(
    stream_ref, com_ref, mgain_ref, again_ref, wg_hbm, wu_hbm, wd_hbm, wq_hbm,
    next_out, qkv_out,
    wg, wu, wd, wq, xin, outbox, arr, gate, up, osend, orecv, rbuf, ret, part_s, part_r, nextb, nextf, qbuf,
    load_sem, send_sem, recv_sem, d_send, d_recv, f_send, f_recv, r_send, r_recv,
):
    dp, z, c, expert = position()
    sems = (send_sem, recv_sem)
    count = arr.shape[2]
    slots = arr.shape[3]
    width = arr.shape[4]
    block = c * 2 + z
    loads = [
        pltpu.make_async_copy(src, dst, load_sem.at[i])
        for i, (src, dst) in enumerate(((wg_hbm, wg), (wu_hbm, wu), (wd_hbm, wd), (wq_hbm, wq)))
    ]
    for load in loads:
        load.start()

    barrier = pltpu.get_barrier_semaphore()
    for offset in (1, 2, 3):
        pl.semaphore_signal(barrier, inc=1, device_id=(group_peer(z, c, offset), expert), device_id_type=MESH)

    def greet(i, carry):
        pl.semaphore_signal(barrier, inc=1, device_id=(dp, lax.rem(expert + i, count)), device_id_type=MESH)
        return carry

    lax.fori_loop(1, count, greet, 0)

    rows = [stream_ref[k].astype(F32) for k in range(NDP)]
    for k, value in enumerate(normalized(rows, [mgain_ref[k] for k in range(NDP)])):
        xin[k] = value
    share = jnp.concatenate([com_ref[d] for d in range(NDP)], axis=0)
    picks = (share > 0).astype(F32).T.astype(BF16)
    for j in range(2):
        picked = jnp.dot(picks, xin[2 * c + j], preferred_element_type=F32).astype(BF16)
        outbox[j] = picked.reshape(count, slots, width)
    pl.semaphore_wait(barrier, count + 2)

    sent = []

    def send(src, dst, number, landed, offset):
        copy = remote(src, dst, sems, number, landed, (group_peer(z, c, offset), expert))
        copy.start()
        sent.append(copy)
        return copy

    def dispatch(to, slot):
        return remote(outbox.at[:, to], arr.at[c, :, slot], (d_send, d_recv), to, slot, (dp, to))

    def forward(source):
        return remote(
            arr.at[c, :, source], arr.at[c, :, source], (f_send, f_recv), source, source,
            (group_peer(z, c, 1), expert),
        )

    def giveback(j, to, slot):
        return remote(rbuf.at[j, to], ret.at[j, slot], (r_send.at[j], r_recv.at[j]), to, slot, (dp, to))

    def start_dispatch(i, carry):
        dispatch(lax.rem(expert + i, count), expert).start()
        return carry

    lax.fori_loop(1, count, start_dispatch, 0)
    for j in range(2):
        arr[c, j, expert] = outbox[j, expert]
    forward(expert).start()

    def pass_on(i, carry):
        source = lax.rem(expert + count - i, count)
        dispatch(source, source).wait_recv()
        forward(source).start()
        return carry

    lax.fori_loop(1, count, pass_on, 0)
    loads[0].wait()
    loads[1].wait()

    def project(half, first):
        for j in range(2):
            rows = arr[half, j].reshape(count * slots, width)
            for total, weight in ((gate, wg), (up, wu)):
                value = jnp.dot(rows, weight[2 * half + j], preferred_element_type=F32)
                if first and j == 0:
                    total[...] = value
                else:
                    total[...] += value

    project(c, True)

    def arrived(source, carry):
        forward(source).wait_recv()
        return carry

    lax.fori_loop(0, count, arrived, 0)
    project(1 - c, False)
    gated = jnp.minimum(gate[...], LIMIT)
    lifted = jnp.clip(up[...], -LIMIT, LIMIT)
    activated = (gated * jax.nn.sigmoid(1.702 * gated) * (lifted + 1.0)).astype(BF16)
    loads[2].wait()

    def down(k):
        return lax.dot_general(activated, wd[k], (((1,), (1,)), ((), ())), preferred_element_type=F32)

    pair_in = []
    for j in range(2):
        osend[j] = down(2 * (1 - c) + j).astype(BF16)
        pair_in.append(send(osend.at[j], orecv.at[j], T_PAIR + j, T_PAIR + j, 1))
    for j in range(2):
        own = down(2 * c + j)
        pair_in[j].wait_recv()
        rbuf[j] = (own + orecv[j].astype(F32)).astype(BF16).reshape(count, slots, width)

        def start_return(i, carry):
            giveback(j, lax.rem(expert + i, count), expert).start()
            return carry

        lax.fori_loop(1, count, start_return, 0)
        ret[j, expert] = rbuf[j, expert]

    high = share.astype(BF16)
    low = (share - high.astype(F32)).astype(BF16)
    both = jnp.concatenate([high, low], axis=0)
    group_rows = share.shape[0]
    for j in range(2):

        def returned(source, carry):
            @pl.when(source != expert)
            def _():
                giveback(j, source, source).wait_recv()

            return carry

        lax.fori_loop(0, count, returned, 0)
        mixed = jnp.dot(both, ret[j].reshape(count * slots, width), preferred_element_type=F32)
        part_s[j] = (mixed[:group_rows] + mixed[group_rows:]).astype(BF16)
    send(part_s, part_r, T_PART, T_PART, 2).wait_recv()
    for j in range(2):
        moe_out = part_s[j].astype(F32) + part_r[j].astype(F32)
        nextb[c, j] = (stream_ref[2 * c + j].astype(F32) + moe_out).astype(BF16)
    next_in = send(nextb.at[c], nextb.at[c], T_NEXT, T_NEXT, 1)
    next_in.wait_recv()
    rows = [nextb[k // 2, k % 2].astype(F32) for k in range(NDP)]
    for k in range(NDP):
        nextf[k] = rows[k]
    inputs = normalized(rows, [again_ref[k] for k in range(NDP)])
    loads[3].wait()
    qkv = sum(jnp.dot(inputs[k], wq[k], preferred_element_type=F32) for k in range(NDP))
    columns = qkv.shape[1]
    for d in range(NDP):
        qbuf[d] = qkv[ROWS * d : ROWS * d + ROWS].astype(BF16)
    own_columns = pl.ds(pl.multiple_of(dp * columns, 128), columns)
    qkv_in = []
    for offset in (2, 3, 1):
        peer = group_peer(z, c, offset)
        theirs = lax.rem(peer, 2) * 2 + lax.div(peer, 2)
        qkv_in.append(
            send(qbuf.at[theirs], qkv_out.at[:, own_columns], T_QKV + offset - 1, T_QKV + offset - 1, offset)
        )
    qkv_out[:, own_columns] = qbuf[block]
    start = pl.multiple_of(block * ROWS, ROWS)
    for k in range(NDP):
        next_out[:, width * k : width * k + width] = nextf[k, pl.ds(start, ROWS), :].astype(BF16)

    def all_sent(i, carry):
        to = lax.rem(expert + i, count)
        dispatch(to, expert).wait_send()
        for j in range(2):
            giveback(j, to, expert).wait_send()
        return carry

    lax.fori_loop(1, count, all_sent, 0)

    def all_passed(source, carry):
        forward(source).wait_send()
        return carry

    lax.fori_loop(0, count, all_passed, 0)
    for copy in sent:
        copy.wait_send()
    for copy in qkv_in:
        copy.wait_recv()


def expert_call(streams, tables, moe_gain, attn_gain, w_gate, w_up, w_down, qkv_weight, count):
    width = streams.shape[2]
    hidden = w_gate.shape[2]
    columns = qkv_weight.shape[1]
    slots = tables.shape[2] // count
    vmem = pl.BlockSpec(memory_space=pltpu.VMEM)
    hbm = pl.BlockSpec(memory_space=pl.ANY)
    group_rows = NDP * ROWS
    all_slots = count * slots
    dma = pltpu.SemaphoreType.DMA
    return pl.pallas_call(
        expert_kernel,
        out_shape=(
            jax.ShapeDtypeStruct((ROWS, NDP * width), BF16),
            jax.ShapeDtypeStruct((ROWS, NDP * columns), BF16),
        ),
        in_specs=[vmem] * 4 + [hbm] * 4,
        out_specs=(vmem, vmem),
        scratch_shapes=[
            pltpu.VMEM((NDP, width, hidden), BF16),
            pltpu.VMEM((NDP, width, hidden), BF16),
            pltpu.VMEM((NDP, width, hidden), BF16),
            pltpu.VMEM((NDP, width, columns), BF16),
            pltpu.VMEM((NDP, group_rows, width), BF16),
            pltpu.VMEM((2, count, slots, width), BF16),
            pltpu.VMEM((2, 2, count, slots, width), BF16),
            pltpu.VMEM((all_slots, hidden), F32),
            pltpu.VMEM((all_slots, hidden), F32),
            pltpu.VMEM((2, all_slots, width), BF16),
            pltpu.VMEM((2, all_slots, width), BF16),
            pltpu.VMEM((2, count, slots, width), BF16),
            pltpu.VMEM((2, count, slots, width), BF16),
            pltpu.VMEM((2, group_rows, width), BF16),
            pltpu.VMEM((2, group_rows, width), BF16),
            pltpu.VMEM((2, 2, group_rows, width), BF16),
            pltpu.VMEM((NDP, group_rows, width), F32),
            pltpu.VMEM((NDP, ROWS, columns), BF16),
            dma((4,)),
            dma((N_SEM_B,)),
            dma((N_SEM_B,)),
            dma((count,)),
            dma((count,)),
            dma((count,)),
            dma((count,)),
            dma((2, count)),
            dma((2, count)),
        ],
        compiler_params=pltpu.CompilerParams(collective_id=1, has_side_effects=True, vmem_limit_bytes=56 * 2**20),
        name="experts",
    )(
        streams,
        tables,
        moe_gain.reshape(NDP, 1, width),
        attn_gain.reshape(NDP, 1, width),
        w_gate.reshape(NDP, width, hidden),
        w_up.reshape(NDP, width, hidden),
        w_down[0].T.reshape(NDP, width, hidden),
        qkv_weight.reshape(NDP, width, columns),
    )


def combine_table(route_ids, route_weights, experts_count, capacity, block):
    rows = route_ids.shape[0]
    experts = jnp.arange(experts_count, dtype=jnp.int32)
    chosen = route_ids[:, :, None] == experts[None, None, :]
    share = route_weights / jnp.sum(route_weights, axis=1, keepdims=True)
    shares = jnp.sum(jnp.where(chosen, share[:, :, None], 0.0), axis=1)
    hit = jnp.any(chosen, axis=1)
    earlier = jnp.arange(rows)[:, None] > jnp.arange(rows)[None, :]
    slot = jnp.sum(jnp.where(earlier[:, :, None] & hit[None, :, :], 1, 0), axis=1)
    column = jnp.arange(NDP * capacity, dtype=jnp.int32)[None, None, :]
    table = jnp.where(hit[:, :, None] & (column == (block * capacity + slot)[:, :, None]), shares[:, :, None], 0.0)
    return table.reshape(rows, experts_count * NDP * capacity)


def body(
    queries,
    kv_pool,
    page_table,
    held_tokens,
    sinks,
    residual,
    route_ids,
    route_weights,
    moe_gain,
    w_gate,
    w_up,
    w_down,
    o_weight,
    attn_gain,
    qkv_weight,
):
    experts_count = lax.axis_size("expert")
    own_rows = queries.shape[0]
    holder = lax.axis_index("dp")
    block = lax.rem(holder, 2) * 2 + lax.div(holder, 2)
    capacity = 2 * own_rows * TOP // experts_count
    table = combine_table(route_ids, route_weights, experts_count, capacity, block)
    streams, tables = attention_call(
        queries, kv_pool, page_table, held_tokens, sinks, residual, table, o_weight
    )
    return expert_call(
        streams, tables, moe_gain, attn_gain, w_gate, w_up, w_down, qkv_weight, experts_count
    )


def solution(mesh):
    in_specs = (
        P(("dp", "expert"), None),
        P(("dp", "expert"), None, None),
        P(("dp", "expert"), None, None),
        P(("dp", "expert"), None),
        P(),
        P(("dp", "expert"), None),
        P(("dp", "expert"), None),
        P(("dp", "expert"), None),
        P(),
        P("expert", None, "dp"),
        P("expert", None, "dp"),
        P("expert", "dp", None),
        P(None, "dp"),
        P(),
        P(None, "dp"),
    )
    out_specs = (P(("dp", "expert"), None), P(("dp", "expert"), None))
    return jax.shard_map(body, mesh=mesh, in_specs=in_specs, out_specs=out_specs, check_vma=False)
```

```python
import math

import jax
import jax.numpy as jnp
from jax import lax
from jax.experimental import pallas as pl
from jax.experimental.pallas import tpu as pltpu
from jax.sharding import PartitionSpec as P

HEADS = 64
KVH = 8
HD = 64
TOP = 4
PAGE = 16
PPH = 16
SPAN = PPH * PAGE
WIDE = KVH * HD
PAIR = 2 * HD
ROWS = 8
NDP = 4

EPSILON = 1e-05
LIMIT = 7.0
MESH = pl.DeviceIdType.MESH
F32 = jnp.float32
BF16 = jnp.bfloat16

S_TAB, S_HELD, S_Q, S_RES, S_COM, S_PAIR_N, S_PAIR_ML, S_X_N, S_X_ML, S_LHS, S_PROJ = 0, 3, 6, 9, 12, 15, 17, 19, 21, 22, 23
S_OUT, S_PART, S_NEXT, S_QKV = 26, 28, 29, 30
N_SEM = 33
L_TAB, L_HELD, L_Q, L_POOL, L_SINK, L_IDS, L_WEIGHTS, L_RES, L_OW, L_MGAIN, L_GATE, L_UP, L_DOWN, L_AGAIN, L_QKV = range(15)


def position():
    dp = lax.axis_index("dp")
    expert = lax.axis_index("expert")
    return dp, lax.div(dp, 2), lax.rem(dp, 2), expert


def group_peer(z, c, offset):
    return lax.rem(z + offset // 2, 2) * 2 + lax.rem(c + offset % 2, 2)


def remote(src, dst, sems, sent, landed, device):
    return pltpu.make_async_remote_copy(
        src_ref=src,
        dst_ref=dst,
        send_sem=sems[0].at[sent],
        recv_sem=sems[1].at[landed],
        device_id=device,
        device_id_type=MESH,
    )


def spread_queries(wide):
    turned = pltpu.roll(wide, HD, 1)
    row = lax.broadcasted_iota(jnp.int32, (HEADS // 2, PAIR), 0)
    lane = lax.broadcasted_iota(jnp.int32, (HEADS // 2, PAIR), 1)
    odd_group = lax.rem(lax.div(row, 4), 2) == 1
    own_half = (lane >= HD) == odd_group
    even = jnp.where(own_half, jnp.where(odd_group, turned, wide), 0.0)
    odd = jnp.where(own_half, jnp.where(odd_group, wide, turned), 0.0)
    tile = lax.div(row, 8)
    parts = []
    for heads in (even, odd):
        parts.append(jnp.concatenate([jnp.where(tile == t, heads, 0.0) for t in range(4)], axis=1))
    return jnp.concatenate(parts, axis=0).astype(BF16)


def fold_values(wide):
    row = lax.broadcasted_iota(jnp.int32, (HEADS // 2, PAIR), 0)
    lane = lax.broadcasted_iota(jnp.int32, (HEADS // 2, PAIR), 1)
    odd_group = lax.rem(lax.div(row, 4), 2) == 1

    def own_tiles(base):
        return jnp.concatenate(
            [wide[base + 8 * t : base + 8 * t + 8, PAIR * t : PAIR * t + PAIR] for t in range(4)], axis=0
        )

    even, odd = own_tiles(0), own_tiles(HEADS // 2)
    even = jnp.where(odd_group, pltpu.roll(even, HD, 1), even)
    odd = jnp.where(odd_group, odd, pltpu.roll(odd, HD, 1))
    return jnp.where(lane < HD, even, odd)


def pair_columns(column):
    lane = lax.broadcasted_iota(jnp.int32, (HEADS // 2, PAIR), 1)
    return jnp.where(lane < HD, column[: HEADS // 2], column[HEADS // 2 :])


def normalized(blocks, gains):
    total = sum(jnp.sum(block * block, axis=1, keepdims=True) for block in blocks)
    width = sum(block.shape[1] for block in blocks)
    scale = lax.rsqrt(total / width + EPSILON)
    return [(block * scale * gain).astype(BF16) for block, gain in zip(blocks, gains)]


def attend(queries, tables, counts, holder, pool, rows, write):
    token = lax.broadcasted_iota(jnp.int32, (HEADS, SPAN), 1)
    scores, held = [], []
    for row in rows:
        keys = jnp.concatenate([pool[tables[row, holder, page], :, :WIDE] for page in range(PPH)], axis=0)
        start = pl.multiple_of(row * (HEADS // 2), HEADS // 2)
        spread = spread_queries(queries[pl.ds(start, HEADS // 2), :])
        scores.append(
            lax.dot_general(spread, keys, (((1,), (1,)), ((), ())), preferred_element_type=F32)
            * (1.0 / math.sqrt(HD))
        )
        held.append(token < counts[holder, row])
    weights, highs, sums = [], [], []
    for score, usable in zip(scores, held):
        high = jnp.max(jnp.where(usable, score, -1e30), axis=1, keepdims=True)
        weight = jnp.where(usable, jnp.exp(score - high), 0.0)
        highs.append(high)
        sums.append(jnp.sum(weight, axis=1, keepdims=True))
        weights.append(weight.astype(BF16))
    results = []
    for row, weight in zip(rows, weights):
        values = jnp.concatenate([pool[tables[row, holder, page], :, WIDE:] for page in range(PPH)], axis=0)
        results.append(fold_values(jnp.dot(weight, values, preferred_element_type=F32)))
    for row, result, high, total in zip(rows, results, highs, sums):
        write(row, result, high, total)


def sink_columns(sinks):
    row = lax.broadcasted_iota(jnp.int32, (HEADS, HEADS), 0)
    lane = lax.broadcasted_iota(jnp.int32, (HEADS, HEADS), 1)
    half = HEADS // 2
    head = jnp.where(row < half, 2 * row, 2 * (row - half) + 1)
    return jnp.sum(jnp.where(lane == head, sinks, 0.0), axis=1, keepdims=True)


def combine_rows(ids, weights, table, block, slots):
    capacity = slots // NDP
    lane = lax.broadcasted_iota(jnp.int32, (1, table.shape[1]), 1)
    of_expert, at_slot = lax.div(lane, slots), lax.rem(lane, slots)
    taken = jnp.zeros_like(lane)
    for row in range(ROWS):
        hit = jnp.zeros_like(lane)
        weight = jnp.zeros(lane.shape, F32)
        total = jnp.zeros(lane.shape, F32)
        for k in range(TOP):
            match = of_expert == ids[k, row]
            hit = jnp.where(match, 1, hit)
            weight = jnp.where(match, weights[k, row], weight)
            total = total + weights[k, row]
        at = (hit == 1) & (at_slot == block * capacity + taken)
        table[row : row + 1, :] = jnp.where(at, weight / total, 0.0)
        taken = taken + hit


STEP = 4


def layer_kernel(
    q_hbm, pool_hbm, tab_hbm, held_hbm, sink_hbm, res_hbm, ids_hbm, weights_hbm, mgain_hbm,
    wg_hbm, wu_hbm, wd_hbm, ow_hbm, again_hbm, wq_hbm,
    next_out, qkv_out,
    pool, ow, wg, wu, wd, wq,
    tabs, helds, ids, weights, sinks, mgain, again, qraw, qwide, resraw, comown, comall,
    keep_n, keep_ml, send_n, send_ml, recv_n, recv_ml, xs_n, xs_ml, xr_n, xr_ml, att, lhs, pall, stream,
    xin, outbox, arr, gate, up, osend, orecv, rbuf, ret, part_s, part_r, nextb, nextf, qbuf,
    load_sem, send_sem, recv_sem, d_send, d_recv, f_send, f_recv, r_send, r_recv,
):
    dp, z, c, expert = position()
    sems = (send_sem, recv_sem)
    count, slots, width = arr.shape[2], arr.shape[3], arr.shape[4]
    block = c * 2 + z

    barrier = pltpu.get_barrier_semaphore()
    for offset in (1, 2, 3):
        pl.semaphore_signal(barrier, inc=1, device_id=(group_peer(z, c, offset), expert), device_id_type=MESH)

    def greet(i, carry):
        pl.semaphore_signal(barrier, inc=1, device_id=(dp, lax.rem(expert + i, count)), device_id_type=MESH)
        return carry

    lax.fori_loop(1, count, greet, 0)
    loads = {}
    for number, src, dst in (
        (L_TAB, tab_hbm, tabs.at[dp]),
        (L_HELD, held_hbm, helds.at[dp]),
        (L_Q, q_hbm, qraw.at[dp]),
        (L_POOL, pool_hbm, pool),
        (L_SINK, sink_hbm, sinks),
        (L_IDS, ids_hbm, ids),
        (L_WEIGHTS, weights_hbm, weights),
        (L_RES, res_hbm, resraw.at[block]),
        (L_OW, ow_hbm, ow),
        (L_MGAIN, mgain_hbm, mgain),
        (L_GATE, wg_hbm, wg),
        (L_UP, wu_hbm, wu),
        (L_DOWN, wd_hbm, wd),
        (L_AGAIN, again_hbm, again),
        (L_QKV, wq_hbm, wq),
    ):
        loads[number] = pltpu.make_async_copy(src, dst, load_sem.at[number])
        loads[number].start()

    sent = []

    def send(src, dst, number, landed, offset):
        copy = remote(src, dst, sems, number, landed, (group_peer(z, c, offset), expert))
        copy.start()
        sent.append(copy)
        return copy

    lane = lax.broadcasted_iota(jnp.int32, (HEADS, PAIR), 1)

    def run_block(offset, number, numerators, stats):
        at = group_peer(z, c, offset)
        half = z if number == 0 else 1 - z
        stats[number] = jnp.zeros((HEADS, PAIR), F32)
        for pair in range(HEADS // 2):
            qwide[pl.ds(pair, ROWS, stride=HEADS // 2), :] = qraw[at, :, PAIR * pair : PAIR * pair + PAIR].astype(F32)

        def write(row, result, high, total):
            numerators[number, row] = result.astype(numerators.dtype)
            place = half * ROWS + row
            tile = jnp.where(lane == place, high, stats[number])
            stats[number] = jnp.where(lane == place + HD, total, tile)

        def step(index, carry):
            rows = [index * STEP + i for i in range(STEP)]
            attend(qwide, tabs.at[at], helds.at[at], dp, pool, rows, write)
            return carry

        lax.fori_loop(0, ROWS // STEP, step, 0)

    tab_in, held_in, q_in, res_in, com_in = {}, {}, {}, {}, {}

    def fetch_block(offset):
        tab_in[offset].wait_recv()
        held_in[offset].wait_recv()
        q_in[offset].wait_recv()

    def send_pair(number):
        return (
            send(send_n.at[number], recv_n.at[number], S_PAIR_N + number, S_PAIR_N + number, 1),
            send(send_ml.at[number], recv_ml.at[number], S_PAIR_ML + number, S_PAIR_ML + number, 1),
        )

    def factors(tile, number):
        half = z if number == 0 else 1 - z
        return pltpu.roll(tile, lax.rem(PAIR - half * ROWS, PAIR), 1)

    def merge_pair(number, incoming):
        for copy in incoming:
            copy.wait_recv()
        mine, other = keep_ml[number], recv_ml[number]
        high = jnp.maximum(mine, other)
        left, right = jnp.exp(mine - high), jnp.exp(other - high)
        total = mine * pltpu.roll(left, HD, 1) + other * pltpu.roll(right, HD, 1)
        keep_ml[number] = jnp.where(lane < HD, high, total)
        left, right = factors(left, number), factors(right, number)
        for row in range(ROWS):
            merged = keep_n[number, row] * pair_columns(left[:, row : row + 1]) + recv_n[number, row].astype(
                F32
            ) * pair_columns(right[:, row : row + 1])
            keep_n[number, row] = merged
            xs_n[number, row] = merged.astype(BF16)
        return send(xs_n.at[number], xr_n.at[1 - number], S_X_N + number, S_X_N + 1 - number, 2)

    pl.semaphore_wait(barrier, count + 2)
    for offset in (2, 3, 1):
        tab_in[offset] = send(tab_hbm, tabs.at[dp], S_TAB + offset - 1, S_TAB + offset - 1, offset)
        held_in[offset] = send(held_hbm, helds.at[dp], S_HELD + offset - 1, S_HELD + offset - 1, offset)
        q_in[offset] = send(q_hbm, qraw.at[dp], S_Q + offset - 1, S_Q + offset - 1, offset)
    for offset in (2, 3, 1):
        res_in[offset] = send(res_hbm, resraw.at[block], S_RES + offset - 1, S_RES + offset - 1, offset)
    for number in (L_IDS, L_WEIGHTS):
        loads[number].wait()
    combine_rows(ids, weights, comown, block, slots)
    comall[block] = comown[...]
    for offset in (2, 3, 1):
        com_in[offset] = send(comown, comall.at[block], S_COM + offset - 1, S_COM + offset - 1, offset)

    for number in (L_TAB, L_HELD, L_Q, L_POOL):
        loads[number].wait()
    run_block(0, 0, keep_n, keep_ml)
    fetch_block(1)
    run_block(1, 0, send_n, send_ml)
    pair_in = [send_pair(0)]
    fetch_block(3)
    run_block(3, 1, send_n, send_ml)
    pair_in.append(send_pair(1))
    cross_in = [merge_pair(0, pair_in[0])]
    fetch_block(2)
    run_block(2, 1, keep_n, keep_ml)
    cross_in.append(merge_pair(1, pair_in[1]))
    xs_ml[...] = keep_ml[0] + keep_ml[1]
    cross_ml = send(xs_ml, xr_ml, S_X_ML, S_X_ML, 2)

    cross_ml.wait_recv()
    loads[L_SINK].wait()
    mine, other, sink = xs_ml[...], xr_ml[...], sink_columns(sinks[...])
    top = jnp.maximum(jnp.maximum(mine, other), sink)
    left, right = jnp.exp(mine - top), jnp.exp(other - top)
    total = mine * pltpu.roll(left, HD, 1) + other * pltpu.roll(right, HD, 1)
    below = pltpu.roll(total, HD, 1) + jnp.exp(sink - top)
    left, right = left / below, right / below
    for number in (0, 1):
        cross_in[1 - number].wait_recv()
        one, two = factors(left, number), factors(right, number)
        half = z if number == 0 else 1 - z
        for row in range(ROWS):
            attention = keep_n[number, row] * pair_columns(one[:, row : row + 1]) + xr_n[number, row].astype(
                F32
            ) * pair_columns(two[:, row : row + 1])
            start = pl.multiple_of((half * ROWS + row) * (HEADS // 2), HEADS // 2)
            att[pl.ds(start, HEADS // 2), :] = attention
    for pair in range(HEADS // 2):
        lhs[c, :, PAIR * pair : PAIR * pair + PAIR] = att[pl.ds(pair, 2 * ROWS, stride=HEADS // 2), :].astype(BF16)
    lhs_in = send(lhs.at[c], lhs.at[c], S_LHS, S_LHS, 1)
    loads[L_OW].wait()
    lhs_in.wait_recv()
    rows = jnp.concatenate([lhs[0], lhs[1]], axis=0)
    projected = lax.dot_general(rows, ow[...], (((1,), (1,)), ((), ())), preferred_element_type=F32)
    pall[dp] = projected.astype(BF16)
    proj_in = [
        send(pall.at[dp], pall.at[dp], S_PROJ + offset - 1, S_PROJ + offset - 1, offset) for offset in (2, 3, 1)
    ]
    for offset in (1, 2, 3):
        res_in[offset].wait_recv()
        com_in[offset].wait_recv()
    for copy in proj_in:
        copy.wait_recv()
    loads[L_RES].wait()
    loads[L_MGAIN].wait()
    rows = []
    for k in range(NDP):
        residual = jnp.concatenate(
            [resraw[d, :, width * k : width * k + width].astype(F32) for d in range(NDP)], axis=0
        )
        rows.append((residual + pall[k].astype(F32)).astype(BF16).astype(F32))
        stream[k] = rows[k]
    gains = [mgain[:, width * k : width * k + width] for k in range(NDP)]
    for k, value in enumerate(normalized(rows, gains)):
        xin[k] = value
    share = jnp.concatenate([comall[d] for d in range(NDP)], axis=0)
    picks = (share > 0).astype(F32).T.astype(BF16)
    for j in range(2):
        picked = jnp.dot(picks, xin[2 * c + j], preferred_element_type=F32).astype(BF16)
        outbox[j] = picked.reshape(count, slots, width)

    def dispatch(to, slot):
        return remote(outbox.at[:, to], arr.at[c, :, slot], (d_send, d_recv), to, slot, (dp, to))

    def forward(source):
        return remote(
            arr.at[c, :, source], arr.at[c, :, source], (f_send, f_recv), source, source,
            (group_peer(z, c, 1), expert),
        )

    def giveback(j, to, slot):
        return remote(rbuf.at[j, to], ret.at[j, slot], (r_send.at[j], r_recv.at[j]), to, slot, (dp, to))

    def start_dispatch(i, carry):
        dispatch(lax.rem(expert + i, count), expert).start()
        return carry

    lax.fori_loop(1, count, start_dispatch, 0)
    for j in range(2):
        arr[c, j, expert] = outbox[j, expert]
    forward(expert).start()

    def pass_on(i, carry):
        source = lax.rem(expert + count - i, count)
        dispatch(source, source).wait_recv()
        forward(source).start()
        return carry

    lax.fori_loop(1, count, pass_on, 0)
    loads[L_GATE].wait()
    loads[L_UP].wait()

    def project(half, first):
        for j in range(2):
            rows = arr[half, j].reshape(count * slots, width)
            for total, weight in ((gate, wg), (up, wu)):
                value = jnp.dot(rows, weight[2 * half + j], preferred_element_type=F32)
                if first and j == 0:
                    total[...] = value
                else:
                    total[...] += value

    project(c, True)

    def arrived(source, carry):
        forward(source).wait_recv()
        return carry

    lax.fori_loop(0, count, arrived, 0)
    project(1 - c, False)
    gated = jnp.minimum(gate[...], LIMIT)
    lifted = jnp.clip(up[...], -LIMIT, LIMIT)
    activated = (gated * jax.nn.sigmoid(1.702 * gated) * (lifted + 1.0)).astype(BF16)
    loads[L_DOWN].wait()

    def down(k):
        return lax.dot_general(activated, wd[k], (((1,), (1,)), ((), ())), preferred_element_type=F32)

    pair_in = []
    for j in range(2):
        osend[j] = down(2 * (1 - c) + j).astype(BF16)
        pair_in.append(send(osend.at[j], orecv.at[j], S_OUT + j, S_OUT + j, 1))
    for j in range(2):
        own = down(2 * c + j)
        pair_in[j].wait_recv()
        rbuf[j] = (own + orecv[j].astype(F32)).astype(BF16).reshape(count, slots, width)

        def start_return(i, carry):
            giveback(j, lax.rem(expert + i, count), expert).start()
            return carry

        lax.fori_loop(1, count, start_return, 0)
        ret[j, expert] = rbuf[j, expert]

    high = share.astype(BF16)
    low = (share - high.astype(F32)).astype(BF16)
    both = jnp.concatenate([high, low], axis=0)
    group_rows = share.shape[0]
    for j in range(2):

        def returned(source, carry):
            @pl.when(source != expert)
            def _():
                giveback(j, source, source).wait_recv()

            return carry

        lax.fori_loop(0, count, returned, 0)
        mixed = jnp.dot(both, ret[j].reshape(count * slots, width), preferred_element_type=F32)
        part_s[j] = (mixed[:group_rows] + mixed[group_rows:]).astype(BF16)
    send(part_s, part_r, S_PART, S_PART, 2).wait_recv()
    for j in range(2):
        moe_out = part_s[j].astype(F32) + part_r[j].astype(F32)
        nextb[c, j] = (stream[2 * c + j] + moe_out).astype(BF16)
    next_in = send(nextb.at[c], nextb.at[c], S_NEXT, S_NEXT, 1)
    next_in.wait_recv()
    rows = [nextb[k // 2, k % 2].astype(F32) for k in range(NDP)]
    for k in range(NDP):
        nextf[k] = rows[k]
    loads[L_AGAIN].wait()
    inputs = normalized(rows, [again[:, width * k : width * k + width] for k in range(NDP)])
    loads[L_QKV].wait()
    qkv = sum(jnp.dot(inputs[k], wq[k], preferred_element_type=F32) for k in range(NDP))
    columns = qkv.shape[1]
    for d in range(NDP):
        qbuf[d] = qkv[ROWS * d : ROWS * d + ROWS].astype(BF16)
    own_columns = pl.ds(pl.multiple_of(dp * columns, 128), columns)
    qkv_in = []
    for offset in (2, 3, 1):
        peer = group_peer(z, c, offset)
        theirs = lax.rem(peer, 2) * 2 + lax.div(peer, 2)
        qkv_in.append(
            send(qbuf.at[theirs], qkv_out.at[:, own_columns], S_QKV + offset - 1, S_QKV + offset - 1, offset)
        )
    qkv_out[:, own_columns] = qbuf[block]
    start = pl.multiple_of(block * ROWS, ROWS)
    for k in range(NDP):
        next_out[:, width * k : width * k + width] = nextf[k, pl.ds(start, ROWS), :].astype(BF16)

    def all_sent(i, carry):
        to = lax.rem(expert + i, count)
        dispatch(to, expert).wait_send()
        for j in range(2):
            giveback(j, to, expert).wait_send()
        return carry

    lax.fori_loop(1, count, all_sent, 0)

    def all_passed(source, carry):
        forward(source).wait_send()
        return carry

    lax.fori_loop(0, count, all_passed, 0)
    for copy in sent:
        copy.wait_send()
    for copy in qkv_in:
        copy.wait_recv()


def layer_call(args, count):
    (queries, kv_pool, page_table, held_tokens, sinks, residual, route_ids, route_weights, moe_gain,
     w_gate, w_up, w_down, o_weight, attn_gain, qkv_weight) = args
    width = residual.shape[1] // NDP
    hidden = w_gate.shape[2]
    columns = qkv_weight.shape[1]
    slots = NDP * (2 * ROWS * TOP // count)
    group_rows = NDP * ROWS
    all_slots = count * slots
    hbm = pl.BlockSpec(memory_space=pltpu.HBM)
    out = pl.BlockSpec(memory_space=pltpu.VMEM)
    vmem, dma = pltpu.VMEM, pltpu.SemaphoreType.DMA
    pairs = (2, ROWS, HEADS // 2, PAIR)
    return pl.pallas_call(
        layer_kernel,
        out_shape=(
            jax.ShapeDtypeStruct((ROWS, NDP * width), BF16),
            jax.ShapeDtypeStruct((ROWS, NDP * columns), BF16),
        ),
        in_specs=[hbm] * 15,
        out_specs=(out, out),
        scratch_shapes=[
            vmem(kv_pool.shape, BF16),
            vmem((width, HEADS * HD), BF16),
            vmem((NDP, width, hidden), BF16),
            vmem((NDP, width, hidden), BF16),
            vmem((NDP, width, hidden), BF16),
            vmem((NDP, width, columns), BF16),
            pltpu.SMEM((NDP,) + page_table.shape, jnp.int32),
            pltpu.SMEM((NDP, NDP, ROWS), jnp.int32),
            pltpu.SMEM((TOP, ROWS), jnp.int32),
            pltpu.SMEM((TOP, ROWS), F32),
            vmem((1, HEADS), F32),
            vmem((1, NDP * width), F32),
            vmem((1, NDP * width), F32),
            vmem((NDP, ROWS, HEADS * HD), BF16),
            vmem((ROWS * HEADS // 2, PAIR), F32),
            vmem((NDP, ROWS, NDP * width), BF16),
            vmem((ROWS, all_slots), F32),
            vmem((NDP, ROWS, all_slots), F32),
            vmem(pairs, F32),
            vmem((2, HEADS, PAIR), F32),
            vmem(pairs, BF16),
            vmem((2, HEADS, PAIR), F32),
            vmem(pairs, BF16),
            vmem((2, HEADS, PAIR), F32),
            vmem(pairs, BF16),
            vmem((HEADS, PAIR), F32),
            vmem(pairs, BF16),
            vmem((HEADS, PAIR), F32),
            vmem((2 * ROWS * HEADS // 2, PAIR), F32),
            vmem((2, 2 * ROWS, HEADS * HD), BF16),
            vmem((NDP, group_rows, width), BF16),
            vmem((NDP, group_rows, width), F32),
            vmem((NDP, group_rows, width), BF16),
            vmem((2, count, slots, width), BF16),
            vmem((2, 2, count, slots, width), BF16),
            vmem((all_slots, hidden), F32),
            vmem((all_slots, hidden), F32),
            vmem((2, all_slots, width), BF16),
            vmem((2, all_slots, width), BF16),
            vmem((2, count, slots, width), BF16),
            vmem((2, count, slots, width), BF16),
            vmem((2, group_rows, width), BF16),
            vmem((2, group_rows, width), BF16),
            vmem((2, 2, group_rows, width), BF16),
            vmem((NDP, group_rows, width), F32),
            vmem((NDP, ROWS, columns), BF16),
            dma((15,)),
            dma((N_SEM,)),
            dma((N_SEM,)),
            dma((count,)),
            dma((count,)),
            dma((count,)),
            dma((count,)),
            dma((2, count)),
            dma((2, count)),
        ],
        compiler_params=pltpu.CompilerParams(collective_id=0, has_side_effects=True, vmem_limit_bytes=44 * 2**20),
        name="layer",
    )(
        queries,
        kv_pool,
        page_table,
        held_tokens.T,
        sinks.reshape(1, HEADS),
        residual,
        route_ids.T,
        route_weights.T,
        moe_gain.reshape(1, NDP * width),
        w_gate.reshape(NDP, width, hidden),
        w_up.reshape(NDP, width, hidden),
        w_down[0].T.reshape(NDP, width, hidden),
        o_weight.T,
        attn_gain.reshape(1, NDP * width),
        qkv_weight.reshape(NDP, width, columns),
    )


def body(*args):
    return layer_call(args, lax.axis_size("expert"))


def solution(mesh):
    in_specs = (
        P(("dp", "expert"), None),
        P(("dp", "expert"), None, None),
        P(("dp", "expert"), None, None),
        P(("dp", "expert"), None),
        P(),
        P(("dp", "expert"), None),
        P(("dp", "expert"), None),
        P(("dp", "expert"), None),
        P(),
        P("expert", None, "dp"),
        P("expert", None, "dp"),
        P("expert", "dp", None),
        P(None, "dp"),
        P(),
        P(None, "dp"),
    )
    out_specs = (P(("dp", "expert"), None), P(("dp", "expert"), None))
    return jax.shard_map(body, mesh=mesh, in_specs=in_specs, out_specs=out_specs, check_vma=False)
```

```python
import math

import jax
import jax.numpy as jnp
from jax import lax
from jax.experimental import pallas as pl
from jax.experimental.pallas import tpu as pltpu
from jax.sharding import PartitionSpec as P

HEADS = 64
KVH = 8
HD = 64
TOP = 4
PAGE = 16
PPH = 16
SPAN = PPH * PAGE
WIDE = KVH * HD
PAIR = 2 * HD
ROWS = 8
NDP = 4

EPSILON = 1e-05
LIMIT = 7.0
MESH = pl.DeviceIdType.MESH
F32 = jnp.float32
BF16 = jnp.bfloat16

S_TAB, S_HELD, S_Q, S_RES, S_COM, S_SUM, S_QKV = range(0, 21, 3)
S_PAIR_N, S_PAIR_ML, S_X_N, S_OUT, S_PART, S_NEXT = range(21, 33, 2)
S_X_ML, S_LHS, S_STREAM, N_SEM = range(33, 37)
L_TAB, L_HELD, L_Q, L_POOL, L_SINK, L_IDS, L_WEIGHTS, L_RES, L_OW, L_MGAIN, L_GATE, L_UP, L_DOWN, L_AGAIN, L_QKV = range(15)


def position():
    dp = lax.axis_index("dp")
    expert = lax.axis_index("expert")
    return dp, lax.div(dp, 2), lax.rem(dp, 2), expert


def group_peer(z, c, offset):
    return lax.rem(z + offset // 2, 2) * 2 + lax.rem(c + offset % 2, 2)


def remote(src, dst, sems, sent, landed, device):
    return pltpu.make_async_remote_copy(
        src_ref=src,
        dst_ref=dst,
        send_sem=sems[0].at[sent],
        recv_sem=sems[1].at[landed],
        device_id=device,
        device_id_type=MESH,
    )


def spread_queries(wide):
    turned = pltpu.roll(wide, HD, 1)
    row = lax.broadcasted_iota(jnp.int32, (HEADS // 2, PAIR), 0)
    lane = lax.broadcasted_iota(jnp.int32, (HEADS // 2, PAIR), 1)
    odd_group = lax.rem(lax.div(row, 4), 2) == 1
    own_half = (lane >= HD) == odd_group
    even = jnp.where(own_half, jnp.where(odd_group, turned, wide), 0.0)
    odd = jnp.where(own_half, jnp.where(odd_group, wide, turned), 0.0)
    tile = lax.div(row, 8)
    parts = []
    for heads in (even, odd):
        parts.append(jnp.concatenate([jnp.where(tile == t, heads, 0.0) for t in range(4)], axis=1))
    return jnp.concatenate(parts, axis=0).astype(BF16)


def fold_values(wide):
    row = lax.broadcasted_iota(jnp.int32, (HEADS // 2, PAIR), 0)
    lane = lax.broadcasted_iota(jnp.int32, (HEADS // 2, PAIR), 1)
    odd_group = lax.rem(lax.div(row, 4), 2) == 1

    def own_tiles(base):
        return jnp.concatenate(
            [wide[base + 8 * t : base + 8 * t + 8, PAIR * t : PAIR * t + PAIR] for t in range(4)], axis=0
        )

    even, odd = own_tiles(0), own_tiles(HEADS // 2)
    even = jnp.where(odd_group, pltpu.roll(even, HD, 1), even)
    odd = jnp.where(odd_group, odd, pltpu.roll(odd, HD, 1))
    return jnp.where(lane < HD, even, odd)


def pair_columns(column):
    lane = lax.broadcasted_iota(jnp.int32, (HEADS // 2, PAIR), 1)
    return jnp.where(lane < HD, column[: HEADS // 2], column[HEADS // 2 :])


def attend(queries, tables, counts, holder, pool, rows, write):
    token = lax.broadcasted_iota(jnp.int32, (HEADS, SPAN), 1)
    scores, held = [], []
    for row in rows:
        keys = jnp.concatenate([pool[tables[row, holder, page], :, :WIDE] for page in range(PPH)], axis=0)
        start = pl.multiple_of(row * (HEADS // 2), HEADS // 2)
        spread = spread_queries(queries[pl.ds(start, HEADS // 2), :])
        scores.append(
            lax.dot_general(spread, keys, (((1,), (1,)), ((), ())), preferred_element_type=F32)
            * (1.0 / math.sqrt(HD))
        )
        held.append(token < counts[holder, row])
    weights, highs, sums = [], [], []
    for score, usable in zip(scores, held):
        high = jnp.max(jnp.where(usable, score, -1e30), axis=1, keepdims=True)
        weight = jnp.where(usable, jnp.exp(score - high), 0.0)
        highs.append(high)
        sums.append(jnp.sum(weight, axis=1, keepdims=True))
        weights.append(weight.astype(BF16))
    results = []
    for row, weight in zip(rows, weights):
        values = jnp.concatenate([pool[tables[row, holder, page], :, WIDE:] for page in range(PPH)], axis=0)
        results.append(fold_values(jnp.dot(weight, values, preferred_element_type=F32)))
    for row, result, high, total in zip(rows, results, highs, sums):
        write(row, result, high, total)


def sink_columns(sinks):
    row = lax.broadcasted_iota(jnp.int32, (HEADS, HEADS), 0)
    lane = lax.broadcasted_iota(jnp.int32, (HEADS, HEADS), 1)
    half = HEADS // 2
    head = jnp.where(row < half, 2 * row, 2 * (row - half) + 1)
    return jnp.sum(jnp.where(lane == head, sinks, 0.0), axis=1, keepdims=True)


def combine_rows(ids, weights, table, block, slots):
    capacity = slots // NDP
    lane = lax.broadcasted_iota(jnp.int32, (1, table.shape[1]), 1)
    of_expert, at_slot = lax.div(lane, slots), lax.rem(lane, slots)
    taken = jnp.zeros_like(lane)
    for row in range(ROWS):
        hit = jnp.zeros_like(lane)
        weight = jnp.zeros(lane.shape, F32)
        total = jnp.zeros(lane.shape, F32)
        for k in range(TOP):
            match = of_expert == ids[k, row]
            hit = jnp.where(match, 1, hit)
            weight = jnp.where(match, weights[k, row], weight)
            total = total + weights[k, row]
        at = (hit == 1) & (at_slot == block * capacity + taken)
        table[row : row + 1, :] = jnp.where(at, weight / total, 0.0)
        taken = taken + hit


STEP = 4


def layer_kernel(
    q_hbm, pool_hbm, tab_hbm, held_hbm, sink_hbm, res_hbm, ids_hbm, weights_hbm, mgain_hbm,
    wg_hbm, wu_hbm, wd_hbm, ow_hbm, again_hbm, wq_hbm,
    next_out, qkv_out,
    pool, ow, wg, wu, wd, wq,
    tabs, helds, ids, weights, sinks, mgain, again, gains, qraw, qwide, resraw, resblk, resall, comown, comall,
    keep_n, keep_ml, send_n, send_ml, recv_n, recv_ml, xs_n, xs_ml, xr_n, xr_ml, att, lhs, stream, sums,
    outbox, arr, gate, up, osend, orecv, rbuf, ret, part_s, part_r, nextb, nextf, qbuf,
    load_sem, send_sem, recv_sem, d_send, d_recv, f_send, f_recv, r_send, r_recv,
):
    dp, z, c, expert = position()
    sems = (send_sem, recv_sem)
    count, slots, width = arr.shape[2], arr.shape[3], arr.shape[4]
    block = c * 2 + z

    barrier = pltpu.get_barrier_semaphore()
    for offset in (1, 2, 3):
        pl.semaphore_signal(barrier, inc=1, device_id=(group_peer(z, c, offset), expert), device_id_type=MESH)

    def greet(i, carry):
        pl.semaphore_signal(barrier, inc=1, device_id=(dp, lax.rem(expert + i, count)), device_id_type=MESH)
        return carry

    lax.fori_loop(1, count, greet, 0)
    loads = {}
    for number, src, dst in (
        (L_TAB, tab_hbm, tabs.at[dp]),
        (L_HELD, held_hbm, helds.at[dp]),
        (L_Q, q_hbm, qraw.at[dp]),
        (L_POOL, pool_hbm, pool),
        (L_IDS, ids_hbm, ids),
        (L_WEIGHTS, weights_hbm, weights),
        (L_RES, res_hbm, resraw),
        (L_MGAIN, mgain_hbm, mgain),
        (L_AGAIN, again_hbm, again),
        (L_SINK, sink_hbm, sinks),
        (L_OW, ow_hbm, ow),
        (L_GATE, wg_hbm, wg),
        (L_UP, wu_hbm, wu),
        (L_DOWN, wd_hbm, wd),
        (L_QKV, wq_hbm, wq),
    ):
        loads[number] = pltpu.make_async_copy(src, dst, load_sem.at[number])
        loads[number].start()

    sent = []

    def send(src, dst, number, landed, offset):
        copy = remote(src, dst, sems, number, landed, (group_peer(z, c, offset), expert))
        copy.start()
        sent.append(copy)
        return copy

    lane = lax.broadcasted_iota(jnp.int32, (HEADS, PAIR), 1)

    def run_block(offset, number, numerators, stats):
        at = group_peer(z, c, offset)
        half = z if number == 0 else 1 - z
        stats[number] = jnp.zeros((HEADS, PAIR), F32)
        for pair in range(HEADS // 2):
            qwide[pl.ds(pair, ROWS, stride=HEADS // 2), :] = qraw[at, :, PAIR * pair : PAIR * pair + PAIR].astype(F32)

        def write(row, result, high, total):
            numerators[number, row] = result.astype(numerators.dtype)
            place = half * ROWS + row
            tile = jnp.where(lane == place, high, stats[number])
            stats[number] = jnp.where(lane == place + HD, total, tile)

        def step(index, carry):
            rows = [index * STEP + i for i in range(STEP)]
            attend(qwide, tabs.at[at], helds.at[at], dp, pool, rows, write)
            return carry

        lax.fori_loop(0, ROWS // STEP, step, 0)

    tab_in, held_in, q_in, res_in, com_in = {}, {}, {}, {}, {}

    def fetch_block(offset):
        tab_in[offset].wait_recv()
        held_in[offset].wait_recv()
        q_in[offset].wait_recv()

    def send_pair(number):
        return (
            send(send_n.at[number], recv_n.at[number], S_PAIR_N + number, S_PAIR_N + number, 1),
            send(send_ml.at[number], recv_ml.at[number], S_PAIR_ML + number, S_PAIR_ML + number, 1),
        )

    def factors(tile, number):
        half = z if number == 0 else 1 - z
        return pltpu.roll(tile, lax.rem(PAIR - half * ROWS, PAIR), 1)

    def merge_pair(number, incoming):
        for copy in incoming:
            copy.wait_recv()
        mine, other = keep_ml[number], recv_ml[number]
        high = jnp.maximum(mine, other)
        left, right = jnp.exp(mine - high), jnp.exp(other - high)
        total = mine * pltpu.roll(left, HD, 1) + other * pltpu.roll(right, HD, 1)
        keep_ml[number] = jnp.where(lane < HD, high, total)
        left, right = factors(left, number), factors(right, number)
        for row in range(ROWS):
            merged = keep_n[number, row] * pair_columns(left[:, row : row + 1]) + recv_n[number, row].astype(
                F32
            ) * pair_columns(right[:, row : row + 1])
            keep_n[number, row] = merged
            xs_n[number, row] = merged.astype(BF16)
        return send(xs_n.at[number], xr_n.at[1 - number], S_X_N + number, S_X_N + 1 - number, 2)

    for number in (L_IDS, L_WEIGHTS, L_RES, L_MGAIN, L_AGAIN):
        loads[number].wait()
    combine_rows(ids, weights, comown, block, slots)
    comall[block] = comown[...]
    for which, gain in enumerate((mgain, again)):
        whole = gain[...].reshape(1, NDP * width)
        for k in range(NDP):
            gains[which, k] = whole[:, width * k : width * k + width]
    for k in range(NDP):
        resblk[k] = resraw[:, width * k : width * k + width]
    resall[block] = resblk[dp]
    for number in (L_TAB, L_HELD, L_Q, L_POOL):
        loads[number].wait()
    run_block(0, 0, keep_n, keep_ml)

    pl.semaphore_wait(barrier, count + 2)
    for offset in (2, 1):
        q_in[offset] = send(q_hbm, qraw.at[dp], S_Q + offset - 1, S_Q + offset - 1, offset)
    for offset in (2, 3, 1):
        tab_in[offset] = send(tab_hbm, tabs.at[dp], S_TAB + offset - 1, S_TAB + offset - 1, offset)
        held_in[offset] = send(held_hbm, helds.at[dp], S_HELD + offset - 1, S_HELD + offset - 1, offset)
    for offset in (2, 3, 1):
        peer = group_peer(z, c, offset)
        res_in[offset] = send(resblk.at[peer], resall.at[block], S_RES + offset - 1, S_RES + offset - 1, offset)
        com_in[offset] = send(comown, comall.at[block], S_COM + offset - 1, S_COM + offset - 1, offset)
    fetch_block(1)
    run_block(1, 0, send_n, send_ml)
    pair_in = [send_pair(0)]
    fetch_block(2)
    cross = group_peer(z, c, 2)
    q_in[3] = send(qraw.at[cross], qraw.at[cross], S_Q + 2, S_Q + 2, 1)
    cross_in = [merge_pair(0, pair_in[0])]
    fetch_block(3)
    run_block(3, 1, send_n, send_ml)
    pair_in.append(send_pair(1))
    run_block(2, 1, keep_n, keep_ml)
    cross_in.append(merge_pair(1, pair_in[1]))
    xs_ml[...] = keep_ml[0] + keep_ml[1]
    cross_ml = send(xs_ml, xr_ml, S_X_ML, S_X_ML, 2)

    cross_ml.wait_recv()
    loads[L_SINK].wait()
    mine, other, sink = xs_ml[...], xr_ml[...], sink_columns(sinks[...])
    top = jnp.maximum(jnp.maximum(mine, other), sink)
    left, right = jnp.exp(mine - top), jnp.exp(other - top)
    total = mine * pltpu.roll(left, HD, 1) + other * pltpu.roll(right, HD, 1)
    below = pltpu.roll(total, HD, 1) + jnp.exp(sink - top)
    left, right = left / below, right / below
    for number in (0, 1):
        cross_in[1 - number].wait_recv()
        one, two = factors(left, number), factors(right, number)
        half = z if number == 0 else 1 - z
        for row in range(ROWS):
            attention = keep_n[number, row] * pair_columns(one[:, row : row + 1]) + xr_n[number, row].astype(
                F32
            ) * pair_columns(two[:, row : row + 1])
            start = pl.multiple_of((half * ROWS + row) * (HEADS // 2), HEADS // 2)
            att[pl.ds(start, HEADS // 2), :] = attention
    for pair in range(HEADS // 2):
        lhs[c, :, PAIR * pair : PAIR * pair + PAIR] = att[pl.ds(pair, 2 * ROWS, stride=HEADS // 2), :].astype(BF16)
    lhs_in = send(lhs.at[c], lhs.at[c], S_LHS, S_LHS, 1)
    loads[L_OW].wait()
    lhs_in.wait_recv()
    rows = jnp.concatenate([lhs[0], lhs[1]], axis=0)
    projected = lax.dot_general(rows, ow[...], (((1,), (1,)), ((), ())), preferred_element_type=F32)
    for offset in (1, 2, 3):
        res_in[offset].wait_recv()
    residual = jnp.concatenate([resall[d].astype(F32) for d in range(NDP)], axis=0)
    stream[z] = (residual + projected.astype(BF16).astype(F32)).astype(BF16)
    stream_in = send(stream.at[z], stream.at[z], S_STREAM, S_STREAM, 2)
    own = stream[z].astype(F32)
    sums[dp] = jnp.broadcast_to(jnp.sum(own * own, axis=1, keepdims=True), sums.shape[1:])
    sum_in = [
        send(sums.at[dp], sums.at[dp], S_SUM + offset - 1, S_SUM + offset - 1, offset) for offset in (2, 3, 1)
    ]
    for offset in (1, 2, 3):
        com_in[offset].wait_recv()
    share = jnp.concatenate([comall[d] for d in range(NDP)], axis=0)
    picks = (share > 0).astype(F32).T.astype(BF16)
    for copy in sum_in:
        copy.wait_recv()
    scale = lax.rsqrt((sums[0] + sums[1] + sums[2] + sums[3]) / (NDP * width) + EPSILON)[:, :1]
    stream_in.wait_recv()
    for j in range(2):
        rows = (stream[j].astype(F32) * scale * gains[0, 2 * j + c]).astype(BF16)
        picked = jnp.dot(picks, rows, preferred_element_type=F32).astype(BF16)
        outbox[j] = picked.reshape(count, slots, width)

    def dispatch(to, slot):
        return remote(outbox.at[:, to], arr.at[c, :, slot], (d_send, d_recv), to, slot, (dp, to))

    def forward(source):
        return remote(
            arr.at[c, :, source], arr.at[c, :, source], (f_send, f_recv), source, source,
            (group_peer(z, c, 1), expert),
        )

    def giveback(j, to, slot):
        return remote(rbuf.at[j, to], ret.at[j, slot], (r_send.at[j], r_recv.at[j]), to, slot, (dp, to))

    def start_dispatch(i, carry):
        dispatch(lax.rem(expert + i, count), expert).start()
        return carry

    lax.fori_loop(1, count, start_dispatch, 0)
    for j in range(2):
        arr[c, j, expert] = outbox[j, expert]
    forward(expert).start()

    def pass_on(i, carry):
        source = lax.rem(expert + count - i, count)
        dispatch(source, source).wait_recv()
        forward(source).start()
        return carry

    lax.fori_loop(1, count, pass_on, 0)
    loads[L_GATE].wait()
    loads[L_UP].wait()

    def project(half, first):
        for j in range(2):
            rows = arr[half, j].reshape(count * slots, width)
            for total, weight in ((gate, wg), (up, wu)):
                value = jnp.dot(rows, weight[2 * j + half], preferred_element_type=F32)
                if first and j == 0:
                    total[...] = value
                else:
                    total[...] += value

    project(c, True)

    def arrived(source, carry):
        forward(source).wait_recv()
        return carry

    lax.fori_loop(0, count, arrived, 0)
    project(1 - c, False)
    gated = jnp.minimum(gate[...], LIMIT)
    lifted = jnp.clip(up[...], -LIMIT, LIMIT)
    activated = (gated * jax.nn.sigmoid(1.702 * gated) * (lifted + 1.0)).astype(BF16)
    loads[L_DOWN].wait()

    def down(k):
        return lax.dot_general(activated, wd[k], (((1,), (1,)), ((), ())), preferred_element_type=F32)

    pair_in = []
    for j in range(2):
        osend[j] = down(2 * j + 1 - c).astype(BF16)
        pair_in.append(send(osend.at[j], orecv.at[j], S_OUT + j, S_OUT + j, 1))
    for j in range(2):
        own = down(2 * j + c)
        pair_in[j].wait_recv()
        rbuf[j] = (own + orecv[j].astype(F32)).astype(BF16).reshape(count, slots, width)

        def start_return(i, carry):
            giveback(j, lax.rem(expert + i, count), expert).start()
            return carry

        lax.fori_loop(1, count, start_return, 0)
        ret[j, expert] = rbuf[j, expert]

    high = share.astype(BF16)
    low = (share - high.astype(F32)).astype(BF16)
    both = jnp.concatenate([high, low], axis=0)
    group_rows = share.shape[0]
    part_in = []
    for j in range(2):

        def returned(source, carry):
            @pl.when(source != expert)
            def _():
                giveback(j, source, source).wait_recv()

            return carry

        lax.fori_loop(0, count, returned, 0)
        mixed = jnp.dot(both, ret[j].reshape(count * slots, width), preferred_element_type=F32)
        part_s[j] = (mixed[:group_rows] + mixed[group_rows:]).astype(BF16)
        part_in.append(send(part_s.at[j], part_r.at[j], S_PART + j, S_PART + j, 2))
    loads[L_QKV].wait()
    next_in = []
    qkv = jnp.zeros((group_rows, wq.shape[2]), F32)
    squares = jnp.zeros((group_rows, 1), F32)

    def project_next(half, j, qkv, squares):
        k = 2 * j + half
        rows = nextb[half, j].astype(F32)
        nextf[k] = rows
        squares += jnp.sum(rows * rows, axis=1, keepdims=True)
        qkv += jnp.dot((rows * gains[1, k]).astype(BF16), wq[k], preferred_element_type=F32)
        return qkv, squares

    for j in range(2):
        part_in[j].wait_recv()
        moe_out = part_s[j].astype(F32) + part_r[j].astype(F32)
        nextb[c, j] = (stream[j].astype(F32) + moe_out).astype(BF16)
        next_in.append(send(nextb.at[c, j], nextb.at[c, j], S_NEXT + j, S_NEXT + j, 1))
        qkv, squares = project_next(c, j, qkv, squares)
    for j in range(2):
        next_in[j].wait_recv()
        qkv, squares = project_next(1 - c, j, qkv, squares)
    qkv = qkv * lax.rsqrt(squares / (NDP * width) + EPSILON)
    columns = qkv.shape[1]
    for d in range(NDP):
        qbuf[d] = qkv[ROWS * d : ROWS * d + ROWS].astype(BF16)
    own_columns = pl.ds(pl.multiple_of(dp * columns, 128), columns)
    qkv_in = []
    for offset in (2, 3, 1):
        peer = group_peer(z, c, offset)
        theirs = lax.rem(peer, 2) * 2 + lax.div(peer, 2)
        qkv_in.append(
            send(qbuf.at[theirs], qkv_out.at[:, own_columns], S_QKV + offset - 1, S_QKV + offset - 1, offset)
        )
    qkv_out[:, own_columns] = qbuf[block]
    start = pl.multiple_of(block * ROWS, ROWS)
    for k in range(NDP):
        next_out[:, width * k : width * k + width] = nextf[k, pl.ds(start, ROWS), :].astype(BF16)

    def all_sent(i, carry):
        to = lax.rem(expert + i, count)
        dispatch(to, expert).wait_send()
        for j in range(2):
            giveback(j, to, expert).wait_send()
        return carry

    lax.fori_loop(1, count, all_sent, 0)

    def all_passed(source, carry):
        forward(source).wait_send()
        return carry

    lax.fori_loop(0, count, all_passed, 0)
    for copy in sent:
        copy.wait_send()
    for copy in qkv_in:
        copy.wait_recv()


def layer_call(args, count):
    (queries, kv_pool, page_table, held_tokens, sinks, residual, route_ids, route_weights, moe_gain,
     w_gate, w_up, w_down, o_weight, attn_gain, qkv_weight) = args
    width = residual.shape[1] // NDP
    hidden = w_gate.shape[2]
    columns = qkv_weight.shape[1]
    slots = NDP * (2 * ROWS * TOP // count)
    group_rows = NDP * ROWS
    all_slots = count * slots
    hbm = pl.BlockSpec(memory_space=pltpu.HBM)
    out = pl.BlockSpec(memory_space=pltpu.VMEM)
    vmem, dma = pltpu.VMEM, pltpu.SemaphoreType.DMA
    pairs = (2, ROWS, HEADS // 2, PAIR)
    return pl.pallas_call(
        layer_kernel,
        out_shape=(
            jax.ShapeDtypeStruct((ROWS, NDP * width), BF16),
            jax.ShapeDtypeStruct((ROWS, NDP * columns), BF16),
        ),
        in_specs=[hbm] * 15,
        out_specs=(out, out),
        scratch_shapes=[
            vmem(kv_pool.shape, BF16),
            vmem((width, HEADS * HD), BF16),
            vmem((NDP, width, hidden), BF16),
            vmem((NDP, width, hidden), BF16),
            vmem((NDP, width, hidden), BF16),
            vmem((NDP, width, columns), BF16),
            pltpu.SMEM((NDP,) + page_table.shape, jnp.int32),
            pltpu.SMEM((NDP, NDP, ROWS), jnp.int32),
            pltpu.SMEM((TOP, ROWS), jnp.int32),
            pltpu.SMEM((TOP, ROWS), F32),
            vmem((1, HEADS), F32),
            vmem((NDP * width,), F32),
            vmem((NDP * width,), F32),
            vmem((2, NDP, 1, width), F32),
            vmem((NDP, ROWS, HEADS * HD), BF16),
            vmem((ROWS * HEADS // 2, PAIR), F32),
            vmem((ROWS, NDP * width), BF16),
            vmem((NDP, ROWS, width), BF16),
            vmem((NDP, ROWS, width), BF16),
            vmem((ROWS, all_slots), F32),
            vmem((NDP, ROWS, all_slots), F32),
            vmem(pairs, F32),
            vmem((2, HEADS, PAIR), F32),
            vmem(pairs, BF16),
            vmem((2, HEADS, PAIR), F32),
            vmem(pairs, BF16),
            vmem((2, HEADS, PAIR), F32),
            vmem(pairs, BF16),
            vmem((HEADS, PAIR), F32),
            vmem(pairs, BF16),
            vmem((HEADS, PAIR), F32),
            vmem((2 * ROWS * HEADS // 2, PAIR), F32),
            vmem((2, 2 * ROWS, HEADS * HD), BF16),
            vmem((2, group_rows, width), BF16),
            vmem((NDP, group_rows, 128), F32),
            vmem((2, count, slots, width), BF16),
            vmem((2, 2, count, slots, width), BF16),
            vmem((all_slots, hidden), F32),
            vmem((all_slots, hidden), F32),
            vmem((2, all_slots, width), BF16),
            vmem((2, all_slots, width), BF16),
            vmem((2, count, slots, width), BF16),
            vmem((2, count, slots, width), BF16),
            vmem((2, group_rows, width), BF16),
            vmem((2, group_rows, width), BF16),
            vmem((2, 2, group_rows, width), BF16),
            vmem((NDP, group_rows, width), F32),
            vmem((NDP, ROWS, columns), BF16),
            dma((15,)),
            dma((N_SEM,)),
            dma((N_SEM,)),
            dma((count,)),
            dma((count,)),
            dma((count,)),
            dma((count,)),
            dma((2, count)),
            dma((2, count)),
        ],
        compiler_params=pltpu.CompilerParams(collective_id=0, has_side_effects=True, vmem_limit_bytes=44 * 2**20),
        name="layer",
    )(*[pltpu.with_memory_space_constraint(x, pltpu.HBM) for x in (
        queries,
        kv_pool,
        page_table,
        held_tokens.T,
        sinks.reshape(1, HEADS),
        residual,
        route_ids.T,
        route_weights.T,
        moe_gain,
        w_gate.reshape(NDP, width, hidden),
        w_up.reshape(NDP, width, hidden),
        w_down[0].T.reshape(NDP, width, hidden),
        o_weight.T,
        attn_gain,
        qkv_weight.reshape(NDP, width, columns),
    )])


def body(*args):
    return layer_call(args, lax.axis_size("expert"))


def solution(mesh):
    in_specs = (
        P(("dp", "expert"), None),
        P(("dp", "expert"), None, None),
        P(("dp", "expert"), None, None),
        P(("dp", "expert"), None),
        P(),
        P(("dp", "expert"), None),
        P(("dp", "expert"), None),
        P(("dp", "expert"), None),
        P(),
        P("expert", None, "dp"),
        P("expert", None, "dp"),
        P("expert", "dp", None),
        P(None, "dp"),
        P(),
        P(None, "dp"),
    )
    out_specs = (P(("dp", "expert"), None), P(("dp", "expert"), None))
    return jax.shard_map(body, mesh=mesh, in_specs=in_specs, out_specs=out_specs, check_vma=False)
```

```python
import math

import jax
import jax.numpy as jnp
from jax import lax
from jax.experimental import pallas as pl
from jax.experimental.pallas import tpu as pltpu
from jax.sharding import PartitionSpec as P

HEADS = 64
KVH = 8
HD = 64
TOP = 4
PAGE = 16
PPH = 16
SPAN = PPH * PAGE
WIDE = KVH * HD
PAIR = 2 * HD
ROWS = 8
NDP = 4

EPSILON = 1e-05
LIMIT = 7.0
MESH = pl.DeviceIdType.MESH
F32 = jnp.float32
BF16 = jnp.bfloat16

S_TAB, S_HELD, S_Q, S_RES, S_COM, S_SUM, S_QKV = range(0, 21, 3)
S_PAIR_N, S_PAIR_ML, S_X_N, S_PART, S_NEXT = range(21, 31, 2)
S_X_ML, S_LHS, S_STREAM, S_OUT, N_SEM = 31, 32, 33, 34, 38
L_TAB, L_HELD, L_Q, L_POOL, L_SINK, L_IDS, L_WEIGHTS, L_RES, L_OW, L_MGAIN, L_GATE, L_UP, L_DOWN, L_AGAIN, L_QKV = range(15)


def position():
    dp = lax.axis_index("dp")
    expert = lax.axis_index("expert")
    return dp, lax.div(dp, 2), lax.rem(dp, 2), expert


def group_peer(z, c, offset):
    return lax.rem(z + offset // 2, 2) * 2 + lax.rem(c + offset % 2, 2)


def remote(src, dst, sems, sent, landed, device):
    return pltpu.make_async_remote_copy(
        src_ref=src,
        dst_ref=dst,
        send_sem=sems[0].at[sent],
        recv_sem=sems[1].at[landed],
        device_id=device,
        device_id_type=MESH,
    )


def spread_queries(wide):
    turned = pltpu.roll(wide, HD, 1)
    row = lax.broadcasted_iota(jnp.int32, (HEADS // 2, PAIR), 0)
    lane = lax.broadcasted_iota(jnp.int32, (HEADS // 2, PAIR), 1)
    odd_group = lax.rem(lax.div(row, 4), 2) == 1
    own_half = (lane >= HD) == odd_group
    even = jnp.where(own_half, jnp.where(odd_group, turned, wide), 0.0)
    odd = jnp.where(own_half, jnp.where(odd_group, wide, turned), 0.0)
    tile = lax.div(row, 8)
    parts = []
    for heads in (even, odd):
        parts.append(jnp.concatenate([jnp.where(tile == t, heads, 0.0) for t in range(4)], axis=1))
    return jnp.concatenate(parts, axis=0).astype(BF16)


def fold_values(wide):
    row = lax.broadcasted_iota(jnp.int32, (HEADS // 2, PAIR), 0)
    lane = lax.broadcasted_iota(jnp.int32, (HEADS // 2, PAIR), 1)
    odd_group = lax.rem(lax.div(row, 4), 2) == 1

    def own_tiles(base):
        return jnp.concatenate(
            [wide[base + 8 * t : base + 8 * t + 8, PAIR * t : PAIR * t + PAIR] for t in range(4)], axis=0
        )

    even, odd = own_tiles(0), own_tiles(HEADS // 2)
    even = jnp.where(odd_group, pltpu.roll(even, HD, 1), even)
    odd = jnp.where(odd_group, odd, pltpu.roll(odd, HD, 1))
    return jnp.where(lane < HD, even, odd)


def pair_columns(column):
    lane = lax.broadcasted_iota(jnp.int32, (HEADS // 2, PAIR), 1)
    return jnp.where(lane < HD, column[: HEADS // 2], column[HEADS // 2 :])


def attend(queries, tables, counts, holder, pool, rows, write):
    token = lax.broadcasted_iota(jnp.int32, (HEADS, SPAN), 1)
    scores, held = [], []
    for row in rows:
        keys = jnp.concatenate([pool[tables[row, holder, page], :, :WIDE] for page in range(PPH)], axis=0)
        start = pl.multiple_of(row * (HEADS // 2), HEADS // 2)
        spread = spread_queries(queries[pl.ds(start, HEADS // 2), :])
        scores.append(
            lax.dot_general(spread, keys, (((1,), (1,)), ((), ())), preferred_element_type=F32)
            * (1.0 / math.sqrt(HD))
        )
        held.append(token < counts[holder, row])
    weights, highs, sums = [], [], []
    for score, usable in zip(scores, held):
        high = jnp.max(jnp.where(usable, score, -1e30), axis=1, keepdims=True)
        weight = jnp.where(usable, jnp.exp(score - high), 0.0)
        highs.append(high)
        sums.append(jnp.sum(weight, axis=1, keepdims=True))
        weights.append(weight.astype(BF16))
    results = []
    for row, weight in zip(rows, weights):
        values = jnp.concatenate([pool[tables[row, holder, page], :, WIDE:] for page in range(PPH)], axis=0)
        results.append(fold_values(jnp.dot(weight, values, preferred_element_type=F32)))
    for row, result, high, total in zip(rows, results, highs, sums):
        write(row, result, high, total)


def sink_columns(sinks):
    row = lax.broadcasted_iota(jnp.int32, (HEADS, HEADS), 0)
    lane = lax.broadcasted_iota(jnp.int32, (HEADS, HEADS), 1)
    half = HEADS // 2
    head = jnp.where(row < half, 2 * row, 2 * (row - half) + 1)
    return jnp.sum(jnp.where(lane == head, sinks, 0.0), axis=1, keepdims=True)


def combine_rows(ids, weights, table, block, slots):
    capacity = slots // NDP
    lane = lax.broadcasted_iota(jnp.int32, (1, table.shape[1]), 1)
    of_expert, at_slot = lax.div(lane, slots), lax.rem(lane, slots)
    taken = jnp.zeros_like(lane)
    for row in range(ROWS):
        hit = jnp.zeros_like(lane)
        weight = jnp.zeros(lane.shape, F32)
        total = jnp.zeros(lane.shape, F32)
        for k in range(TOP):
            match = of_expert == ids[k, row]
            hit = jnp.where(match, 1, hit)
            weight = jnp.where(match, weights[k, row], weight)
            total = total + weights[k, row]
        at = (hit == 1) & (at_slot == block * capacity + taken)
        table[row : row + 1, :] = jnp.where(at, weight / total, 0.0)
        taken = taken + hit


STEP = 4


def layer_kernel(
    q_hbm, pool_hbm, tab_hbm, held_hbm, sink_hbm, res_hbm, ids_hbm, weights_hbm, mgain_hbm,
    wg_hbm, wu_hbm, wd_hbm, ow_hbm, again_hbm, wq_hbm,
    next_out, qkv_out,
    pool, ow, wg, wu, wd, wq,
    tabs, helds, ids, weights, sinks, mgain, again, gains, qraw, qwide, resraw, resblk, resall, comown, comall,
    keep_n, keep_ml, send_n, send_ml, recv_n, recv_ml, xs_n, xs_ml, xr_n, xr_ml, att, lhs, stream, sums,
    outbox, arr, gate, up, osend, orecv, kept, rbuf, ret, part_s, part_r, nextb, nextf, qbuf,
    load_sem, send_sem, recv_sem, d_send, d_recv, f_send, f_recv, r_send, r_recv,
):
    dp, z, c, expert = position()
    sems = (send_sem, recv_sem)
    count, slots, width = arr.shape[2], arr.shape[3], arr.shape[4]
    block = c * 2 + z

    barrier = pltpu.get_barrier_semaphore()
    for offset in (1, 2, 3):
        pl.semaphore_signal(barrier, inc=1, device_id=(group_peer(z, c, offset), expert), device_id_type=MESH)

    def greet(i, carry):
        pl.semaphore_signal(barrier, inc=1, device_id=(dp, lax.rem(expert + i, count)), device_id_type=MESH)
        return carry

    lax.fori_loop(1, count, greet, 0)
    loads = {}
    for number, src, dst in (
        (L_TAB, tab_hbm, tabs.at[dp]),
        (L_HELD, held_hbm, helds.at[dp]),
        (L_Q, q_hbm, qraw.at[dp]),
        (L_POOL, pool_hbm, pool),
        (L_IDS, ids_hbm, ids),
        (L_WEIGHTS, weights_hbm, weights),
        (L_RES, res_hbm, resraw),
        (L_MGAIN, mgain_hbm, mgain),
        (L_AGAIN, again_hbm, again),
        (L_SINK, sink_hbm, sinks),
        (L_OW, ow_hbm, ow),
        (L_GATE, wg_hbm, wg),
        (L_UP, wu_hbm, wu),
        (L_DOWN, wd_hbm, wd),
        (L_QKV, wq_hbm, wq),
    ):
        loads[number] = pltpu.make_async_copy(src, dst, load_sem.at[number])
        loads[number].start()

    sent = []

    def send(src, dst, number, landed, offset):
        copy = remote(src, dst, sems, number, landed, (group_peer(z, c, offset), expert))
        copy.start()
        sent.append(copy)
        return copy

    lane = lax.broadcasted_iota(jnp.int32, (HEADS, PAIR), 1)

    def run_block(offset, number, numerators, stats):
        at = group_peer(z, c, offset)
        half = z if number == 0 else 1 - z
        stats[number] = jnp.zeros((HEADS, PAIR), F32)
        for pair in range(HEADS // 2):
            qwide[pl.ds(pair, ROWS, stride=HEADS // 2), :] = qraw[at, :, PAIR * pair : PAIR * pair + PAIR].astype(F32)

        def write(row, result, high, total):
            numerators[number, row] = result.astype(numerators.dtype)
            place = half * ROWS + row
            tile = jnp.where(lane == place, high, stats[number])
            stats[number] = jnp.where(lane == place + HD, total, tile)

        def step(index, carry):
            rows = [index * STEP + i for i in range(STEP)]
            attend(qwide, tabs.at[at], helds.at[at], dp, pool, rows, write)
            return carry

        lax.fori_loop(0, ROWS // STEP, step, 0)

    tab_in, held_in, q_in, res_in, com_in = {}, {}, {}, {}, {}

    def fetch_block(offset):
        tab_in[offset].wait_recv()
        held_in[offset].wait_recv()
        q_in[offset].wait_recv()

    def send_pair(number):
        return (
            send(send_n.at[number], recv_n.at[number], S_PAIR_N + number, S_PAIR_N + number, 1),
            send(send_ml.at[number], recv_ml.at[number], S_PAIR_ML + number, S_PAIR_ML + number, 1),
        )

    def factors(tile, number):
        half = z if number == 0 else 1 - z
        return pltpu.roll(tile, lax.rem(PAIR - half * ROWS, PAIR), 1)

    def merge_pair(number, incoming):
        for copy in incoming:
            copy.wait_recv()
        mine, other = keep_ml[number], recv_ml[number]
        high = jnp.maximum(mine, other)
        left, right = jnp.exp(mine - high), jnp.exp(other - high)
        total = mine * pltpu.roll(left, HD, 1) + other * pltpu.roll(right, HD, 1)
        keep_ml[number] = jnp.where(lane < HD, high, total)
        left, right = factors(left, number), factors(right, number)
        for row in range(ROWS):
            merged = keep_n[number, row] * pair_columns(left[:, row : row + 1]) + recv_n[number, row].astype(
                F32
            ) * pair_columns(right[:, row : row + 1])
            keep_n[number, row] = merged
            xs_n[number, row] = merged.astype(BF16)
        return send(xs_n.at[number], xr_n.at[1 - number], S_X_N + number, S_X_N + 1 - number, 2)

    for number in (L_IDS, L_WEIGHTS, L_RES, L_MGAIN, L_AGAIN):
        loads[number].wait()
    combine_rows(ids, weights, comown, block, slots)
    comall[block] = comown[...]
    for which, gain in enumerate((mgain, again)):
        whole = gain[...].reshape(1, NDP * width)
        for k in range(NDP):
            gains[which, k] = whole[:, width * k : width * k + width]
    for k in range(NDP):
        resblk[k] = resraw[:, width * k : width * k + width]
    resall[block] = resblk[dp]
    for number in (L_TAB, L_HELD, L_Q, L_POOL):
        loads[number].wait()
    run_block(0, 0, keep_n, keep_ml)

    pl.semaphore_wait(barrier, count + 2)
    for offset in (2, 1):
        q_in[offset] = send(q_hbm, qraw.at[dp], S_Q + offset - 1, S_Q + offset - 1, offset)
    for offset in (2, 3, 1):
        tab_in[offset] = send(tab_hbm, tabs.at[dp], S_TAB + offset - 1, S_TAB + offset - 1, offset)
        held_in[offset] = send(held_hbm, helds.at[dp], S_HELD + offset - 1, S_HELD + offset - 1, offset)
    for offset in (2, 3, 1):
        peer = group_peer(z, c, offset)
        res_in[offset] = send(resblk.at[peer], resall.at[block], S_RES + offset - 1, S_RES + offset - 1, offset)
        com_in[offset] = send(comown, comall.at[block], S_COM + offset - 1, S_COM + offset - 1, offset)
    fetch_block(1)
    run_block(1, 0, send_n, send_ml)
    pair_in = [send_pair(0)]
    fetch_block(2)
    cross = group_peer(z, c, 2)
    q_in[3] = send(qraw.at[cross], qraw.at[cross], S_Q + 2, S_Q + 2, 1)
    cross_in = [merge_pair(0, pair_in[0])]
    fetch_block(3)
    run_block(3, 1, send_n, send_ml)
    pair_in.append(send_pair(1))
    run_block(2, 1, keep_n, keep_ml)
    cross_in.append(merge_pair(1, pair_in[1]))
    xs_ml[...] = keep_ml[0] + keep_ml[1]
    cross_ml = send(xs_ml, xr_ml, S_X_ML, S_X_ML, 2)

    cross_ml.wait_recv()
    loads[L_SINK].wait()
    mine, other, sink = xs_ml[...], xr_ml[...], sink_columns(sinks[...])
    top = jnp.maximum(jnp.maximum(mine, other), sink)
    left, right = jnp.exp(mine - top), jnp.exp(other - top)
    total = mine * pltpu.roll(left, HD, 1) + other * pltpu.roll(right, HD, 1)
    below = pltpu.roll(total, HD, 1) + jnp.exp(sink - top)
    left, right = left / below, right / below
    for number in (0, 1):
        cross_in[1 - number].wait_recv()
        one, two = factors(left, number), factors(right, number)
        half = z if number == 0 else 1 - z
        for row in range(ROWS):
            attention = keep_n[number, row] * pair_columns(one[:, row : row + 1]) + xr_n[number, row].astype(
                F32
            ) * pair_columns(two[:, row : row + 1])
            start = pl.multiple_of((half * ROWS + row) * (HEADS // 2), HEADS // 2)
            att[pl.ds(start, HEADS // 2), :] = attention
    for pair in range(HEADS // 2):
        lhs[c, :, PAIR * pair : PAIR * pair + PAIR] = att[pl.ds(pair, 2 * ROWS, stride=HEADS // 2), :].astype(BF16)
    lhs_in = send(lhs.at[c], lhs.at[c], S_LHS, S_LHS, 1)
    loads[L_OW].wait()
    lhs_in.wait_recv()
    rows = jnp.concatenate([lhs[0], lhs[1]], axis=0)
    projected = lax.dot_general(rows, ow[...], (((1,), (1,)), ((), ())), preferred_element_type=F32)
    for offset in (1, 2, 3):
        res_in[offset].wait_recv()
    residual = jnp.concatenate([resall[d].astype(F32) for d in range(NDP)], axis=0)
    stream[z] = (residual + projected.astype(BF16).astype(F32)).astype(BF16)
    stream_in = send(stream.at[z], stream.at[z], S_STREAM, S_STREAM, 2)
    own = stream[z].astype(F32)
    group_rows = own.shape[0]
    diagonal = lax.broadcasted_iota(jnp.int32, (group_rows, 128), 0) == lax.broadcasted_iota(
        jnp.int32, (group_rows, 128), 1
    )
    square = jnp.sum(own * own, axis=1, keepdims=True)
    sums[dp] = jnp.broadcast_to(
        jnp.sum(jnp.where(diagonal, square, 0.0), axis=0, keepdims=True), sums.shape[1:]
    )
    sum_in = [
        send(sums.at[dp], sums.at[dp], S_SUM + offset - 1, S_SUM + offset - 1, offset) for offset in (2, 3, 1)
    ]
    for offset in (1, 2, 3):
        com_in[offset].wait_recv()
    share = jnp.concatenate([comall[d] for d in range(NDP)], axis=0)
    picks = (share > 0).astype(F32).T.astype(BF16)
    for copy in sum_in:
        copy.wait_recv()
    square = (sums[0] + sums[1] + sums[2] + sums[3])[:1]
    square = jnp.sum(jnp.where(diagonal, square, 0.0), axis=1, keepdims=True)
    scale = lax.rsqrt(square / (NDP * width) + EPSILON)
    stream_in.wait_recv()
    for j in range(2):
        rows = (stream[j].astype(F32) * scale * gains[0, 2 * j + c]).astype(BF16)
        picked = jnp.dot(picks, rows, preferred_element_type=F32).astype(BF16)
        outbox[j] = picked.reshape(count, slots, width)

    def partner(place, sign):
        dy = 2 * lax.rem(lax.div(place, 8), 2) + lax.div(place, 16)
        dz, dx = lax.rem(lax.div(place, 4), 2), lax.rem(place, 4)
        at_z = lax.rem(lax.div(expert, 16) + dz, 2)
        at_y = lax.rem(lax.rem(lax.div(expert, 4), 4) + sign * dy + 4, 4)
        at_x = lax.rem(lax.rem(expert, 4) + sign * dx + 4, 4)
        return 16 * at_z + 4 * at_y + at_x

    def dispatch(place):
        to = partner(place, 1)
        return remote(outbox.at[:, to], arr.at[c, :, place], (d_send, d_recv), place, place, (dp, to))

    def forward(place):
        return remote(
            arr.at[c, :, place], arr.at[c, :, place], (f_send, f_recv), place, place,
            (group_peer(z, c, 1), expert),
        )

    def giveback(j, place):
        to = partner(place, -1)
        return remote(
            rbuf.at[j, place], ret.at[j, expert], (r_send.at[j], r_recv.at[j]), place, place, (dp, to)
        )

    def each(first, last, act):
        def step(place, carry):
            act(place)
            return carry

        lax.fori_loop(first, last, step, 0)

    batch = count // 2
    batch_rows = batch * slots

    def pass_on(place):
        dispatch(place).wait_recv()
        forward(place).start()

    def project(first_place, half, first):
        for j in range(2):
            rows = arr[half, j, first_place : first_place + batch].reshape(batch_rows, width)
            for total, weight in ((gate, wg), (up, wu)):
                value = jnp.dot(rows, weight[2 * j + half], preferred_element_type=F32)
                if first and j == 0:
                    total[...] = value
                else:
                    total[...] += value

    def apply_experts(number):
        first_place = number * batch
        project(first_place, c, True)
        each(first_place, first_place + batch, lambda place: forward(place).wait_recv())
        project(first_place, 1 - c, False)
        gated = jnp.minimum(gate[...], LIMIT)
        lifted = jnp.clip(up[...], -LIMIT, LIMIT)
        activated = (gated * jax.nn.sigmoid(1.702 * gated) * (lifted + 1.0)).astype(BF16)

        def down(k):
            return lax.dot_general(activated, wd[k], (((1,), (1,)), ((), ())), preferred_element_type=F32)

        incoming = []
        for j in range(2):
            osend[number, j] = down(2 * j + 1 - c).astype(BF16)
            at = S_OUT + 2 * number + j
            incoming.append(send(osend.at[number, j], orecv.at[number, j], at, at, 1))
        for j in range(2):
            kept[j] = down(2 * j + c)
        return incoming

    def give_back(number, incoming):
        first_place = number * batch
        for j in range(2):
            incoming[j].wait_recv()
            total = (kept[j] + orecv[number, j].astype(F32)).astype(BF16)
            rbuf[j, first_place : first_place + batch] = total.reshape(batch, slots, width)
            each(max(first_place, 1), first_place + batch, lambda place: giveback(j, place).start())

    each(1, count, lambda place: dispatch(place).start())
    for j in range(2):
        arr[c, j, 0] = outbox[j, expert]
    forward(0).start()
    each(1, batch, pass_on)
    for number in (L_GATE, L_UP, L_DOWN):
        loads[number].wait()
    incoming = apply_experts(0)
    each(batch, count, pass_on)
    give_back(0, incoming)
    incoming = apply_experts(1)
    give_back(1, incoming)
    for j in range(2):
        ret[j, expert] = rbuf[j, 0]

    high = share.astype(BF16)
    low = (share - high.astype(F32)).astype(BF16)
    both = jnp.concatenate([high, low], axis=0)
    part_in = []
    for j in range(2):
        each(1, count, lambda place: giveback(j, place).wait_recv())
        mixed = jnp.dot(both, ret[j].reshape(count * slots, width), preferred_element_type=F32)
        part_s[j] = (mixed[:group_rows] + mixed[group_rows:]).astype(BF16)
        part_in.append(send(part_s.at[j], part_r.at[j], S_PART + j, S_PART + j, 2))
    loads[L_QKV].wait()
    next_in = []
    qkv = jnp.zeros((group_rows, wq.shape[2]), F32)
    squares = jnp.zeros((group_rows, 1), F32)

    def project_next(half, j, qkv, squares):
        k = 2 * j + half
        rows = nextb[half, j].astype(F32)
        nextf[k] = rows
        squares += jnp.sum(rows * rows, axis=1, keepdims=True)
        qkv += jnp.dot((rows * gains[1, k]).astype(BF16), wq[k], preferred_element_type=F32)
        return qkv, squares

    for j in range(2):
        part_in[j].wait_recv()
        moe_out = part_s[j].astype(F32) + part_r[j].astype(F32)
        nextb[c, j] = (stream[j].astype(F32) + moe_out).astype(BF16)
        next_in.append(send(nextb.at[c, j], nextb.at[c, j], S_NEXT + j, S_NEXT + j, 1))
        qkv, squares = project_next(c, j, qkv, squares)
    for j in range(2):
        next_in[j].wait_recv()
        qkv, squares = project_next(1 - c, j, qkv, squares)
    qkv = qkv * lax.rsqrt(squares / (NDP * width) + EPSILON)
    columns = qkv.shape[1]
    for d in range(NDP):
        qbuf[d] = qkv[ROWS * d : ROWS * d + ROWS].astype(BF16)
    own_columns = pl.ds(pl.multiple_of(dp * columns, 128), columns)
    qkv_in = []
    for offset in (2, 3, 1):
        peer = group_peer(z, c, offset)
        theirs = lax.rem(peer, 2) * 2 + lax.div(peer, 2)
        qkv_in.append(
            send(qbuf.at[theirs], qkv_out.at[:, own_columns], S_QKV + offset - 1, S_QKV + offset - 1, offset)
        )
    qkv_out[:, own_columns] = qbuf[block]
    start = pl.multiple_of(block * ROWS, ROWS)
    for k in range(NDP):
        next_out[:, width * k : width * k + width] = nextf[k, pl.ds(start, ROWS), :].astype(BF16)

    def all_sent(place):
        dispatch(place).wait_send()
        for j in range(2):
            giveback(j, place).wait_send()

    each(1, count, all_sent)
    each(0, count, lambda place: forward(place).wait_send())
    for copy in sent:
        copy.wait_send()
    for copy in qkv_in:
        copy.wait_recv()


def layer_call(args, count):
    (queries, kv_pool, page_table, held_tokens, sinks, residual, route_ids, route_weights, moe_gain,
     w_gate, w_up, w_down, o_weight, attn_gain, qkv_weight) = args
    width = residual.shape[1] // NDP
    hidden = w_gate.shape[2]
    columns = qkv_weight.shape[1]
    slots = NDP * (2 * ROWS * TOP // count)
    group_rows = NDP * ROWS
    all_slots = count * slots
    hbm = pl.BlockSpec(memory_space=pltpu.HBM)
    out = pl.BlockSpec(memory_space=pltpu.VMEM)
    vmem, dma = pltpu.VMEM, pltpu.SemaphoreType.DMA
    pairs = (2, ROWS, HEADS // 2, PAIR)
    return pl.pallas_call(
        layer_kernel,
        out_shape=(
            jax.ShapeDtypeStruct((ROWS, NDP * width), BF16),
            jax.ShapeDtypeStruct((ROWS, NDP * columns), BF16),
        ),
        in_specs=[hbm] * 15,
        out_specs=(out, out),
        scratch_shapes=[
            vmem(kv_pool.shape, BF16),
            vmem((width, HEADS * HD), BF16),
            vmem((NDP, width, hidden), BF16),
            vmem((NDP, width, hidden), BF16),
            vmem((NDP, width, hidden), BF16),
            vmem((NDP, width, columns), BF16),
            pltpu.SMEM((NDP,) + page_table.shape, jnp.int32),
            pltpu.SMEM((NDP, NDP, ROWS), jnp.int32),
            pltpu.SMEM((TOP, ROWS), jnp.int32),
            pltpu.SMEM((TOP, ROWS), F32),
            vmem((1, HEADS), F32),
            vmem((NDP * width,), F32),
            vmem((NDP * width,), F32),
            vmem((2, NDP, 1, width), F32),
            vmem((NDP, ROWS, HEADS * HD), BF16),
            vmem((ROWS * HEADS // 2, PAIR), F32),
            vmem((ROWS, NDP * width), BF16),
            vmem((NDP, ROWS, width), BF16),
            vmem((NDP, ROWS, width), BF16),
            vmem((ROWS, all_slots), F32),
            vmem((NDP, ROWS, all_slots), F32),
            vmem(pairs, F32),
            vmem((2, HEADS, PAIR), F32),
            vmem(pairs, BF16),
            vmem((2, HEADS, PAIR), F32),
            vmem(pairs, BF16),
            vmem((2, HEADS, PAIR), F32),
            vmem(pairs, BF16),
            vmem((HEADS, PAIR), F32),
            vmem(pairs, BF16),
            vmem((HEADS, PAIR), F32),
            vmem((2 * ROWS * HEADS // 2, PAIR), F32),
            vmem((2, 2 * ROWS, HEADS * HD), BF16),
            vmem((2, group_rows, width), BF16),
            vmem((NDP, 8, 128), F32),
            vmem((2, count, slots, width), BF16),
            vmem((2, 2, count, slots, width), BF16),
            vmem((all_slots // 2, hidden), F32),
            vmem((all_slots // 2, hidden), F32),
            vmem((2, 2, all_slots // 2, width), BF16),
            vmem((2, 2, all_slots // 2, width), BF16),
            vmem((2, all_slots // 2, width), F32),
            vmem((2, count, slots, width), BF16),
            vmem((2, count, slots, width), BF16),
            vmem((2, group_rows, width), BF16),
            vmem((2, group_rows, width), BF16),
            vmem((2, 2, group_rows, width), BF16),
            vmem((NDP, group_rows, width), F32),
            vmem((NDP, ROWS, columns), BF16),
            dma((15,)),
            dma((N_SEM,)),
            dma((N_SEM,)),
            dma((count,)),
            dma((count,)),
            dma((count,)),
            dma((count,)),
            dma((2, count)),
            dma((2, count)),
        ],
        compiler_params=pltpu.CompilerParams(collective_id=0, has_side_effects=True, vmem_limit_bytes=44 * 2**20),
        name="layer",
    )(*[pltpu.with_memory_space_constraint(x, pltpu.HBM) for x in (
        queries,
        kv_pool,
        page_table,
        held_tokens.T,
        sinks.reshape(1, HEADS),
        residual,
        route_ids.T,
        route_weights.T,
        moe_gain,
        w_gate.reshape(NDP, width, hidden),
        w_up.reshape(NDP, width, hidden),
        w_down[0].T.reshape(NDP, width, hidden),
        o_weight.T,
        attn_gain,
        qkv_weight.reshape(NDP, width, columns),
    )])


def body(*args):
    return layer_call(args, lax.axis_size("expert"))


def solution(mesh):
    in_specs = (
        P(("dp", "expert"), None),
        P(("dp", "expert"), None, None),
        P(("dp", "expert"), None, None),
        P(("dp", "expert"), None),
        P(),
        P(("dp", "expert"), None),
        P(("dp", "expert"), None),
        P(("dp", "expert"), None),
        P(),
        P("expert", None, "dp"),
        P("expert", None, "dp"),
        P("expert", "dp", None),
        P(None, "dp"),
        P(),
        P(None, "dp"),
    )
    out_specs = (P(("dp", "expert"), None), P(("dp", "expert"), None))
    return jax.shard_map(body, mesh=mesh, in_specs=in_specs, out_specs=out_specs, check_vma=False)
```

```python
import math

import jax
import jax.numpy as jnp
from jax import lax
from jax.experimental import pallas as pl
from jax.experimental.pallas import tpu as pltpu
from jax.sharding import PartitionSpec as P

HEADS = 64
KVH = 8
HD = 64
TOP = 4
PAGE = 16
PPH = 16
SPAN = PPH * PAGE
WIDE = KVH * HD
PAIR = 2 * HD
ROWS = 8
NDP = 4

EPSILON = 1e-05
LIMIT = 7.0
MESH = pl.DeviceIdType.MESH
F32 = jnp.float32
BF16 = jnp.bfloat16

S_TAB, S_HELD, S_Q, S_RES, S_COM, S_SUM, S_QKV = range(0, 21, 3)
S_PAIR_N, S_PAIR_ML, S_X_N, S_PART, S_NEXT = range(21, 31, 2)
S_X_ML, S_LHS, S_STREAM, S_OUT, N_SEM = 31, 32, 33, 34, 38
L_TAB, L_HELD, L_Q, L_POOL, L_SINK, L_IDS, L_WEIGHTS, L_RES, L_OW, L_MGAIN, L_GATE, L_UP, L_DOWN, L_AGAIN, L_QKV = range(15)


def position():
    dp = lax.axis_index("dp")
    expert = lax.axis_index("expert")
    return dp, lax.div(dp, 2), lax.rem(dp, 2), expert


def group_peer(z, c, offset):
    return lax.rem(z + offset // 2, 2) * 2 + lax.rem(c + offset % 2, 2)


def remote(src, dst, sems, sent, landed, device):
    return pltpu.make_async_remote_copy(
        src_ref=src,
        dst_ref=dst,
        send_sem=sems[0].at[sent],
        recv_sem=sems[1].at[landed],
        device_id=device,
        device_id_type=MESH,
    )


def spread_queries(wide):
    turned = pltpu.roll(wide, HD, 1)
    row = lax.broadcasted_iota(jnp.int32, (HEADS // 2, PAIR), 0)
    lane = lax.broadcasted_iota(jnp.int32, (HEADS // 2, PAIR), 1)
    odd_group = lax.rem(lax.div(row, 4), 2) == 1
    own_half = (lane >= HD) == odd_group
    even = jnp.where(own_half, jnp.where(odd_group, turned, wide), 0.0)
    odd = jnp.where(own_half, jnp.where(odd_group, wide, turned), 0.0)
    tile = lax.div(row, 8)
    parts = []
    for heads in (even, odd):
        parts.append(jnp.concatenate([jnp.where(tile == t, heads, 0.0) for t in range(4)], axis=1))
    return jnp.concatenate(parts, axis=0).astype(BF16)


def fold_values(wide):
    row = lax.broadcasted_iota(jnp.int32, (HEADS // 2, PAIR), 0)
    lane = lax.broadcasted_iota(jnp.int32, (HEADS // 2, PAIR), 1)
    odd_group = lax.rem(lax.div(row, 4), 2) == 1

    def own_tiles(base):
        return jnp.concatenate(
            [wide[base + 8 * t : base + 8 * t + 8, PAIR * t : PAIR * t + PAIR] for t in range(4)], axis=0
        )

    even, odd = own_tiles(0), own_tiles(HEADS // 2)
    even = jnp.where(odd_group, pltpu.roll(even, HD, 1), even)
    odd = jnp.where(odd_group, odd, pltpu.roll(odd, HD, 1))
    return jnp.where(lane < HD, even, odd)


def pair_columns(column):
    lane = lax.broadcasted_iota(jnp.int32, (HEADS // 2, PAIR), 1)
    return jnp.where(lane < HD, column[: HEADS // 2], column[HEADS // 2 :])


def attend(queries, tables, counts, holder, pool, rows, write):
    token = lax.broadcasted_iota(jnp.int32, (HEADS, SPAN), 1)
    scores, held = [], []
    for row in rows:
        keys = jnp.concatenate([pool[tables[row, holder, page], :, :WIDE] for page in range(PPH)], axis=0)
        start = pl.multiple_of(row * (HEADS // 2), HEADS // 2)
        spread = spread_queries(queries[pl.ds(start, HEADS // 2), :])
        scores.append(
            lax.dot_general(spread, keys, (((1,), (1,)), ((), ())), preferred_element_type=F32)
            * (1.0 / math.sqrt(HD))
        )
        held.append(token < counts[holder, row])
    weights, highs, sums = [], [], []
    for score, usable in zip(scores, held):
        high = jnp.max(jnp.where(usable, score, -1e30), axis=1, keepdims=True)
        weight = jnp.where(usable, jnp.exp(score - high), 0.0)
        highs.append(high)
        sums.append(jnp.sum(weight, axis=1, keepdims=True))
        weights.append(weight.astype(BF16))
    results = []
    for row, weight in zip(rows, weights):
        values = jnp.concatenate([pool[tables[row, holder, page], :, WIDE:] for page in range(PPH)], axis=0)
        results.append(fold_values(jnp.dot(weight, values, preferred_element_type=F32)))
    for row, result, high, total in zip(rows, results, highs, sums):
        write(row, result, high, total)


def sink_columns(sinks):
    row = lax.broadcasted_iota(jnp.int32, (HEADS, HEADS), 0)
    lane = lax.broadcasted_iota(jnp.int32, (HEADS, HEADS), 1)
    half = HEADS // 2
    head = jnp.where(row < half, 2 * row, 2 * (row - half) + 1)
    return jnp.sum(jnp.where(lane == head, sinks, 0.0), axis=1, keepdims=True)


def combine_rows(ids, weights, table, block, slots):
    capacity = slots // NDP
    lane = lax.broadcasted_iota(jnp.int32, (1, table.shape[1]), 1)
    of_expert, at_slot = lax.div(lane, slots), lax.rem(lane, slots)
    taken = jnp.zeros_like(lane)
    for row in range(ROWS):
        hit = jnp.zeros_like(lane)
        weight = jnp.zeros(lane.shape, F32)
        total = jnp.zeros(lane.shape, F32)
        for k in range(TOP):
            match = of_expert == ids[k, row]
            hit = jnp.where(match, 1, hit)
            weight = jnp.where(match, weights[k, row], weight)
            total = total + weights[k, row]
        at = (hit == 1) & (at_slot == block * capacity + taken)
        table[row : row + 1, :] = jnp.where(at, weight / total, 0.0)
        taken = taken + hit


STEP = 4


def layer_kernel(
    q_hbm, pool_hbm, tab_hbm, held_hbm, sink_hbm, res_hbm, ids_hbm, weights_hbm, mgain_hbm,
    wg_hbm, wu_hbm, wd_hbm, ow_hbm, again_hbm, wq_hbm,
    next_out, qkv_out,
    pool, ow, wg, wu, wd, wq,
    tabs, helds, ids, weights, sinks, mgain, again, gains, qraw, qwide, resraw, resblk, resall, comown, comall,
    keep_n, keep_ml, send_n, send_ml, recv_n, recv_ml, xs_n, xs_ml, xr_n, xr_ml, att, lhs, stream, sums,
    outbox, arr, gate, up, osend, orecv, kept, rbuf, ret, part_s, part_r, nextb, nextf, qbuf,
    load_sem, send_sem, recv_sem, d_send, d_recv, f_send, f_recv, r_send, r_recv, round_sem,
):
    dp, z, c, expert = position()
    sems = (send_sem, recv_sem)
    count, slots, width = arr.shape[2], arr.shape[3], arr.shape[4]
    block = c * 2 + z

    barrier = pltpu.get_barrier_semaphore()
    for offset in (1, 2, 3):
        pl.semaphore_signal(barrier, inc=1, device_id=(group_peer(z, c, offset), expert), device_id_type=MESH)

    def neighbour(digit):
        step = 1 << digit
        return (dp, expert + step * (1 - 2 * lax.rem(lax.div(expert, step), 2)))

    digits = count.bit_length() - 1
    for digit in range(digits):
        pl.semaphore_signal(barrier, inc=1, device_id=neighbour(digit), device_id_type=MESH)

    def know(digit):
        pl.semaphore_signal(round_sem.at[digit], inc=1, device_id=neighbour(digit), device_id_type=MESH)
        pl.semaphore_wait(round_sem.at[digit], 1)

    loads = {}
    for number, src, dst in (
        (L_TAB, tab_hbm, tabs.at[dp]),
        (L_HELD, held_hbm, helds.at[dp]),
        (L_Q, q_hbm, qraw.at[dp]),
        (L_POOL, pool_hbm, pool),
        (L_IDS, ids_hbm, ids),
        (L_WEIGHTS, weights_hbm, weights),
        (L_RES, res_hbm, resraw),
        (L_MGAIN, mgain_hbm, mgain),
        (L_AGAIN, again_hbm, again),
        (L_SINK, sink_hbm, sinks),
        (L_OW, ow_hbm, ow),
        (L_GATE, wg_hbm, wg),
        (L_UP, wu_hbm, wu),
        (L_DOWN, wd_hbm, wd),
        (L_QKV, wq_hbm, wq),
    ):
        loads[number] = pltpu.make_async_copy(src, dst, load_sem.at[number])
        loads[number].start()

    sent = []

    def send(src, dst, number, landed, offset):
        copy = remote(src, dst, sems, number, landed, (group_peer(z, c, offset), expert))
        copy.start()
        sent.append(copy)
        return copy

    lane = lax.broadcasted_iota(jnp.int32, (HEADS, PAIR), 1)

    def run_block(offset, number, numerators, stats):
        at = group_peer(z, c, offset)
        half = z if number == 0 else 1 - z
        stats[number] = jnp.zeros((HEADS, PAIR), F32)
        for pair in range(HEADS // 2):
            qwide[pl.ds(pair, ROWS, stride=HEADS // 2), :] = qraw[at, :, PAIR * pair : PAIR * pair + PAIR].astype(F32)

        def write(row, result, high, total):
            numerators[number, row] = result.astype(numerators.dtype)
            place = half * ROWS + row
            tile = jnp.where(lane == place, high, stats[number])
            stats[number] = jnp.where(lane == place + HD, total, tile)

        def step(index, carry):
            rows = [index * STEP + i for i in range(STEP)]
            attend(qwide, tabs.at[at], helds.at[at], dp, pool, rows, write)
            return carry

        lax.fori_loop(0, ROWS // STEP, step, 0)

    tab_in, held_in, q_in, res_in, com_in = {}, {}, {}, {}, {}

    def fetch_block(offset):
        tab_in[offset].wait_recv()
        held_in[offset].wait_recv()
        q_in[offset].wait_recv()

    def send_pair(number):
        return (
            send(send_n.at[number], recv_n.at[number], S_PAIR_N + number, S_PAIR_N + number, 1),
            send(send_ml.at[number], recv_ml.at[number], S_PAIR_ML + number, S_PAIR_ML + number, 1),
        )

    def factors(tile, number):
        half = z if number == 0 else 1 - z
        return pltpu.roll(tile, lax.rem(PAIR - half * ROWS, PAIR), 1)

    def merge_pair(number, incoming):
        for copy in incoming:
            copy.wait_recv()
        mine, other = keep_ml[number], recv_ml[number]
        high = jnp.maximum(mine, other)
        left, right = jnp.exp(mine - high), jnp.exp(other - high)
        total = mine * pltpu.roll(left, HD, 1) + other * pltpu.roll(right, HD, 1)
        keep_ml[number] = jnp.where(lane < HD, high, total)
        left, right = factors(left, number), factors(right, number)
        for row in range(ROWS):
            merged = keep_n[number, row] * pair_columns(left[:, row : row + 1]) + recv_n[number, row].astype(
                F32
            ) * pair_columns(right[:, row : row + 1])
            keep_n[number, row] = merged
            xs_n[number, row] = merged.astype(BF16)
        return send(xs_n.at[number], xr_n.at[1 - number], S_X_N + number, S_X_N + 1 - number, 2)

    pl.semaphore_wait(barrier, 3 + digits)
    for offset in (2, 1):
        q_in[offset] = send(q_hbm, qraw.at[dp], S_Q + offset - 1, S_Q + offset - 1, offset)
    for offset in (2, 3, 1):
        tab_in[offset] = send(tab_hbm, tabs.at[dp], S_TAB + offset - 1, S_TAB + offset - 1, offset)
        held_in[offset] = send(held_hbm, helds.at[dp], S_HELD + offset - 1, S_HELD + offset - 1, offset)
    for number in (L_TAB, L_HELD, L_Q, L_POOL):
        loads[number].wait()
    run_block(0, 0, keep_n, keep_ml)
    know(0)
    fetch_block(1)
    run_block(1, 0, send_n, send_ml)
    pair_in = [send_pair(0)]
    know(1)
    for number in (L_IDS, L_WEIGHTS, L_RES, L_MGAIN, L_AGAIN):
        loads[number].wait()
    combine_rows(ids, weights, comown, block, slots)
    comall[block] = comown[...]
    for which, gain in enumerate((mgain, again)):
        whole = gain[...].reshape(1, NDP * width)
        for k in range(NDP):
            gains[which, k] = whole[:, width * k : width * k + width]
    for k in range(NDP):
        resblk[k] = resraw[:, width * k : width * k + width]
    resall[block] = resblk[dp]
    fetch_block(2)
    cross = group_peer(z, c, 2)
    q_in[3] = send(qraw.at[cross], qraw.at[cross], S_Q + 2, S_Q + 2, 1)
    for offset in (2, 3, 1):
        peer = group_peer(z, c, offset)
        res_in[offset] = send(resblk.at[peer], resall.at[block], S_RES + offset - 1, S_RES + offset - 1, offset)
        com_in[offset] = send(comown, comall.at[block], S_COM + offset - 1, S_COM + offset - 1, offset)
    cross_in = [merge_pair(0, pair_in[0])]
    know(2)
    fetch_block(3)
    run_block(3, 1, send_n, send_ml)
    pair_in.append(send_pair(1))
    know(3)
    run_block(2, 1, keep_n, keep_ml)
    cross_in.append(merge_pair(1, pair_in[1]))
    xs_ml[...] = keep_ml[0] + keep_ml[1]
    cross_ml = send(xs_ml, xr_ml, S_X_ML, S_X_ML, 2)

    cross_ml.wait_recv()
    loads[L_SINK].wait()
    mine, other, sink = xs_ml[...], xr_ml[...], sink_columns(sinks[...])
    top = jnp.maximum(jnp.maximum(mine, other), sink)
    left, right = jnp.exp(mine - top), jnp.exp(other - top)
    total = mine * pltpu.roll(left, HD, 1) + other * pltpu.roll(right, HD, 1)
    below = pltpu.roll(total, HD, 1) + jnp.exp(sink - top)
    left, right = left / below, right / below
    for number in (0, 1):
        cross_in[1 - number].wait_recv()
        one, two = factors(left, number), factors(right, number)
        half = z if number == 0 else 1 - z
        for row in range(ROWS):
            attention = keep_n[number, row] * pair_columns(one[:, row : row + 1]) + xr_n[number, row].astype(
                F32
            ) * pair_columns(two[:, row : row + 1])
            start = pl.multiple_of((half * ROWS + row) * (HEADS // 2), HEADS // 2)
            att[pl.ds(start, HEADS // 2), :] = attention
    for pair in range(HEADS // 2):
        lhs[c, :, PAIR * pair : PAIR * pair + PAIR] = att[pl.ds(pair, 2 * ROWS, stride=HEADS // 2), :].astype(BF16)
    lhs_in = send(lhs.at[c], lhs.at[c], S_LHS, S_LHS, 1)
    for digit in range(4, digits):
        know(digit)
    for offset in (1, 2, 3):
        res_in[offset].wait_recv()
        com_in[offset].wait_recv()
    residual = jnp.concatenate([resall[d].astype(F32) for d in range(NDP)], axis=0)
    share = jnp.concatenate([comall[d] for d in range(NDP)], axis=0)
    picks = (share > 0).astype(F32).T.astype(BF16)
    loads[L_OW].wait()
    lhs_in.wait_recv()
    rows = jnp.concatenate([lhs[0], lhs[1]], axis=0)
    projected = lax.dot_general(rows, ow[...], (((1,), (1,)), ((), ())), preferred_element_type=F32)
    stream[z] = (residual + projected.astype(BF16).astype(F32)).astype(BF16)
    stream_in = send(stream.at[z], stream.at[z], S_STREAM, S_STREAM, 2)
    own = stream[z].astype(F32)
    group_rows = own.shape[0]
    diagonal = lax.broadcasted_iota(jnp.int32, (group_rows, 128), 0) == lax.broadcasted_iota(
        jnp.int32, (group_rows, 128), 1
    )
    square = jnp.sum(own * own, axis=1, keepdims=True)
    sums[dp] = jnp.broadcast_to(
        jnp.sum(jnp.where(diagonal, square, 0.0), axis=0, keepdims=True), sums.shape[1:]
    )
    sum_in = [
        send(sums.at[dp], sums.at[dp], S_SUM + offset - 1, S_SUM + offset - 1, offset) for offset in (2, 3, 1)
    ]
    for copy in sum_in:
        copy.wait_recv()
    square = (sums[0] + sums[1] + sums[2] + sums[3])[:1]
    square = jnp.sum(jnp.where(diagonal, square, 0.0), axis=1, keepdims=True)
    scale = lax.rsqrt(square / (NDP * width) + EPSILON)
    stream_in.wait_recv()
    for j in range(2):
        rows = (stream[j].astype(F32) * scale * gains[0, 2 * j + c]).astype(BF16)
        picked = jnp.dot(picks, rows, preferred_element_type=F32).astype(BF16)
        outbox[j] = picked.reshape(count, slots, width)

    def partner(place, sign):
        dy = 2 * lax.rem(lax.div(place, 8), 2) + lax.div(place, 16)
        dz, dx = lax.rem(lax.div(place, 4), 2), lax.rem(place, 4)
        at_z = lax.rem(lax.div(expert, 16) + dz, 2)
        at_y = lax.rem(lax.rem(lax.div(expert, 4), 4) + sign * dy + 4, 4)
        at_x = lax.rem(lax.rem(expert, 4) + sign * dx + 4, 4)
        return 16 * at_z + 4 * at_y + at_x

    def dispatch(place):
        to = partner(place, 1)
        return remote(outbox.at[:, to], arr.at[c, :, place], (d_send, d_recv), place, place, (dp, to))

    def forward(place):
        return remote(
            arr.at[c, :, place], arr.at[c, :, place], (f_send, f_recv), place, place,
            (group_peer(z, c, 1), expert),
        )

    def giveback(j, place):
        to = partner(place, -1)
        return remote(
            rbuf.at[j, place], ret.at[j, expert], (r_send.at[j], r_recv.at[j]), place, place, (dp, to)
        )

    def each(first, last, act):
        def step(place, carry):
            act(place)
            return carry

        lax.fori_loop(first, last, step, 0)

    batch = count // 2
    batch_rows = batch * slots

    def pass_on(place):
        dispatch(place).wait_recv()
        forward(place).start()

    def project(first_place, half, first):
        for j in range(2):
            rows = arr[half, j, first_place : first_place + batch].reshape(batch_rows, width)
            for total, weight in ((gate, wg), (up, wu)):
                value = jnp.dot(rows, weight[2 * j + half], preferred_element_type=F32)
                if first and j == 0:
                    total[...] = value
                else:
                    total[...] += value

    def apply_experts(number):
        first_place = number * batch
        project(first_place, c, True)
        each(first_place, first_place + batch, lambda place: forward(place).wait_recv())
        project(first_place, 1 - c, False)
        gated = jnp.minimum(gate[...], LIMIT)
        lifted = jnp.clip(up[...], -LIMIT, LIMIT)
        activated = (gated * jax.nn.sigmoid(1.702 * gated) * (lifted + 1.0)).astype(BF16)

        def down(k):
            return lax.dot_general(activated, wd[k], (((1,), (1,)), ((), ())), preferred_element_type=F32)

        incoming = []
        for j in range(2):
            osend[number, j] = down(2 * j + 1 - c).astype(BF16)
            at = S_OUT + 2 * number + j
            incoming.append(send(osend.at[number, j], orecv.at[number, j], at, at, 1))
        for j in range(2):
            kept[j] = down(2 * j + c)
        return incoming

    def give_back(number, incoming):
        first_place = number * batch
        for j in range(2):
            incoming[j].wait_recv()
            total = (kept[j] + orecv[number, j].astype(F32)).astype(BF16)
            rbuf[j, first_place : first_place + batch] = total.reshape(batch, slots, width)
            each(max(first_place, 1), first_place + batch, lambda place: giveback(j, place).start())

    each(1, count, lambda place: dispatch(place).start())
    for j in range(2):
        arr[c, j, 0] = outbox[j, expert]
    forward(0).start()
    each(1, batch, pass_on)
    for number in (L_GATE, L_UP, L_DOWN):
        loads[number].wait()
    incoming = apply_experts(0)
    each(batch, count, pass_on)
    give_back(0, incoming)
    incoming = apply_experts(1)
    give_back(1, incoming)
    for j in range(2):
        ret[j, expert] = rbuf[j, 0]

    high = share.astype(BF16)
    low = (share - high.astype(F32)).astype(BF16)
    both = jnp.concatenate([high, low], axis=0)
    part_in = []
    for j in range(2):
        each(1, count, lambda place: giveback(j, place).wait_recv())
        mixed = jnp.dot(both, ret[j].reshape(count * slots, width), preferred_element_type=F32)
        part_s[j] = (mixed[:group_rows] + mixed[group_rows:]).astype(BF16)
        part_in.append(send(part_s.at[j], part_r.at[j], S_PART + j, S_PART + j, 2))
    loads[L_QKV].wait()
    next_in = []
    qkv = jnp.zeros((group_rows, wq.shape[2]), F32)
    squares = jnp.zeros((group_rows, 1), F32)

    def project_next(half, j, qkv, squares):
        k = 2 * j + half
        rows = nextb[half, j].astype(F32)
        nextf[k] = rows
        squares += jnp.sum(rows * rows, axis=1, keepdims=True)
        qkv += jnp.dot((rows * gains[1, k]).astype(BF16), wq[k], preferred_element_type=F32)
        return qkv, squares

    for j in range(2):
        part_in[j].wait_recv()
        moe_out = part_s[j].astype(F32) + part_r[j].astype(F32)
        nextb[c, j] = (stream[j].astype(F32) + moe_out).astype(BF16)
        next_in.append(send(nextb.at[c, j], nextb.at[c, j], S_NEXT + j, S_NEXT + j, 1))
        qkv, squares = project_next(c, j, qkv, squares)
    for j in range(2):
        next_in[j].wait_recv()
        qkv, squares = project_next(1 - c, j, qkv, squares)
    qkv = qkv * lax.rsqrt(squares / (NDP * width) + EPSILON)
    columns = qkv.shape[1]
    for d in range(NDP):
        qbuf[d] = qkv[ROWS * d : ROWS * d + ROWS].astype(BF16)
    own_columns = pl.ds(pl.multiple_of(dp * columns, 128), columns)
    qkv_in = []
    for offset in (2, 3, 1):
        peer = group_peer(z, c, offset)
        theirs = lax.rem(peer, 2) * 2 + lax.div(peer, 2)
        qkv_in.append(
            send(qbuf.at[theirs], qkv_out.at[:, own_columns], S_QKV + offset - 1, S_QKV + offset - 1, offset)
        )
    qkv_out[:, own_columns] = qbuf[block]
    start = pl.multiple_of(block * ROWS, ROWS)
    for k in range(NDP):
        next_out[:, width * k : width * k + width] = nextf[k, pl.ds(start, ROWS), :].astype(BF16)

    def all_sent(place):
        dispatch(place).wait_send()
        for j in range(2):
            giveback(j, place).wait_send()

    each(1, count, all_sent)
    each(0, count, lambda place: forward(place).wait_send())
    for copy in sent:
        copy.wait_send()
    for copy in qkv_in:
        copy.wait_recv()


def layer_call(args, count):
    (queries, kv_pool, page_table, held_tokens, sinks, residual, route_ids, route_weights, moe_gain,
     w_gate, w_up, w_down, o_weight, attn_gain, qkv_weight) = args
    width = residual.shape[1] // NDP
    hidden = w_gate.shape[2]
    columns = qkv_weight.shape[1]
    slots = NDP * (2 * ROWS * TOP // count)
    group_rows = NDP * ROWS
    all_slots = count * slots
    hbm = pl.BlockSpec(memory_space=pltpu.HBM)
    out = pl.BlockSpec(memory_space=pltpu.VMEM)
    vmem, dma = pltpu.VMEM, pltpu.SemaphoreType.DMA
    pairs = (2, ROWS, HEADS // 2, PAIR)
    return pl.pallas_call(
        layer_kernel,
        out_shape=(
            jax.ShapeDtypeStruct((ROWS, NDP * width), BF16),
            jax.ShapeDtypeStruct((ROWS, NDP * columns), BF16),
        ),
        in_specs=[hbm] * 15,
        out_specs=(out, out),
        scratch_shapes=[
            vmem(kv_pool.shape, BF16),
            vmem((width, HEADS * HD), BF16),
            vmem((NDP, width, hidden), BF16),
            vmem((NDP, width, hidden), BF16),
            vmem((NDP, width, hidden), BF16),
            vmem((NDP, width, columns), BF16),
            pltpu.SMEM((NDP,) + page_table.shape, jnp.int32),
            pltpu.SMEM((NDP, NDP, ROWS), jnp.int32),
            pltpu.SMEM((TOP, ROWS), jnp.int32),
            pltpu.SMEM((TOP, ROWS), F32),
            vmem((1, HEADS), F32),
            vmem((NDP * width,), F32),
            vmem((NDP * width,), F32),
            vmem((2, NDP, 1, width), F32),
            vmem((NDP, ROWS, HEADS * HD), BF16),
            vmem((ROWS * HEADS // 2, PAIR), F32),
            vmem((ROWS, NDP * width), BF16),
            vmem((NDP, ROWS, width), BF16),
            vmem((NDP, ROWS, width), BF16),
            vmem((ROWS, all_slots), F32),
            vmem((NDP, ROWS, all_slots), F32),
            vmem(pairs, F32),
            vmem((2, HEADS, PAIR), F32),
            vmem(pairs, BF16),
            vmem((2, HEADS, PAIR), F32),
            vmem(pairs, BF16),
            vmem((2, HEADS, PAIR), F32),
            vmem(pairs, BF16),
            vmem((HEADS, PAIR), F32),
            vmem(pairs, BF16),
            vmem((HEADS, PAIR), F32),
            vmem((2 * ROWS * HEADS // 2, PAIR), F32),
            vmem((2, 2 * ROWS, HEADS * HD), BF16),
            vmem((2, group_rows, width), BF16),
            vmem((NDP, 8, 128), F32),
            vmem((2, count, slots, width), BF16),
            vmem((2, 2, count, slots, width), BF16),
            vmem((all_slots // 2, hidden), F32),
            vmem((all_slots // 2, hidden), F32),
            vmem((2, 2, all_slots // 2, width), BF16),
            vmem((2, 2, all_slots // 2, width), BF16),
            vmem((2, all_slots // 2, width), F32),
            vmem((2, count, slots, width), BF16),
            vmem((2, count, slots, width), BF16),
            vmem((2, group_rows, width), BF16),
            vmem((2, group_rows, width), BF16),
            vmem((2, 2, group_rows, width), BF16),
            vmem((NDP, group_rows, width), F32),
            vmem((NDP, ROWS, columns), BF16),
            dma((15,)),
            dma((N_SEM,)),
            dma((N_SEM,)),
            dma((count,)),
            dma((count,)),
            dma((count,)),
            dma((count,)),
            dma((2, count)),
            dma((2, count)),
            pltpu.SemaphoreType.REGULAR((count.bit_length() - 1,)),
        ],
        compiler_params=pltpu.CompilerParams(collective_id=0, has_side_effects=True, vmem_limit_bytes=44 * 2**20),
        name="layer",
    )(*[pltpu.with_memory_space_constraint(x, pltpu.HBM) for x in (
        queries,
        kv_pool,
        page_table,
        held_tokens.T,
        sinks.reshape(1, HEADS),
        residual,
        route_ids.T,
        route_weights.T,
        moe_gain,
        w_gate.reshape(NDP, width, hidden),
        w_up.reshape(NDP, width, hidden),
        w_down[0].T.reshape(NDP, width, hidden),
        o_weight.T,
        attn_gain,
        qkv_weight.reshape(NDP, width, columns),
    )])


def body(*args):
    return layer_call(args, lax.axis_size("expert"))


def solution(mesh):
    in_specs = (
        P(("dp", "expert"), None),
        P(("dp", "expert"), None, None),
        P(("dp", "expert"), None, None),
        P(("dp", "expert"), None),
        P(),
        P(("dp", "expert"), None),
        P(("dp", "expert"), None),
        P(("dp", "expert"), None),
        P(),
        P("expert", None, "dp"),
        P("expert", None, "dp"),
        P("expert", "dp", None),
        P(None, "dp"),
        P(),
        P(None, "dp"),
    )
    out_specs = (P(("dp", "expert"), None), P(("dp", "expert"), None))
    return jax.shard_map(body, mesh=mesh, in_specs=in_specs, out_specs=out_specs, check_vma=False)
```

```python
import math

import jax
import jax.numpy as jnp
from jax import lax
from jax.experimental import pallas as pl
from jax.experimental.pallas import tpu as pltpu
from jax.sharding import PartitionSpec as P

HEADS = 64
KVH = 8
HD = 64
TOP = 4
PAGE = 16
PPH = 16
SPAN = PPH * PAGE
WIDE = KVH * HD
PAIR = 2 * HD
ROWS = 8
NDP = 4

EPSILON = 1e-05
LIMIT = 7.0
MESH = pl.DeviceIdType.MESH
F32 = jnp.float32
BF16 = jnp.bfloat16

S_TAB, S_HELD, S_Q, S_RES, S_COM, S_SUM, S_QKV = range(0, 21, 3)
S_PAIR_N, S_PAIR_ML, S_X_N, S_PART, S_NEXT = range(21, 31, 2)
S_X_ML, S_LHS, S_STREAM, S_OUT, N_SEM = 31, 32, 33, 34, 38
L_TAB, L_HELD, L_Q, L_POOL, L_SINK, L_IDS, L_WEIGHTS, L_RES, L_OW, L_MGAIN, L_GATE, L_UP, L_DOWN, L_AGAIN, L_QKV = range(15)


def position():
    dp = lax.axis_index("dp")
    expert = lax.axis_index("expert")
    return dp, lax.div(dp, 2), lax.rem(dp, 2), expert


def group_peer(z, c, offset):
    return lax.rem(z + offset // 2, 2) * 2 + lax.rem(c + offset % 2, 2)


def remote(src, dst, sems, sent, landed, device):
    return pltpu.make_async_remote_copy(
        src_ref=src,
        dst_ref=dst,
        send_sem=sems[0].at[sent],
        recv_sem=sems[1].at[landed],
        device_id=device,
        device_id_type=MESH,
    )


def spread_queries(wide):
    turned = pltpu.roll(wide, HD, 1)
    row = lax.broadcasted_iota(jnp.int32, (HEADS // 2, PAIR), 0)
    lane = lax.broadcasted_iota(jnp.int32, (HEADS // 2, PAIR), 1)
    odd_group = lax.rem(lax.div(row, 4), 2) == 1
    own_half = (lane >= HD) == odd_group
    even = jnp.where(own_half, jnp.where(odd_group, turned, wide), 0.0)
    odd = jnp.where(own_half, jnp.where(odd_group, wide, turned), 0.0)
    tile = lax.div(row, 8)
    parts = []
    for heads in (even, odd):
        parts.append(jnp.concatenate([jnp.where(tile == t, heads, 0.0) for t in range(4)], axis=1))
    return jnp.concatenate(parts, axis=0).astype(BF16)


def fold_values(wide):
    row = lax.broadcasted_iota(jnp.int32, (HEADS // 2, PAIR), 0)
    lane = lax.broadcasted_iota(jnp.int32, (HEADS // 2, PAIR), 1)
    odd_group = lax.rem(lax.div(row, 4), 2) == 1

    def own_tiles(base):
        return jnp.concatenate(
            [wide[base + 8 * t : base + 8 * t + 8, PAIR * t : PAIR * t + PAIR] for t in range(4)], axis=0
        )

    even, odd = own_tiles(0), own_tiles(HEADS // 2)
    even = jnp.where(odd_group, pltpu.roll(even, HD, 1), even)
    odd = jnp.where(odd_group, odd, pltpu.roll(odd, HD, 1))
    return jnp.where(lane < HD, even, odd)


def pair_columns(column):
    lane = lax.broadcasted_iota(jnp.int32, (HEADS // 2, PAIR), 1)
    return jnp.where(lane < HD, column[: HEADS // 2], column[HEADS // 2 :])


def attend(queries, tables, counts, holder, pool, rows, write):
    token = lax.broadcasted_iota(jnp.int32, (HEADS, SPAN), 1)
    scores, held = [], []
    for row in rows:
        keys = jnp.concatenate([pool[tables[row, holder, page], :, :WIDE] for page in range(PPH)], axis=0)
        start = pl.multiple_of(row * (HEADS // 2), HEADS // 2)
        spread = spread_queries(queries[pl.ds(start, HEADS // 2), :])
        scores.append(
            lax.dot_general(spread, keys, (((1,), (1,)), ((), ())), preferred_element_type=F32)
            * (1.0 / math.sqrt(HD))
        )
        held.append(token < counts[holder, row])
    weights, highs, sums = [], [], []
    for score, usable in zip(scores, held):
        high = jnp.max(jnp.where(usable, score, -1e30), axis=1, keepdims=True)
        weight = jnp.where(usable, jnp.exp(score - high), 0.0)
        highs.append(high)
        sums.append(jnp.sum(weight, axis=1, keepdims=True))
        weights.append(weight.astype(BF16))
    results = []
    for row, weight in zip(rows, weights):
        values = jnp.concatenate([pool[tables[row, holder, page], :, WIDE:] for page in range(PPH)], axis=0)
        results.append(fold_values(jnp.dot(weight, values, preferred_element_type=F32)))
    for row, result, high, total in zip(rows, results, highs, sums):
        write(row, result, high, total)


def sink_columns(sinks):
    row = lax.broadcasted_iota(jnp.int32, (HEADS, HEADS), 0)
    lane = lax.broadcasted_iota(jnp.int32, (HEADS, HEADS), 1)
    half = HEADS // 2
    head = jnp.where(row < half, 2 * row, 2 * (row - half) + 1)
    return jnp.sum(jnp.where(lane == head, sinks, 0.0), axis=1, keepdims=True)


def combine_rows(ids, weights, table, block, slots):
    capacity = slots // NDP
    lane = lax.broadcasted_iota(jnp.int32, (1, table.shape[1]), 1)
    of_expert, at_slot = lax.div(lane, slots), lax.rem(lane, slots)
    taken = jnp.zeros_like(lane)
    for row in range(ROWS):
        hit = jnp.zeros_like(lane)
        weight = jnp.zeros(lane.shape, F32)
        total = jnp.zeros(lane.shape, F32)
        for k in range(TOP):
            match = of_expert == ids[k, row]
            hit = jnp.where(match, 1, hit)
            weight = jnp.where(match, weights[k, row], weight)
            total = total + weights[k, row]
        at = (hit == 1) & (at_slot == block * capacity + taken)
        table[row : row + 1, :] = jnp.where(at, weight / total, 0.0)
        taken = taken + hit


STEP = 8


def layer_kernel(
    q_hbm, pool_hbm, tab_hbm, held_hbm, sink_hbm, res_hbm, ids_hbm, weights_hbm, mgain_hbm,
    wg_hbm, wu_hbm, wd_hbm, ow_hbm, again_hbm, wq_hbm,
    next_out, qkv_out,
    pool, ow, wg, wu, wd, wq,
    tabs, helds, ids, weights, sinks, mgain, again, gains, qraw, qwide, resraw, resblk, resall, comown, comall,
    keep_n, keep_ml, send_n, send_ml, recv_n, recv_ml, xs_n, xs_ml, xr_n, xr_ml, att, lhs, stream, sums,
    outbox, arr, gate, up, osend, orecv, kept, rbuf, ret, part_s, part_r, nextb, nextf, qbuf,
    load_sem, send_sem, recv_sem, d_send, d_recv, f_send, f_recv, r_send, r_recv, round_sem,
):
    dp, z, c, expert = position()
    sems = (send_sem, recv_sem)
    count, slots, width = arr.shape[2], arr.shape[3], arr.shape[4]
    block = c * 2 + z

    barrier = pltpu.get_barrier_semaphore()
    for offset in (1, 2, 3):
        pl.semaphore_signal(barrier, inc=1, device_id=(group_peer(z, c, offset), expert), device_id_type=MESH)

    def neighbour(digit):
        step = 1 << digit
        return (dp, expert + step * (1 - 2 * lax.rem(lax.div(expert, step), 2)))

    digits = count.bit_length() - 1
    for digit in range(digits):
        pl.semaphore_signal(barrier, inc=1, device_id=neighbour(digit), device_id_type=MESH)

    def know(digit):
        if digit > 0:
            pl.semaphore_wait(round_sem.at[digit - 1], 1)
        if digit < digits:
            pl.semaphore_signal(round_sem.at[digit], inc=1, device_id=neighbour(digit), device_id_type=MESH)

    loads = {}
    for number, src, dst in (
        (L_TAB, tab_hbm, tabs.at[dp]),
        (L_HELD, held_hbm, helds.at[dp]),
        (L_Q, q_hbm, qraw.at[dp]),
        (L_POOL, pool_hbm, pool),
        (L_IDS, ids_hbm, ids),
        (L_WEIGHTS, weights_hbm, weights),
        (L_RES, res_hbm, resraw),
        (L_MGAIN, mgain_hbm, mgain),
        (L_AGAIN, again_hbm, again),
        (L_SINK, sink_hbm, sinks),
        (L_OW, ow_hbm, ow),
        (L_GATE, wg_hbm, wg),
        (L_UP, wu_hbm, wu),
        (L_DOWN, wd_hbm, wd),
        (L_QKV, wq_hbm, wq),
    ):
        loads[number] = pltpu.make_async_copy(src, dst, load_sem.at[number])
        loads[number].start()

    sent = []

    def send(src, dst, number, landed, offset):
        copy = remote(src, dst, sems, number, landed, (group_peer(z, c, offset), expert))
        copy.start()
        sent.append(copy)
        return copy

    lane = lax.broadcasted_iota(jnp.int32, (HEADS, PAIR), 1)

    def run_block(offset, number, numerators, stats):
        at = group_peer(z, c, offset)
        half = z if number == 0 else 1 - z
        stats[number] = jnp.zeros((HEADS, PAIR), F32)
        for pair in range(HEADS // 2):
            qwide[pl.ds(pair, ROWS, stride=HEADS // 2), :] = qraw[at, :, PAIR * pair : PAIR * pair + PAIR].astype(F32)

        def write(row, result, high, total):
            numerators[number, row] = result.astype(numerators.dtype)
            place = half * ROWS + row
            tile = jnp.where(lane == place, high, stats[number])
            stats[number] = jnp.where(lane == place + HD, total, tile)

        def step(index, carry):
            rows = [index * STEP + i for i in range(STEP)]
            attend(qwide, tabs.at[at], helds.at[at], dp, pool, rows, write)
            return carry

        lax.fori_loop(0, ROWS // STEP, step, 0)

    tab_in, held_in, q_in, res_in, com_in = {}, {}, {}, {}, {}

    def fetch_block(offset):
        tab_in[offset].wait_recv()
        held_in[offset].wait_recv()
        q_in[offset].wait_recv()

    def send_pair(number):
        return (
            send(send_n.at[number], recv_n.at[number], S_PAIR_N + number, S_PAIR_N + number, 1),
            send(send_ml.at[number], recv_ml.at[number], S_PAIR_ML + number, S_PAIR_ML + number, 1),
        )

    def factors(tile, number):
        half = z if number == 0 else 1 - z
        return pltpu.roll(tile, lax.rem(PAIR - half * ROWS, PAIR), 1)

    def merge_pair(number, incoming):
        for copy in incoming:
            copy.wait_recv()
        mine, other = keep_ml[number], recv_ml[number]
        high = jnp.maximum(mine, other)
        left, right = jnp.exp(mine - high), jnp.exp(other - high)
        total = mine * pltpu.roll(left, HD, 1) + other * pltpu.roll(right, HD, 1)
        keep_ml[number] = jnp.where(lane < HD, high, total)
        left, right = factors(left, number), factors(right, number)
        for row in range(ROWS):
            merged = keep_n[number, row] * pair_columns(left[:, row : row + 1]) + recv_n[number, row].astype(
                F32
            ) * pair_columns(right[:, row : row + 1])
            keep_n[number, row] = merged
            xs_n[number, row] = merged.astype(BF16)
        return send(xs_n.at[number], xr_n.at[1 - number], S_X_N + number, S_X_N + 1 - number, 2)

    pl.semaphore_wait(barrier, 3 + digits)
    know(0)
    for offset in (2, 1):
        q_in[offset] = send(q_hbm, qraw.at[dp], S_Q + offset - 1, S_Q + offset - 1, offset)
    for offset in (2, 3, 1):
        tab_in[offset] = send(tab_hbm, tabs.at[dp], S_TAB + offset - 1, S_TAB + offset - 1, offset)
        held_in[offset] = send(held_hbm, helds.at[dp], S_HELD + offset - 1, S_HELD + offset - 1, offset)
    for number in (L_IDS, L_WEIGHTS, L_RES, L_MGAIN, L_AGAIN):
        loads[number].wait()
    combine_rows(ids, weights, comown, block, slots)
    comall[block] = comown[...]
    for which, gain in enumerate((mgain, again)):
        whole = gain[...].reshape(1, NDP * width)
        for k in range(NDP):
            gains[which, k] = whole[:, width * k : width * k + width]
    for k in range(NDP):
        resblk[k] = resraw[:, width * k : width * k + width]
    resall[block] = resblk[dp]
    for number in (L_TAB, L_HELD, L_Q, L_POOL):
        loads[number].wait()
    run_block(0, 0, keep_n, keep_ml)
    fetch_block(1)
    run_block(1, 0, send_n, send_ml)
    pair_in = [send_pair(0)]
    know(1)
    fetch_block(2)
    cross = group_peer(z, c, 2)
    q_in[3] = send(qraw.at[cross], qraw.at[cross], S_Q + 2, S_Q + 2, 1)
    for offset in (2, 3, 1):
        peer = group_peer(z, c, offset)
        res_in[offset] = send(resblk.at[peer], resall.at[block], S_RES + offset - 1, S_RES + offset - 1, offset)
        com_in[offset] = send(comown, comall.at[block], S_COM + offset - 1, S_COM + offset - 1, offset)
    cross_in = [merge_pair(0, pair_in[0])]
    know(2)
    fetch_block(3)
    run_block(3, 1, send_n, send_ml)
    pair_in.append(send_pair(1))
    know(3)
    run_block(2, 1, keep_n, keep_ml)
    cross_in.append(merge_pair(1, pair_in[1]))
    xs_ml[...] = keep_ml[0] + keep_ml[1]
    cross_ml = send(xs_ml, xr_ml, S_X_ML, S_X_ML, 2)

    cross_ml.wait_recv()
    loads[L_SINK].wait()
    mine, other, sink = xs_ml[...], xr_ml[...], sink_columns(sinks[...])
    top = jnp.maximum(jnp.maximum(mine, other), sink)
    left, right = jnp.exp(mine - top), jnp.exp(other - top)
    total = mine * pltpu.roll(left, HD, 1) + other * pltpu.roll(right, HD, 1)
    below = pltpu.roll(total, HD, 1) + jnp.exp(sink - top)
    left, right = left / below, right / below
    for number in (0, 1):
        cross_in[1 - number].wait_recv()
        one, two = factors(left, number), factors(right, number)
        half = z if number == 0 else 1 - z
        for row in range(ROWS):
            attention = keep_n[number, row] * pair_columns(one[:, row : row + 1]) + xr_n[number, row].astype(
                F32
            ) * pair_columns(two[:, row : row + 1])
            start = pl.multiple_of((half * ROWS + row) * (HEADS // 2), HEADS // 2)
            att[pl.ds(start, HEADS // 2), :] = attention
    for pair in range(HEADS // 2):
        lhs[c, :, PAIR * pair : PAIR * pair + PAIR] = att[pl.ds(pair, 2 * ROWS, stride=HEADS // 2), :].astype(BF16)
    lhs_in = send(lhs.at[c], lhs.at[c], S_LHS, S_LHS, 1)
    for digit in range(4, digits):
        know(digit)
    for offset in (1, 2, 3):
        res_in[offset].wait_recv()
        com_in[offset].wait_recv()
    residual = jnp.concatenate([resall[d].astype(F32) for d in range(NDP)], axis=0)
    share = jnp.concatenate([comall[d] for d in range(NDP)], axis=0)
    picks = (share > 0).astype(F32).T.astype(BF16)
    loads[L_OW].wait()
    lhs_in.wait_recv()
    rows = jnp.concatenate([lhs[0], lhs[1]], axis=0)
    projected = lax.dot_general(rows, ow[...], (((1,), (1,)), ((), ())), preferred_element_type=F32)
    stream[z] = (residual + projected.astype(BF16).astype(F32)).astype(BF16)
    stream_in = send(stream.at[z], stream.at[z], S_STREAM, S_STREAM, 2)
    own = stream[z].astype(F32)
    group_rows = own.shape[0]
    diagonal = lax.broadcasted_iota(jnp.int32, (group_rows, 128), 0) == lax.broadcasted_iota(
        jnp.int32, (group_rows, 128), 1
    )
    square = jnp.sum(own * own, axis=1, keepdims=True)
    sums[dp] = jnp.broadcast_to(
        jnp.sum(jnp.where(diagonal, square, 0.0), axis=0, keepdims=True), sums.shape[1:]
    )
    sum_in = [
        send(sums.at[dp], sums.at[dp], S_SUM + offset - 1, S_SUM + offset - 1, offset) for offset in (2, 3, 1)
    ]
    for copy in sum_in:
        copy.wait_recv()
    square = (sums[0] + sums[1] + sums[2] + sums[3])[:1]
    square = jnp.sum(jnp.where(diagonal, square, 0.0), axis=1, keepdims=True)
    scale = lax.rsqrt(square / (NDP * width) + EPSILON)
    stream_in.wait_recv()
    for j in range(2):
        rows = (stream[j].astype(F32) * scale * gains[0, 2 * j + c]).astype(BF16)
        picked = jnp.dot(picks, rows, preferred_element_type=F32).astype(BF16)
        outbox[j] = picked.reshape(count, slots, width)

    def partner(place, sign):
        dy = 2 * lax.rem(lax.div(place, 8), 2) + lax.div(place, 16)
        dz, dx = lax.rem(lax.div(place, 4), 2), lax.rem(place, 4)
        at_z = lax.rem(lax.div(expert, 16) + dz, 2)
        at_y = lax.rem(lax.rem(lax.div(expert, 4), 4) + sign * dy + 4, 4)
        at_x = lax.rem(lax.rem(expert, 4) + sign * dx + 4, 4)
        return 16 * at_z + 4 * at_y + at_x

    def dispatch(place):
        to = partner(place, 1)
        return remote(outbox.at[:, to], arr.at[c, :, place], (d_send, d_recv), place, place, (dp, to))

    def forward(place):
        return remote(
            arr.at[c, :, place], arr.at[c, :, place], (f_send, f_recv), place, place,
            (group_peer(z, c, 1), expert),
        )

    def giveback(j, place):
        to = partner(place, -1)
        return remote(
            rbuf.at[j, place], ret.at[j, expert], (r_send.at[j], r_recv.at[j]), place, place, (dp, to)
        )

    def each(first, last, act):
        def step(place, carry):
            act(place)
            return carry

        lax.fori_loop(first, last, step, 0)

    batch = count // 2
    batch_rows = batch * slots

    def pass_on(place):
        dispatch(place).wait_recv()
        forward(place).start()

    def project(first_place, half, first):
        for j in range(2):
            rows = arr[half, j, first_place : first_place + batch].reshape(batch_rows, width)
            for total, weight in ((gate, wg), (up, wu)):
                value = jnp.dot(rows, weight[2 * j + half], preferred_element_type=F32)
                if first and j == 0:
                    total[...] = value
                else:
                    total[...] += value

    def apply_experts(number):
        first_place = number * batch
        project(first_place, c, True)
        each(first_place, first_place + batch, lambda place: forward(place).wait_recv())
        project(first_place, 1 - c, False)
        gated = jnp.minimum(gate[...], LIMIT)
        lifted = jnp.clip(up[...], -LIMIT, LIMIT)
        activated = (gated * jax.nn.sigmoid(1.702 * gated) * (lifted + 1.0)).astype(BF16)

        def down(k):
            return lax.dot_general(activated, wd[k], (((1,), (1,)), ((), ())), preferred_element_type=F32)

        incoming = []
        for j in range(2):
            osend[number, j] = down(2 * j + 1 - c).astype(BF16)
            at = S_OUT + 2 * number + j
            incoming.append(send(osend.at[number, j], orecv.at[number, j], at, at, 1))
        for j in range(2):
            kept[j] = down(2 * j + c)
        return incoming

    def give_back(number, incoming):
        first_place = number * batch
        for j in range(2):
            incoming[j].wait_recv()
            total = (kept[j] + orecv[number, j].astype(F32)).astype(BF16)
            rbuf[j, first_place : first_place + batch] = total.reshape(batch, slots, width)
            each(max(first_place, 1), first_place + batch, lambda place: giveback(j, place).start())

    know(digits)
    each(1, count, lambda place: dispatch(place).start())
    for j in range(2):
        arr[c, j, 0] = outbox[j, expert]
    forward(0).start()
    each(1, batch, pass_on)
    for number in (L_GATE, L_UP, L_DOWN):
        loads[number].wait()
    incoming = apply_experts(0)
    each(batch, count, pass_on)
    give_back(0, incoming)
    incoming = apply_experts(1)
    give_back(1, incoming)
    for j in range(2):
        ret[j, expert] = rbuf[j, 0]

    high = share.astype(BF16)
    low = (share - high.astype(F32)).astype(BF16)
    both = jnp.concatenate([high, low], axis=0)
    part_in = []
    for j in range(2):
        each(1, count, lambda place: giveback(j, place).wait_recv())
        mixed = jnp.dot(both, ret[j].reshape(count * slots, width), preferred_element_type=F32)
        part_s[j] = (mixed[:group_rows] + mixed[group_rows:]).astype(BF16)
        part_in.append(send(part_s.at[j], part_r.at[j], S_PART + j, S_PART + j, 2))
    loads[L_QKV].wait()
    next_in = []
    qkv = jnp.zeros((group_rows, wq.shape[2]), F32)
    squares = jnp.zeros((group_rows, 1), F32)

    def project_next(half, j, qkv, squares):
        k = 2 * j + half
        rows = nextb[half, j].astype(F32)
        nextf[k] = rows
        squares += jnp.sum(rows * rows, axis=1, keepdims=True)
        qkv += jnp.dot((rows * gains[1, k]).astype(BF16), wq[k], preferred_element_type=F32)
        return qkv, squares

    for j in range(2):
        part_in[j].wait_recv()
        moe_out = part_s[j].astype(F32) + part_r[j].astype(F32)
        nextb[c, j] = (stream[j].astype(F32) + moe_out).astype(BF16)
        next_in.append(send(nextb.at[c, j], nextb.at[c, j], S_NEXT + j, S_NEXT + j, 1))
        qkv, squares = project_next(c, j, qkv, squares)
    for j in range(2):
        next_in[j].wait_recv()
        qkv, squares = project_next(1 - c, j, qkv, squares)
    qkv = qkv * lax.rsqrt(squares / (NDP * width) + EPSILON)
    columns = qkv.shape[1]
    for d in range(NDP):
        qbuf[d] = qkv[ROWS * d : ROWS * d + ROWS].astype(BF16)
    own_columns = pl.ds(pl.multiple_of(dp * columns, 128), columns)
    qkv_in = []
    for offset in (2, 3, 1):
        peer = group_peer(z, c, offset)
        theirs = lax.rem(peer, 2) * 2 + lax.div(peer, 2)
        qkv_in.append(
            send(qbuf.at[theirs], qkv_out.at[:, own_columns], S_QKV + offset - 1, S_QKV + offset - 1, offset)
        )
    qkv_out[:, own_columns] = qbuf[block]
    start = pl.multiple_of(block * ROWS, ROWS)
    for k in range(NDP):
        next_out[:, width * k : width * k + width] = nextf[k, pl.ds(start, ROWS), :].astype(BF16)

    def all_sent(place):
        dispatch(place).wait_send()
        for j in range(2):
            giveback(j, place).wait_send()

    each(1, count, all_sent)
    each(0, count, lambda place: forward(place).wait_send())
    for copy in sent:
        copy.wait_send()
    for copy in qkv_in:
        copy.wait_recv()


def layer_call(args, count):
    (queries, kv_pool, page_table, held_tokens, sinks, residual, route_ids, route_weights, moe_gain,
     w_gate, w_up, w_down, o_weight, attn_gain, qkv_weight) = args
    width = residual.shape[1] // NDP
    hidden = w_gate.shape[2]
    columns = qkv_weight.shape[1]
    slots = NDP * (2 * ROWS * TOP // count)
    group_rows = NDP * ROWS
    all_slots = count * slots
    hbm = pl.BlockSpec(memory_space=pltpu.HBM)
    out = pl.BlockSpec(memory_space=pltpu.VMEM)
    vmem, dma = pltpu.VMEM, pltpu.SemaphoreType.DMA
    pairs = (2, ROWS, HEADS // 2, PAIR)
    return pl.pallas_call(
        layer_kernel,
        out_shape=(
            jax.ShapeDtypeStruct((ROWS, NDP * width), BF16),
            jax.ShapeDtypeStruct((ROWS, NDP * columns), BF16),
        ),
        in_specs=[hbm] * 15,
        out_specs=(out, out),
        scratch_shapes=[
            vmem(kv_pool.shape, BF16),
            vmem((width, HEADS * HD), BF16),
            vmem((NDP, width, hidden), BF16),
            vmem((NDP, width, hidden), BF16),
            vmem((NDP, width, hidden), BF16),
            vmem((NDP, width, columns), BF16),
            pltpu.SMEM((NDP,) + page_table.shape, jnp.int32),
            pltpu.SMEM((NDP, NDP, ROWS), jnp.int32),
            pltpu.SMEM((TOP, ROWS), jnp.int32),
            pltpu.SMEM((TOP, ROWS), F32),
            vmem((1, HEADS), F32),
            vmem((NDP * width,), F32),
            vmem((NDP * width,), F32),
            vmem((2, NDP, 1, width), F32),
            vmem((NDP, ROWS, HEADS * HD), BF16),
            vmem((ROWS * HEADS // 2, PAIR), F32),
            vmem((ROWS, NDP * width), BF16),
            vmem((NDP, ROWS, width), BF16),
            vmem((NDP, ROWS, width), BF16),
            vmem((ROWS, all_slots), F32),
            vmem((NDP, ROWS, all_slots), F32),
            vmem(pairs, F32),
            vmem((2, HEADS, PAIR), F32),
            vmem(pairs, BF16),
            vmem((2, HEADS, PAIR), F32),
            vmem(pairs, BF16),
            vmem((2, HEADS, PAIR), F32),
            vmem(pairs, BF16),
            vmem((HEADS, PAIR), F32),
            vmem(pairs, BF16),
            vmem((HEADS, PAIR), F32),
            vmem((2 * ROWS * HEADS // 2, PAIR), F32),
            vmem((2, 2 * ROWS, HEADS * HD), BF16),
            vmem((2, group_rows, width), BF16),
            vmem((NDP, 8, 128), F32),
            vmem((2, count, slots, width), BF16),
            vmem((2, 2, count, slots, width), BF16),
            vmem((all_slots // 2, hidden), F32),
            vmem((all_slots // 2, hidden), F32),
            vmem((2, 2, all_slots // 2, width), BF16),
            vmem((2, 2, all_slots // 2, width), BF16),
            vmem((2, all_slots // 2, width), F32),
            vmem((2, count, slots, width), BF16),
            vmem((2, count, slots, width), BF16),
            vmem((2, group_rows, width), BF16),
            vmem((2, group_rows, width), BF16),
            vmem((2, 2, group_rows, width), BF16),
            vmem((NDP, group_rows, width), F32),
            vmem((NDP, ROWS, columns), BF16),
            dma((15,)),
            dma((N_SEM,)),
            dma((N_SEM,)),
            dma((count,)),
            dma((count,)),
            dma((count,)),
            dma((count,)),
            dma((2, count)),
            dma((2, count)),
            pltpu.SemaphoreType.REGULAR((count.bit_length() - 1,)),
        ],
        compiler_params=pltpu.CompilerParams(collective_id=0, has_side_effects=True, vmem_limit_bytes=44 * 2**20),
        name="layer",
    )(*[pltpu.with_memory_space_constraint(x, pltpu.HBM) for x in (
        queries,
        kv_pool,
        page_table,
        held_tokens.T,
        sinks.reshape(1, HEADS),
        residual,
        route_ids.T,
        route_weights.T,
        moe_gain,
        w_gate.reshape(NDP, width, hidden),
        w_up.reshape(NDP, width, hidden),
        w_down[0].T.reshape(NDP, width, hidden),
        o_weight.T,
        attn_gain,
        qkv_weight.reshape(NDP, width, columns),
    )])


def body(*args):
    return layer_call(args, lax.axis_size("expert"))


def solution(mesh):
    in_specs = (
        P(("dp", "expert"), None),
        P(("dp", "expert"), None, None),
        P(("dp", "expert"), None, None),
        P(("dp", "expert"), None),
        P(),
        P(("dp", "expert"), None),
        P(("dp", "expert"), None),
        P(("dp", "expert"), None),
        P(),
        P("expert", None, "dp"),
        P("expert", None, "dp"),
        P("expert", "dp", None),
        P(None, "dp"),
        P(),
        P(None, "dp"),
    )
    out_specs = (P(("dp", "expert"), None), P(("dp", "expert"), None))
    return jax.shard_map(body, mesh=mesh, in_specs=in_specs, out_specs=out_specs, check_vma=False)
```

```python
import math

import jax
import jax.numpy as jnp
from jax import lax
from jax.experimental import pallas as pl
from jax.experimental.pallas import tpu as pltpu
from jax.sharding import PartitionSpec as P

HEADS = 64
KVH = 8
HD = 64
TOP = 4
PAGE = 16
PPH = 16
SPAN = PPH * PAGE
WIDE = KVH * HD
PAIR = 2 * HD
ROWS = 8
NDP = 4

EPSILON = 1e-05
LIMIT = 7.0
MESH = pl.DeviceIdType.MESH
F32 = jnp.float32
BF16 = jnp.bfloat16

S_TAB, S_HELD, S_Q, S_RES, S_COM, S_SUM, S_QKV = range(0, 21, 3)
S_PAIR_N, S_PAIR_ML, S_X_N, S_PART, S_NEXT = range(21, 31, 2)
BATCHES = 4
S_X_ML, S_LHS, S_STREAM, S_OUT, N_SEM = 31, 32, 33, 34, 34 + 2 * BATCHES
L_TAB, L_HELD, L_Q, L_POOL, L_SINK, L_IDS, L_WEIGHTS, L_RES, L_OW, L_MGAIN, L_GATE, L_UP, L_DOWN, L_AGAIN, L_QKV = range(15)


def position():
    dp = lax.axis_index("dp")
    expert = lax.axis_index("expert")
    return dp, lax.div(dp, 2), lax.rem(dp, 2), expert


def group_peer(z, c, offset):
    return lax.rem(z + offset // 2, 2) * 2 + lax.rem(c + offset % 2, 2)


def remote(src, dst, sems, sent, landed, device):
    return pltpu.make_async_remote_copy(
        src_ref=src,
        dst_ref=dst,
        send_sem=sems[0].at[sent],
        recv_sem=sems[1].at[landed],
        device_id=device,
        device_id_type=MESH,
    )


def spread_queries(wide):
    turned = pltpu.roll(wide, HD, 1)
    row = lax.broadcasted_iota(jnp.int32, (HEADS // 2, PAIR), 0)
    lane = lax.broadcasted_iota(jnp.int32, (HEADS // 2, PAIR), 1)
    odd_group = lax.rem(lax.div(row, 4), 2) == 1
    own_half = (lane >= HD) == odd_group
    even = jnp.where(own_half, jnp.where(odd_group, turned, wide), 0.0)
    odd = jnp.where(own_half, jnp.where(odd_group, wide, turned), 0.0)
    tile = lax.div(row, 8)
    parts = []
    for heads in (even, odd):
        parts.append(jnp.concatenate([jnp.where(tile == t, heads, 0.0) for t in range(4)], axis=1))
    return jnp.concatenate(parts, axis=0).astype(BF16)


def fold_values(wide):
    row = lax.broadcasted_iota(jnp.int32, (HEADS // 2, PAIR), 0)
    lane = lax.broadcasted_iota(jnp.int32, (HEADS // 2, PAIR), 1)
    odd_group = lax.rem(lax.div(row, 4), 2) == 1

    def own_tiles(base):
        return jnp.concatenate(
            [wide[base + 8 * t : base + 8 * t + 8, PAIR * t : PAIR * t + PAIR] for t in range(4)], axis=0
        )

    even, odd = own_tiles(0), own_tiles(HEADS // 2)
    even = jnp.where(odd_group, pltpu.roll(even, HD, 1), even)
    odd = jnp.where(odd_group, odd, pltpu.roll(odd, HD, 1))
    return jnp.where(lane < HD, even, odd)


def pair_columns(column):
    lane = lax.broadcasted_iota(jnp.int32, (HEADS // 2, PAIR), 1)
    return jnp.where(lane < HD, column[: HEADS // 2], column[HEADS // 2 :])


def attend(queries, tables, counts, holder, pool, rows, write):
    token = lax.broadcasted_iota(jnp.int32, (HEADS, SPAN), 1)
    scores, held = [], []
    for row in rows:
        keys = jnp.concatenate([pool[tables[row, holder, page], :, :WIDE] for page in range(PPH)], axis=0)
        start = pl.multiple_of(row * (HEADS // 2), HEADS // 2)
        spread = spread_queries(queries[pl.ds(start, HEADS // 2), :])
        scores.append(
            lax.dot_general(spread, keys, (((1,), (1,)), ((), ())), preferred_element_type=F32)
            * (1.0 / math.sqrt(HD))
        )
        held.append(token < counts[holder, row])
    weights, highs, sums = [], [], []
    for score, usable in zip(scores, held):
        high = jnp.max(jnp.where(usable, score, -1e30), axis=1, keepdims=True)
        weight = jnp.where(usable, jnp.exp(score - high), 0.0)
        highs.append(high)
        sums.append(jnp.sum(weight, axis=1, keepdims=True))
        weights.append(weight.astype(BF16))
    results = []
    for row, weight in zip(rows, weights):
        values = jnp.concatenate([pool[tables[row, holder, page], :, WIDE:] for page in range(PPH)], axis=0)
        results.append(fold_values(jnp.dot(weight, values, preferred_element_type=F32)))
    for row, result, high, total in zip(rows, results, highs, sums):
        write(row, result, high, total)


def sink_columns(sinks):
    row = lax.broadcasted_iota(jnp.int32, (HEADS, HEADS), 0)
    lane = lax.broadcasted_iota(jnp.int32, (HEADS, HEADS), 1)
    half = HEADS // 2
    head = jnp.where(row < half, 2 * row, 2 * (row - half) + 1)
    return jnp.sum(jnp.where(lane == head, sinks, 0.0), axis=1, keepdims=True)


def combine_rows(ids, weights, table, block, slots):
    capacity = slots // NDP
    lane = lax.broadcasted_iota(jnp.int32, (1, table.shape[1]), 1)
    of_expert, at_slot = lax.div(lane, slots), lax.rem(lane, slots)
    taken = jnp.zeros_like(lane)
    for row in range(ROWS):
        hit = jnp.zeros_like(lane)
        weight = jnp.zeros(lane.shape, F32)
        total = jnp.zeros(lane.shape, F32)
        for k in range(TOP):
            match = of_expert == ids[k, row]
            hit = jnp.where(match, 1, hit)
            weight = jnp.where(match, weights[k, row], weight)
            total = total + weights[k, row]
        at = (hit == 1) & (at_slot == block * capacity + taken)
        table[row : row + 1, :] = jnp.where(at, weight / total, 0.0)
        taken = taken + hit


STEP = 8


def layer_kernel(
    q_hbm, pool_hbm, tab_hbm, held_hbm, sink_hbm, res_hbm, ids_hbm, weights_hbm, mgain_hbm,
    wg_hbm, wu_hbm, wd_hbm, ow_hbm, again_hbm, wq_hbm,
    next_out, qkv_out,
    pool, ow, wg, wu, wd, wq,
    tabs, helds, ids, weights, sinks, mgain, again, gains, qraw, qwide, resraw, resblk, resall, comown, comall,
    keep_n, keep_ml, send_n, send_ml, recv_n, recv_ml, xs_n, xs_ml, xr_n, xr_ml, att, lhs, stream, sums,
    outbox, arr, gate, up, osend, orecv, kept, rbuf, ret, part_s, part_r, nextb, nextf, qbuf,
    load_sem, send_sem, recv_sem, d_send, d_recv, f_send, f_recv, r_send, r_recv, round_sem,
):
    dp, z, c, expert = position()
    sems = (send_sem, recv_sem)
    count, slots, width = arr.shape[2], arr.shape[3], arr.shape[4]
    block = c * 2 + z

    barrier = pltpu.get_barrier_semaphore()
    for offset in (1, 2, 3):
        pl.semaphore_signal(barrier, inc=1, device_id=(group_peer(z, c, offset), expert), device_id_type=MESH)

    def neighbour(digit):
        step = 1 << digit
        return (dp, expert + step * (1 - 2 * lax.rem(lax.div(expert, step), 2)))

    digits = count.bit_length() - 1
    for digit in range(digits):
        pl.semaphore_signal(barrier, inc=1, device_id=neighbour(digit), device_id_type=MESH)

    def know(digit):
        if digit > 0:
            pl.semaphore_wait(round_sem.at[digit - 1], 1)
        if digit < digits:
            pl.semaphore_signal(round_sem.at[digit], inc=1, device_id=neighbour(digit), device_id_type=MESH)

    loads = {}
    for number, src, dst in (
        (L_TAB, tab_hbm, tabs.at[dp]),
        (L_HELD, held_hbm, helds.at[dp]),
        (L_Q, q_hbm, qraw.at[dp]),
        (L_POOL, pool_hbm, pool),
        (L_IDS, ids_hbm, ids),
        (L_WEIGHTS, weights_hbm, weights),
        (L_RES, res_hbm, resraw),
        (L_MGAIN, mgain_hbm, mgain),
        (L_AGAIN, again_hbm, again),
        (L_SINK, sink_hbm, sinks),
        (L_OW, ow_hbm, ow),
        (L_GATE, wg_hbm, wg),
        (L_UP, wu_hbm, wu),
        (L_DOWN, wd_hbm, wd),
        (L_QKV, wq_hbm, wq),
    ):
        loads[number] = pltpu.make_async_copy(src, dst, load_sem.at[number])
        loads[number].start()

    sent = []

    def send(src, dst, number, landed, offset):
        copy = remote(src, dst, sems, number, landed, (group_peer(z, c, offset), expert))
        copy.start()
        sent.append(copy)
        return copy

    lane = lax.broadcasted_iota(jnp.int32, (HEADS, PAIR), 1)

    def run_block(offset, number, numerators, stats):
        at = group_peer(z, c, offset)
        half = z if number == 0 else 1 - z
        stats[number] = jnp.zeros((HEADS, PAIR), F32)
        for pair in range(HEADS // 2):
            qwide[pl.ds(pair, ROWS, stride=HEADS // 2), :] = qraw[at, :, PAIR * pair : PAIR * pair + PAIR].astype(F32)

        def write(row, result, high, total):
            numerators[number, row] = result.astype(numerators.dtype)
            place = half * ROWS + row
            tile = jnp.where(lane == place, high, stats[number])
            stats[number] = jnp.where(lane == place + HD, total, tile)

        def step(index, carry):
            rows = [index * STEP + i for i in range(STEP)]
            attend(qwide, tabs.at[at], helds.at[at], dp, pool, rows, write)
            return carry

        lax.fori_loop(0, ROWS // STEP, step, 0)

    tab_in, held_in, q_in, res_in, com_in = {}, {}, {}, {}, {}

    def fetch_block(offset):
        tab_in[offset].wait_recv()
        held_in[offset].wait_recv()
        q_in[offset].wait_recv()

    def send_pair(number):
        return (
            send(send_n.at[number], recv_n.at[number], S_PAIR_N + number, S_PAIR_N + number, 1),
            send(send_ml.at[number], recv_ml.at[number], S_PAIR_ML + number, S_PAIR_ML + number, 1),
        )

    def factors(tile, number):
        half = z if number == 0 else 1 - z
        return pltpu.roll(tile, lax.rem(PAIR - half * ROWS, PAIR), 1)

    def merge_pair(number, incoming):
        for copy in incoming:
            copy.wait_recv()
        mine, other = keep_ml[number], recv_ml[number]
        high = jnp.maximum(mine, other)
        left, right = jnp.exp(mine - high), jnp.exp(other - high)
        total = mine * pltpu.roll(left, HD, 1) + other * pltpu.roll(right, HD, 1)
        keep_ml[number] = jnp.where(lane < HD, high, total)
        left, right = factors(left, number), factors(right, number)
        for row in range(ROWS):
            merged = keep_n[number, row] * pair_columns(left[:, row : row + 1]) + recv_n[number, row].astype(
                F32
            ) * pair_columns(right[:, row : row + 1])
            keep_n[number, row] = merged
            xs_n[number, row] = merged.astype(BF16)
        return send(xs_n.at[number], xr_n.at[1 - number], S_X_N + number, S_X_N + 1 - number, 2)

    pl.semaphore_wait(barrier, 3 + digits)
    know(0)
    for offset in (2, 1):
        q_in[offset] = send(q_hbm, qraw.at[dp], S_Q + offset - 1, S_Q + offset - 1, offset)
    for offset in (2, 3, 1):
        tab_in[offset] = send(tab_hbm, tabs.at[dp], S_TAB + offset - 1, S_TAB + offset - 1, offset)
        held_in[offset] = send(held_hbm, helds.at[dp], S_HELD + offset - 1, S_HELD + offset - 1, offset)
    for number in (L_IDS, L_WEIGHTS, L_RES, L_MGAIN, L_AGAIN):
        loads[number].wait()
    combine_rows(ids, weights, comown, block, slots)
    comall[block] = comown[...]
    for which, gain in enumerate((mgain, again)):
        whole = gain[...].reshape(1, NDP * width)
        for k in range(NDP):
            gains[which, k] = whole[:, width * k : width * k + width]
    for k in range(NDP):
        resblk[k] = resraw[:, width * k : width * k + width]
    resall[block] = resblk[dp]
    for number in (L_TAB, L_HELD, L_Q, L_POOL):
        loads[number].wait()
    run_block(0, 0, keep_n, keep_ml)
    fetch_block(1)
    run_block(1, 0, send_n, send_ml)
    pair_in = [send_pair(0)]
    know(1)
    fetch_block(2)
    cross = group_peer(z, c, 2)
    q_in[3] = send(qraw.at[cross], qraw.at[cross], S_Q + 2, S_Q + 2, 1)
    for offset in (2, 3, 1):
        peer = group_peer(z, c, offset)
        res_in[offset] = send(resblk.at[peer], resall.at[block], S_RES + offset - 1, S_RES + offset - 1, offset)
        com_in[offset] = send(comown, comall.at[block], S_COM + offset - 1, S_COM + offset - 1, offset)
    cross_in = [merge_pair(0, pair_in[0])]
    know(2)
    fetch_block(3)
    run_block(3, 1, send_n, send_ml)
    pair_in.append(send_pair(1))
    know(3)
    run_block(2, 1, keep_n, keep_ml)
    cross_in.append(merge_pair(1, pair_in[1]))
    xs_ml[...] = keep_ml[0] + keep_ml[1]
    cross_ml = send(xs_ml, xr_ml, S_X_ML, S_X_ML, 2)

    cross_ml.wait_recv()
    loads[L_SINK].wait()
    mine, other, sink = xs_ml[...], xr_ml[...], sink_columns(sinks[...])
    top = jnp.maximum(jnp.maximum(mine, other), sink)
    left, right = jnp.exp(mine - top), jnp.exp(other - top)
    total = mine * pltpu.roll(left, HD, 1) + other * pltpu.roll(right, HD, 1)
    below = pltpu.roll(total, HD, 1) + jnp.exp(sink - top)
    left, right = left / below, right / below
    for number in (0, 1):
        cross_in[1 - number].wait_recv()
        one, two = factors(left, number), factors(right, number)
        half = z if number == 0 else 1 - z
        for row in range(ROWS):
            attention = keep_n[number, row] * pair_columns(one[:, row : row + 1]) + xr_n[number, row].astype(
                F32
            ) * pair_columns(two[:, row : row + 1])
            start = pl.multiple_of((half * ROWS + row) * (HEADS // 2), HEADS // 2)
            att[pl.ds(start, HEADS // 2), :] = attention
    for pair in range(HEADS // 2):
        lhs[c, :, PAIR * pair : PAIR * pair + PAIR] = att[pl.ds(pair, 2 * ROWS, stride=HEADS // 2), :].astype(BF16)
    lhs_in = send(lhs.at[c], lhs.at[c], S_LHS, S_LHS, 1)
    for digit in range(4, digits):
        know(digit)
    for offset in (1, 2, 3):
        res_in[offset].wait_recv()
        com_in[offset].wait_recv()
    residual = jnp.concatenate([resall[d].astype(F32) for d in range(NDP)], axis=0)
    share = jnp.concatenate([comall[d] for d in range(NDP)], axis=0)
    picks = (share > 0).astype(F32).T.astype(BF16)
    loads[L_OW].wait()
    lhs_in.wait_recv()
    rows = jnp.concatenate([lhs[0], lhs[1]], axis=0)
    projected = lax.dot_general(rows, ow[...], (((1,), (1,)), ((), ())), preferred_element_type=F32)
    stream[z] = (residual + projected.astype(BF16).astype(F32)).astype(BF16)
    stream_in = send(stream.at[z], stream.at[z], S_STREAM, S_STREAM, 2)
    own = stream[z].astype(F32)
    group_rows = own.shape[0]
    diagonal = lax.broadcasted_iota(jnp.int32, (group_rows, 128), 0) == lax.broadcasted_iota(
        jnp.int32, (group_rows, 128), 1
    )
    square = jnp.sum(own * own, axis=1, keepdims=True)
    sums[dp] = jnp.broadcast_to(
        jnp.sum(jnp.where(diagonal, square, 0.0), axis=0, keepdims=True), sums.shape[1:]
    )
    sum_in = [
        send(sums.at[dp], sums.at[dp], S_SUM + offset - 1, S_SUM + offset - 1, offset) for offset in (2, 3, 1)
    ]
    for copy in sum_in:
        copy.wait_recv()
    square = (sums[0] + sums[1] + sums[2] + sums[3])[:1]
    square = jnp.sum(jnp.where(diagonal, square, 0.0), axis=1, keepdims=True)
    scale = lax.rsqrt(square / (NDP * width) + EPSILON)
    stream_in.wait_recv()
    for j in range(2):
        rows = (stream[j].astype(F32) * scale * gains[0, 2 * j + c]).astype(BF16)
        picked = jnp.dot(picks, rows, preferred_element_type=F32).astype(BF16)
        outbox[j] = picked.reshape(count, slots, width)

    def partner(place, sign):
        dy = 2 * lax.rem(lax.div(place, 8), 2) + lax.div(place, 16)
        dz, dx = lax.rem(lax.div(place, 4), 2), lax.rem(place, 4)
        at_z = lax.rem(lax.div(expert, 16) + dz, 2)
        at_y = lax.rem(lax.rem(lax.div(expert, 4), 4) + sign * dy + 4, 4)
        at_x = lax.rem(lax.rem(expert, 4) + sign * dx + 4, 4)
        return 16 * at_z + 4 * at_y + at_x

    def dispatch(place):
        to = partner(place, 1)
        return remote(outbox.at[:, to], arr.at[c, :, place], (d_send, d_recv), place, place, (dp, to))

    def forward(place):
        return remote(
            arr.at[c, :, place], arr.at[c, :, place], (f_send, f_recv), place, place,
            (group_peer(z, c, 1), expert),
        )

    def giveback(j, place):
        to = partner(place, -1)
        return remote(
            rbuf.at[j, place], ret.at[j, expert], (r_send.at[j], r_recv.at[j]), place, place, (dp, to)
        )

    def each(first, last, act):
        def step(place, carry):
            act(place)
            return carry

        lax.fori_loop(first, last, step, 0)

    batch = count // BATCHES
    batch_rows = batch * slots

    def pass_on(place):
        dispatch(place).wait_recv()
        forward(place).start()

    def project(first_place, half, first):
        for j in range(2):
            rows = arr[half, j, first_place : first_place + batch].reshape(batch_rows, width)
            for total, weight in ((gate, wg), (up, wu)):
                value = jnp.dot(rows, weight[2 * j + half], preferred_element_type=F32)
                if first and j == 0:
                    total[...] = value
                else:
                    total[...] += value

    def apply_experts(number):
        first_place = number * batch
        project(first_place, c, True)
        each(first_place, first_place + batch, lambda place: forward(place).wait_recv())
        project(first_place, 1 - c, False)
        gated = jnp.minimum(gate[...], LIMIT)
        lifted = jnp.clip(up[...], -LIMIT, LIMIT)
        activated = (gated * jax.nn.sigmoid(1.702 * gated) * (lifted + 1.0)).astype(BF16)

        def down(k):
            return lax.dot_general(activated, wd[k], (((1,), (1,)), ((), ())), preferred_element_type=F32)

        incoming = []
        for j in range(2):
            osend[number, j] = down(2 * j + 1 - c).astype(BF16)
            at = S_OUT + 2 * number + j
            incoming.append(send(osend.at[number, j], orecv.at[number, j], at, at, 1))
        for j in range(2):
            kept[j] = down(2 * j + c)
        return incoming

    def give_back(number, incoming):
        first_place = number * batch
        for j in range(2):
            incoming[j].wait_recv()
            total = (kept[j] + orecv[number, j].astype(F32)).astype(BF16)
            rbuf[j, first_place : first_place + batch] = total.reshape(batch, slots, width)
            each(max(first_place, 1), first_place + batch, lambda place: giveback(j, place).start())

    know(digits)
    each(1, count, lambda place: dispatch(place).start())
    for j in range(2):
        arr[c, j, 0] = outbox[j, expert]
    forward(0).start()
    for number in (L_GATE, L_UP, L_DOWN):
        loads[number].wait()
    incoming = None
    for number in range(BATCHES):
        each(max(1, batch * number), batch * (number + 1), pass_on)
        if number > 0:
            give_back(number - 1, incoming)
        incoming = apply_experts(number)
    give_back(BATCHES - 1, incoming)
    for j in range(2):
        ret[j, expert] = rbuf[j, 0]

    high = share.astype(BF16)
    low = (share - high.astype(F32)).astype(BF16)
    both = jnp.concatenate([high, low], axis=0)
    part_in = []
    for j in range(2):
        each(1, count, lambda place: giveback(j, place).wait_recv())
        mixed = jnp.dot(both, ret[j].reshape(count * slots, width), preferred_element_type=F32)
        part_s[j] = (mixed[:group_rows] + mixed[group_rows:]).astype(BF16)
        part_in.append(send(part_s.at[j], part_r.at[j], S_PART + j, S_PART + j, 2))
    loads[L_QKV].wait()
    next_in = []
    qkv = jnp.zeros((group_rows, wq.shape[2]), F32)
    squares = jnp.zeros((group_rows, 1), F32)

    def project_next(half, j, qkv, squares):
        k = 2 * j + half
        rows = nextb[half, j].astype(F32)
        nextf[k] = rows
        squares += jnp.sum(rows * rows, axis=1, keepdims=True)
        qkv += jnp.dot((rows * gains[1, k]).astype(BF16), wq[k], preferred_element_type=F32)
        return qkv, squares

    for j in range(2):
        part_in[j].wait_recv()
        moe_out = part_s[j].astype(F32) + part_r[j].astype(F32)
        nextb[c, j] = (stream[j].astype(F32) + moe_out).astype(BF16)
        next_in.append(send(nextb.at[c, j], nextb.at[c, j], S_NEXT + j, S_NEXT + j, 1))
        qkv, squares = project_next(c, j, qkv, squares)
    for j in range(2):
        next_in[j].wait_recv()
        qkv, squares = project_next(1 - c, j, qkv, squares)
    qkv = qkv * lax.rsqrt(squares / (NDP * width) + EPSILON)
    columns = qkv.shape[1]
    for d in range(NDP):
        qbuf[d] = qkv[ROWS * d : ROWS * d + ROWS].astype(BF16)
    own_columns = pl.ds(pl.multiple_of(dp * columns, 128), columns)
    qkv_in = []
    for offset in (2, 3, 1):
        peer = group_peer(z, c, offset)
        theirs = lax.rem(peer, 2) * 2 + lax.div(peer, 2)
        qkv_in.append(
            send(qbuf.at[theirs], qkv_out.at[:, own_columns], S_QKV + offset - 1, S_QKV + offset - 1, offset)
        )
    qkv_out[:, own_columns] = qbuf[block]
    start = pl.multiple_of(block * ROWS, ROWS)
    for k in range(NDP):
        next_out[:, width * k : width * k + width] = nextf[k, pl.ds(start, ROWS), :].astype(BF16)

    def all_sent(place):
        dispatch(place).wait_send()
        for j in range(2):
            giveback(j, place).wait_send()

    each(1, count, all_sent)
    each(0, count, lambda place: forward(place).wait_send())
    for copy in sent:
        copy.wait_send()
    for copy in qkv_in:
        copy.wait_recv()


def layer_call(args, count):
    (queries, kv_pool, page_table, held_tokens, sinks, residual, route_ids, route_weights, moe_gain,
     w_gate, w_up, w_down, o_weight, attn_gain, qkv_weight) = args
    width = residual.shape[1] // NDP
    hidden = w_gate.shape[2]
    columns = qkv_weight.shape[1]
    slots = NDP * (2 * ROWS * TOP // count)
    group_rows = NDP * ROWS
    all_slots = count * slots
    hbm = pl.BlockSpec(memory_space=pltpu.HBM)
    out = pl.BlockSpec(memory_space=pltpu.VMEM)
    vmem, dma = pltpu.VMEM, pltpu.SemaphoreType.DMA
    pairs = (2, ROWS, HEADS // 2, PAIR)
    return pl.pallas_call(
        layer_kernel,
        out_shape=(
            jax.ShapeDtypeStruct((ROWS, NDP * width), BF16),
            jax.ShapeDtypeStruct((ROWS, NDP * columns), BF16),
        ),
        in_specs=[hbm] * 15,
        out_specs=(out, out),
        scratch_shapes=[
            vmem(kv_pool.shape, BF16),
            vmem((width, HEADS * HD), BF16),
            vmem((NDP, width, hidden), BF16),
            vmem((NDP, width, hidden), BF16),
            vmem((NDP, width, hidden), BF16),
            vmem((NDP, width, columns), BF16),
            pltpu.SMEM((NDP,) + page_table.shape, jnp.int32),
            pltpu.SMEM((NDP, NDP, ROWS), jnp.int32),
            pltpu.SMEM((TOP, ROWS), jnp.int32),
            pltpu.SMEM((TOP, ROWS), F32),
            vmem((1, HEADS), F32),
            vmem((NDP * width,), F32),
            vmem((NDP * width,), F32),
            vmem((2, NDP, 1, width), F32),
            vmem((NDP, ROWS, HEADS * HD), BF16),
            vmem((ROWS * HEADS // 2, PAIR), F32),
            vmem((ROWS, NDP * width), BF16),
            vmem((NDP, ROWS, width), BF16),
            vmem((NDP, ROWS, width), BF16),
            vmem((ROWS, all_slots), F32),
            vmem((NDP, ROWS, all_slots), F32),
            vmem(pairs, F32),
            vmem((2, HEADS, PAIR), F32),
            vmem(pairs, BF16),
            vmem((2, HEADS, PAIR), F32),
            vmem(pairs, BF16),
            vmem((2, HEADS, PAIR), F32),
            vmem(pairs, BF16),
            vmem((HEADS, PAIR), F32),
            vmem(pairs, BF16),
            vmem((HEADS, PAIR), F32),
            vmem((2 * ROWS * HEADS // 2, PAIR), F32),
            vmem((2, 2 * ROWS, HEADS * HD), BF16),
            vmem((2, group_rows, width), BF16),
            vmem((NDP, 8, 128), F32),
            vmem((2, count, slots, width), BF16),
            vmem((2, 2, count, slots, width), BF16),
            vmem((all_slots // BATCHES, hidden), F32),
            vmem((all_slots // BATCHES, hidden), F32),
            vmem((BATCHES, 2, all_slots // BATCHES, width), BF16),
            vmem((BATCHES, 2, all_slots // BATCHES, width), BF16),
            vmem((2, all_slots // BATCHES, width), F32),
            vmem((2, count, slots, width), BF16),
            vmem((2, count, slots, width), BF16),
            vmem((2, group_rows, width), BF16),
            vmem((2, group_rows, width), BF16),
            vmem((2, 2, group_rows, width), BF16),
            vmem((NDP, group_rows, width), F32),
            vmem((NDP, ROWS, columns), BF16),
            dma((15,)),
            dma((N_SEM,)),
            dma((N_SEM,)),
            dma((count,)),
            dma((count,)),
            dma((count,)),
            dma((count,)),
            dma((2, count)),
            dma((2, count)),
            pltpu.SemaphoreType.REGULAR((count.bit_length() - 1,)),
        ],
        compiler_params=pltpu.CompilerParams(collective_id=0, has_side_effects=True, vmem_limit_bytes=44 * 2**20),
        name="layer",
    )(*[pltpu.with_memory_space_constraint(x, pltpu.HBM) for x in (
        queries,
        kv_pool,
        page_table,
        held_tokens.T,
        sinks.reshape(1, HEADS),
        residual,
        route_ids.T,
        route_weights.T,
        moe_gain,
        w_gate.reshape(NDP, width, hidden),
        w_up.reshape(NDP, width, hidden),
        w_down[0].T.reshape(NDP, width, hidden),
        o_weight.T,
        attn_gain,
        qkv_weight.reshape(NDP, width, columns),
    )])


def body(*args):
    return layer_call(args, lax.axis_size("expert"))


def solution(mesh):
    in_specs = (
        P(("dp", "expert"), None),
        P(("dp", "expert"), None, None),
        P(("dp", "expert"), None, None),
        P(("dp", "expert"), None),
        P(),
        P(("dp", "expert"), None),
        P(("dp", "expert"), None),
        P(("dp", "expert"), None),
        P(),
        P("expert", None, "dp"),
        P("expert", None, "dp"),
        P("expert", "dp", None),
        P(None, "dp"),
        P(),
        P(None, "dp"),
    )
    out_specs = (P(("dp", "expert"), None), P(("dp", "expert"), None))
    return jax.shard_map(body, mesh=mesh, in_specs=in_specs, out_specs=out_specs, check_vma=False)
```

```python
import math

import jax
import jax.numpy as jnp
from jax import lax
from jax.experimental import pallas as pl
from jax.experimental.pallas import tpu as pltpu
from jax.sharding import PartitionSpec as P

HEADS = 64
KVH = 8
HD = 64
TOP = 4
PAGE = 16
PPH = 16
SPAN = PPH * PAGE
WIDE = KVH * HD
PAIR = 2 * HD
ROWS = 8
NDP = 4

EPSILON = 1e-05
LIMIT = 7.0
MESH = pl.DeviceIdType.MESH
F32 = jnp.float32
BF16 = jnp.bfloat16

S_TAB, S_HELD, S_Q, S_RES, S_COM, S_SUM, S_QKV = range(0, 21, 3)
S_PAIR_N, S_PAIR_ML, S_X_N, S_PART, S_NEXT = range(21, 31, 2)
BATCHES = 4
S_X_ML, S_LHS, S_STREAM, S_OUT, N_SEM = 31, 32, 33, 34, 34 + 2 * BATCHES
L_TAB, L_HELD, L_Q, L_POOL, L_SINK, L_IDS, L_WEIGHTS, L_RES, L_OW, L_MGAIN, L_GATE, L_UP, L_DOWN, L_AGAIN, L_QKV = range(15)


def position():
    dp = lax.axis_index("dp")
    expert = lax.axis_index("expert")
    return dp, lax.div(dp, 2), lax.rem(dp, 2), expert


def group_peer(z, c, offset):
    return lax.rem(z + offset // 2, 2) * 2 + lax.rem(c + offset % 2, 2)


def remote(src, dst, sems, sent, landed, device):
    return pltpu.make_async_remote_copy(
        src_ref=src,
        dst_ref=dst,
        send_sem=sems[0].at[sent],
        recv_sem=sems[1].at[landed],
        device_id=device,
        device_id_type=MESH,
    )


def spread_queries(wide):
    turned = pltpu.roll(wide, HD, 1)
    row = lax.broadcasted_iota(jnp.int32, (HEADS // 2, PAIR), 0)
    lane = lax.broadcasted_iota(jnp.int32, (HEADS // 2, PAIR), 1)
    odd_group = lax.rem(lax.div(row, 4), 2) == 1
    own_half = (lane >= HD) == odd_group
    even = jnp.where(own_half, jnp.where(odd_group, turned, wide), 0.0)
    odd = jnp.where(own_half, jnp.where(odd_group, wide, turned), 0.0)
    tile = lax.div(row, 8)
    parts = []
    for heads in (even, odd):
        parts.append(jnp.concatenate([jnp.where(tile == t, heads, 0.0) for t in range(4)], axis=1))
    return jnp.concatenate(parts, axis=0).astype(BF16)


def fold_values(wide):
    row = lax.broadcasted_iota(jnp.int32, (HEADS // 2, PAIR), 0)
    lane = lax.broadcasted_iota(jnp.int32, (HEADS // 2, PAIR), 1)
    odd_group = lax.rem(lax.div(row, 4), 2) == 1

    def own_tiles(base):
        return jnp.concatenate(
            [wide[base + 8 * t : base + 8 * t + 8, PAIR * t : PAIR * t + PAIR] for t in range(4)], axis=0
        )

    even, odd = own_tiles(0), own_tiles(HEADS // 2)
    even = jnp.where(odd_group, pltpu.roll(even, HD, 1), even)
    odd = jnp.where(odd_group, odd, pltpu.roll(odd, HD, 1))
    return jnp.where(lane < HD, even, odd)


def pair_columns(column):
    lane = lax.broadcasted_iota(jnp.int32, (HEADS // 2, PAIR), 1)
    return jnp.where(lane < HD, column[: HEADS // 2], column[HEADS // 2 :])


def attend(queries, tables, counts, holder, pool, rows, write):
    token = lax.broadcasted_iota(jnp.int32, (HEADS, SPAN), 1)
    scores, held = [], []
    for row in rows:
        keys = jnp.concatenate([pool[tables[row, holder, page], :, :WIDE] for page in range(PPH)], axis=0)
        start = pl.multiple_of(row * (HEADS // 2), HEADS // 2)
        spread = spread_queries(queries[pl.ds(start, HEADS // 2), :])
        scores.append(
            lax.dot_general(spread, keys, (((1,), (1,)), ((), ())), preferred_element_type=F32)
            * (1.0 / math.sqrt(HD))
        )
        held.append(token < counts[holder, row])
    weights, highs, sums = [], [], []
    for score, usable in zip(scores, held):
        high = jnp.max(jnp.where(usable, score, -1e30), axis=1, keepdims=True)
        weight = jnp.where(usable, jnp.exp(score - high), 0.0)
        highs.append(high)
        sums.append(jnp.sum(weight, axis=1, keepdims=True))
        weights.append(weight.astype(BF16))
    results = []
    for row, weight in zip(rows, weights):
        values = jnp.concatenate([pool[tables[row, holder, page], :, WIDE:] for page in range(PPH)], axis=0)
        results.append(fold_values(jnp.dot(weight, values, preferred_element_type=F32)))
    for row, result, high, total in zip(rows, results, highs, sums):
        write(row, result, high, total)


def sink_columns(sinks):
    row = lax.broadcasted_iota(jnp.int32, (HEADS, HEADS), 0)
    lane = lax.broadcasted_iota(jnp.int32, (HEADS, HEADS), 1)
    half = HEADS // 2
    head = jnp.where(row < half, 2 * row, 2 * (row - half) + 1)
    return jnp.sum(jnp.where(lane == head, sinks, 0.0), axis=1, keepdims=True)


def combine_rows(ids, weights, table, block, slots):
    capacity = slots // NDP
    lane = lax.broadcasted_iota(jnp.int32, (1, table.shape[1]), 1)
    of_expert, at_slot = lax.div(lane, slots), lax.rem(lane, slots)
    taken = jnp.zeros_like(lane)
    for row in range(ROWS):
        hit = jnp.zeros_like(lane)
        weight = jnp.zeros(lane.shape, F32)
        total = jnp.zeros(lane.shape, F32)
        for k in range(TOP):
            match = of_expert == ids[k, row]
            hit = jnp.where(match, 1, hit)
            weight = jnp.where(match, weights[k, row], weight)
            total = total + weights[k, row]
        at = (hit == 1) & (at_slot == block * capacity + taken)
        table[row : row + 1, :] = jnp.where(at, weight / total, 0.0)
        taken = taken + hit


STEP = 8


def layer_kernel(
    q_hbm, pool_hbm, tab_hbm, held_hbm, sink_hbm, res_hbm, ids_hbm, weights_hbm, mgain_hbm,
    wg_hbm, wu_hbm, wd_hbm, ow_hbm, again_hbm, wq_hbm,
    next_out, qkv_out,
    pool, ow, wg, wu, wd, wq,
    tabs, helds, ids, weights, sinks, mgain, again, gains, qraw, qwide, resraw, resblk, resall, comown, comall,
    keep_n, keep_ml, send_n, send_ml, recv_n, recv_ml, xs_n, xs_ml, xr_n, xr_ml, att, lhs, stream, sums,
    outbox, arr, gate, up, osend, orecv, kept, rbuf, ret, part_s, part_r, nextb, nextf, qbuf,
    load_sem, send_sem, recv_sem, d_send, d_recv, f_send, f_recv, r_send, r_recv, round_sem,
):
    dp, z, c, expert = position()
    sems = (send_sem, recv_sem)
    count, slots, width = arr.shape[2], arr.shape[3], arr.shape[4]
    block = c * 2 + z

    barrier = pltpu.get_barrier_semaphore()
    for offset in (1, 2, 3):
        pl.semaphore_signal(barrier, inc=1, device_id=(group_peer(z, c, offset), expert), device_id_type=MESH)

    def neighbour(digit):
        step = 1 << digit
        return (dp, expert + step * (1 - 2 * lax.rem(lax.div(expert, step), 2)))

    digits = count.bit_length() - 1
    for digit in range(digits):
        pl.semaphore_signal(barrier, inc=1, device_id=neighbour(digit), device_id_type=MESH)

    def know(digit):
        if digit > 0:
            pl.semaphore_wait(round_sem.at[digit - 1], 1)
        if digit < digits:
            pl.semaphore_signal(round_sem.at[digit], inc=1, device_id=neighbour(digit), device_id_type=MESH)

    loads = {}
    for number, src, dst in (
        (L_TAB, tab_hbm, tabs.at[dp]),
        (L_HELD, held_hbm, helds.at[dp]),
        (L_Q, q_hbm, qraw.at[dp]),
        (L_POOL, pool_hbm, pool),
        (L_IDS, ids_hbm, ids),
        (L_WEIGHTS, weights_hbm, weights),
        (L_RES, res_hbm, resraw),
        (L_MGAIN, mgain_hbm, mgain),
        (L_AGAIN, again_hbm, again),
        (L_SINK, sink_hbm, sinks),
        (L_OW, ow_hbm, ow),
        (L_GATE, wg_hbm, wg),
        (L_UP, wu_hbm, wu),
        (L_DOWN, wd_hbm, wd),
        (L_QKV, wq_hbm, wq),
    ):
        loads[number] = pltpu.make_async_copy(src, dst, load_sem.at[number])
        loads[number].start()

    sent = []

    def send(src, dst, number, landed, offset):
        copy = remote(src, dst, sems, number, landed, (group_peer(z, c, offset), expert))
        copy.start()
        sent.append(copy)
        return copy

    lane = lax.broadcasted_iota(jnp.int32, (HEADS, PAIR), 1)

    def run_block(offset, number, numerators, stats):
        at = group_peer(z, c, offset)
        half = z if number == 0 else 1 - z
        stats[number] = jnp.zeros((HEADS, PAIR), F32)
        for pair in range(HEADS // 2):
            qwide[pl.ds(pair, ROWS, stride=HEADS // 2), :] = qraw[at, :, PAIR * pair : PAIR * pair + PAIR].astype(F32)

        def write(row, result, high, total):
            numerators[number, row] = result.astype(numerators.dtype)
            place = half * ROWS + row
            tile = jnp.where(lane == place, high, stats[number])
            stats[number] = jnp.where(lane == place + HD, total, tile)

        def step(index, carry):
            rows = [index * STEP + i for i in range(STEP)]
            attend(qwide, tabs.at[at], helds.at[at], dp, pool, rows, write)
            return carry

        lax.fori_loop(0, ROWS // STEP, step, 0)

    tab_in, held_in, q_in, res_in, com_in = {}, {}, {}, {}, {}

    def fetch_block(offset):
        tab_in[offset].wait_recv()
        held_in[offset].wait_recv()
        q_in[offset].wait_recv()

    def send_pair(number):
        return (
            send(send_n.at[number], recv_n.at[number], S_PAIR_N + number, S_PAIR_N + number, 1),
            send(send_ml.at[number], recv_ml.at[number], S_PAIR_ML + number, S_PAIR_ML + number, 1),
        )

    def factors(tile, number):
        half = z if number == 0 else 1 - z
        return pltpu.roll(tile, lax.rem(PAIR - half * ROWS, PAIR), 1)

    cross_ml = []

    def merge_pair(number, incoming):
        for copy in incoming:
            copy.wait_recv()
        mine, other = keep_ml[number], recv_ml[number]
        high = jnp.maximum(mine, other)
        left, right = jnp.exp(mine - high), jnp.exp(other - high)
        total = mine * pltpu.roll(left, HD, 1) + other * pltpu.roll(right, HD, 1)
        keep_ml[number] = jnp.where(lane < HD, high, total)
        if number == 1:
            xs_ml[...] = keep_ml[0] + keep_ml[1]
            cross_ml.append(send(xs_ml, xr_ml, S_X_ML, S_X_ML, 2))
        left, right = factors(left, number), factors(right, number)
        for row in range(ROWS):
            merged = keep_n[number, row] * pair_columns(left[:, row : row + 1]) + recv_n[number, row].astype(
                F32
            ) * pair_columns(right[:, row : row + 1])
            keep_n[number, row] = merged
            xs_n[number, row] = merged.astype(BF16)
        return send(xs_n.at[number], xr_n.at[1 - number], S_X_N + number, S_X_N + 1 - number, 2)

    pl.semaphore_wait(barrier, 3 + digits)
    know(0)
    for offset in (2, 1):
        q_in[offset] = send(q_hbm, qraw.at[dp], S_Q + offset - 1, S_Q + offset - 1, offset)
    for offset in (2, 3, 1):
        tab_in[offset] = send(tab_hbm, tabs.at[dp], S_TAB + offset - 1, S_TAB + offset - 1, offset)
        held_in[offset] = send(held_hbm, helds.at[dp], S_HELD + offset - 1, S_HELD + offset - 1, offset)
    for number in (L_IDS, L_WEIGHTS, L_RES, L_MGAIN, L_AGAIN):
        loads[number].wait()
    combine_rows(ids, weights, comown, block, slots)
    comall[block] = comown[...]
    for which, gain in enumerate((mgain, again)):
        whole = gain[...].reshape(1, NDP * width)
        for k in range(NDP):
            gains[which, k] = whole[:, width * k : width * k + width]
    for k in range(NDP):
        resblk[k] = resraw[:, width * k : width * k + width]
    resall[block] = resblk[dp]
    for number in (L_TAB, L_HELD, L_Q, L_POOL):
        loads[number].wait()
    run_block(0, 0, keep_n, keep_ml)
    fetch_block(1)
    run_block(1, 0, send_n, send_ml)
    pair_in = [send_pair(0)]
    know(1)
    fetch_block(2)
    cross = group_peer(z, c, 2)
    q_in[3] = send(qraw.at[cross], qraw.at[cross], S_Q + 2, S_Q + 2, 1)
    for offset in (2, 3, 1):
        peer = group_peer(z, c, offset)
        res_in[offset] = send(resblk.at[peer], resall.at[block], S_RES + offset - 1, S_RES + offset - 1, offset)
        com_in[offset] = send(comown, comall.at[block], S_COM + offset - 1, S_COM + offset - 1, offset)
    cross_in = [merge_pair(0, pair_in[0])]
    know(2)
    fetch_block(3)
    run_block(3, 1, send_n, send_ml)
    pair_in.append(send_pair(1))
    know(3)
    run_block(2, 1, keep_n, keep_ml)
    cross_in.append(merge_pair(1, pair_in[1]))
    cross_ml[0].wait_recv()
    loads[L_SINK].wait()
    mine, other, sink = xs_ml[...], xr_ml[...], sink_columns(sinks[...])
    top = jnp.maximum(jnp.maximum(mine, other), sink)
    left, right = jnp.exp(mine - top), jnp.exp(other - top)
    total = mine * pltpu.roll(left, HD, 1) + other * pltpu.roll(right, HD, 1)
    below = pltpu.roll(total, HD, 1) + jnp.exp(sink - top)
    left, right = left / below, right / below
    for number in (1, 0):
        cross_in[1 - number].wait_recv()
        one, two = factors(left, number), factors(right, number)
        half = z if number == 0 else 1 - z
        for row in range(ROWS):
            attention = keep_n[number, row] * pair_columns(one[:, row : row + 1]) + xr_n[number, row].astype(
                F32
            ) * pair_columns(two[:, row : row + 1])
            start = pl.multiple_of((half * ROWS + row) * (HEADS // 2), HEADS // 2)
            att[pl.ds(start, HEADS // 2), :] = attention
    for pair in range(HEADS // 2):
        lhs[c, :, PAIR * pair : PAIR * pair + PAIR] = att[pl.ds(pair, 2 * ROWS, stride=HEADS // 2), :].astype(BF16)
    lhs_in = send(lhs.at[c], lhs.at[c], S_LHS, S_LHS, 1)
    for digit in range(4, digits):
        know(digit)
    for offset in (1, 2, 3):
        res_in[offset].wait_recv()
        com_in[offset].wait_recv()
    residual = jnp.concatenate([resall[d].astype(F32) for d in range(NDP)], axis=0)
    share = jnp.concatenate([comall[d] for d in range(NDP)], axis=0)
    picks = (share > 0).astype(F32).T.astype(BF16)
    loads[L_OW].wait()
    lhs_in.wait_recv()
    rows = jnp.concatenate([lhs[0], lhs[1]], axis=0)
    projected = lax.dot_general(rows, ow[...], (((1,), (1,)), ((), ())), preferred_element_type=F32)
    stream[z] = (residual + projected.astype(BF16).astype(F32)).astype(BF16)
    stream_in = send(stream.at[z], stream.at[z], S_STREAM, S_STREAM, 2)
    own = stream[z].astype(F32)
    group_rows = own.shape[0]
    diagonal = lax.broadcasted_iota(jnp.int32, (group_rows, 128), 0) == lax.broadcasted_iota(
        jnp.int32, (group_rows, 128), 1
    )
    square = jnp.sum(own * own, axis=1, keepdims=True)
    sums[dp] = jnp.broadcast_to(
        jnp.sum(jnp.where(diagonal, square, 0.0), axis=0, keepdims=True), sums.shape[1:]
    )
    sum_in = [
        send(sums.at[dp], sums.at[dp], S_SUM + offset - 1, S_SUM + offset - 1, offset) for offset in (2, 3, 1)
    ]
    for copy in sum_in:
        copy.wait_recv()
    square = (sums[0] + sums[1] + sums[2] + sums[3])[:1]
    square = jnp.sum(jnp.where(diagonal, square, 0.0), axis=1, keepdims=True)
    scale = lax.rsqrt(square / (NDP * width) + EPSILON)
    stream_in.wait_recv()
    for j in range(2):
        rows = (stream[j].astype(F32) * scale * gains[0, 2 * j + c]).astype(BF16)
        picked = jnp.dot(picks, rows, preferred_element_type=F32).astype(BF16)
        outbox[j] = picked.reshape(count, slots, width)

    def partner(place, sign):
        dy = 2 * lax.rem(lax.div(place, 8), 2) + lax.div(place, 16)
        dz, dx = lax.rem(lax.div(place, 4), 2), lax.rem(place, 4)
        at_z = lax.rem(lax.div(expert, 16) + dz, 2)
        at_y = lax.rem(lax.rem(lax.div(expert, 4), 4) + sign * dy + 4, 4)
        at_x = lax.rem(lax.rem(expert, 4) + sign * dx + 4, 4)
        return 16 * at_z + 4 * at_y + at_x

    def dispatch(place):
        to = partner(place, 1)
        return remote(outbox.at[:, to], arr.at[c, :, place], (d_send, d_recv), place, place, (dp, to))

    def forward(place):
        return remote(
            arr.at[c, :, place], arr.at[c, :, place], (f_send, f_recv), place, place,
            (group_peer(z, c, 1), expert),
        )

    def giveback(j, place):
        to = partner(place, -1)
        return remote(
            rbuf.at[j, place], ret.at[j, expert], (r_send.at[j], r_recv.at[j]), place, place, (dp, to)
        )

    def each(first, last, act):
        def step(place, carry):
            act(place)
            return carry

        lax.fori_loop(first, last, step, 0)

    batch = count // BATCHES
    batch_rows = batch * slots

    def pass_on(place):
        dispatch(place).wait_recv()
        forward(place).start()

    def project(first_place, half, first):
        for j in range(2):
            rows = arr[half, j, first_place : first_place + batch].reshape(batch_rows, width)
            for total, weight in ((gate, wg), (up, wu)):
                value = jnp.dot(rows, weight[2 * j + half], preferred_element_type=F32)
                if first and j == 0:
                    total[...] = value
                else:
                    total[...] += value

    def apply_experts(number):
        first_place = number * batch
        project(first_place, c, True)
        each(first_place, first_place + batch, lambda place: forward(place).wait_recv())
        project(first_place, 1 - c, False)
        gated = jnp.minimum(gate[...], LIMIT)
        lifted = jnp.clip(up[...], -LIMIT, LIMIT)
        activated = (gated * jax.nn.sigmoid(1.702 * gated) * (lifted + 1.0)).astype(BF16)

        def down(k):
            return lax.dot_general(activated, wd[k], (((1,), (1,)), ((), ())), preferred_element_type=F32)

        incoming = []
        for j in range(2):
            osend[number, j] = down(2 * j + 1 - c).astype(BF16)
            at = S_OUT + 2 * number + j
            incoming.append(send(osend.at[number, j], orecv.at[number, j], at, at, 1))
        for j in range(2):
            kept[j] = down(2 * j + c)
        return incoming

    def give_back(number, incoming):
        first_place = number * batch
        for j in range(2):
            incoming[j].wait_recv()
            total = (kept[j] + orecv[number, j].astype(F32)).astype(BF16)
            rbuf[j, first_place : first_place + batch] = total.reshape(batch, slots, width)
            each(max(first_place, 1), first_place + batch, lambda place: giveback(j, place).start())

    know(digits)
    each(1, count, lambda place: dispatch(place).start())
    for j in range(2):
        arr[c, j, 0] = outbox[j, expert]
    forward(0).start()
    for number in (L_GATE, L_UP, L_DOWN):
        loads[number].wait()
    incoming = None
    for number in range(BATCHES):
        each(max(1, batch * number), batch * (number + 1), pass_on)
        if number > 0:
            give_back(number - 1, incoming)
        incoming = apply_experts(number)
    give_back(BATCHES - 1, incoming)
    for j in range(2):
        ret[j, expert] = rbuf[j, 0]

    high = share.astype(BF16)
    low = (share - high.astype(F32)).astype(BF16)
    both = jnp.concatenate([high, low], axis=0)
    part_in = []
    for j in range(2):
        each(1, count, lambda place: giveback(j, place).wait_recv())
        mixed = jnp.dot(both, ret[j].reshape(count * slots, width), preferred_element_type=F32)
        part_s[j] = (mixed[:group_rows] + mixed[group_rows:]).astype(BF16)
        part_in.append(send(part_s.at[j], part_r.at[j], S_PART + j, S_PART + j, 2))
    loads[L_QKV].wait()
    next_in = []
    qkv = jnp.zeros((group_rows, wq.shape[2]), F32)
    squares = jnp.zeros((group_rows, 1), F32)

    def project_next(half, j, qkv, squares):
        k = 2 * j + half
        rows = nextb[half, j].astype(F32)
        nextf[k] = rows
        squares += jnp.sum(rows * rows, axis=1, keepdims=True)
        qkv += jnp.dot((rows * gains[1, k]).astype(BF16), wq[k], preferred_element_type=F32)
        return qkv, squares

    for j in range(2):
        part_in[j].wait_recv()
        moe_out = part_s[j].astype(F32) + part_r[j].astype(F32)
        nextb[c, j] = (stream[j].astype(F32) + moe_out).astype(BF16)
        next_in.append(send(nextb.at[c, j], nextb.at[c, j], S_NEXT + j, S_NEXT + j, 1))
        qkv, squares = project_next(c, j, qkv, squares)
    for j in range(2):
        next_in[j].wait_recv()
        qkv, squares = project_next(1 - c, j, qkv, squares)
    qkv = qkv * lax.rsqrt(squares / (NDP * width) + EPSILON)
    columns = qkv.shape[1]
    for d in range(NDP):
        qbuf[d] = qkv[ROWS * d : ROWS * d + ROWS].astype(BF16)
    own_columns = pl.ds(pl.multiple_of(dp * columns, 128), columns)
    qkv_in = []
    for offset in (2, 3, 1):
        peer = group_peer(z, c, offset)
        theirs = lax.rem(peer, 2) * 2 + lax.div(peer, 2)
        qkv_in.append(
            send(qbuf.at[theirs], qkv_out.at[:, own_columns], S_QKV + offset - 1, S_QKV + offset - 1, offset)
        )
    qkv_out[:, own_columns] = qbuf[block]
    start = pl.multiple_of(block * ROWS, ROWS)
    for k in range(NDP):
        next_out[:, width * k : width * k + width] = nextf[k, pl.ds(start, ROWS), :].astype(BF16)

    def all_sent(place):
        dispatch(place).wait_send()
        for j in range(2):
            giveback(j, place).wait_send()

    each(1, count, all_sent)
    each(0, count, lambda place: forward(place).wait_send())
    for copy in sent:
        copy.wait_send()
    for copy in qkv_in:
        copy.wait_recv()


def layer_call(args, count):
    (queries, kv_pool, page_table, held_tokens, sinks, residual, route_ids, route_weights, moe_gain,
     w_gate, w_up, w_down, o_weight, attn_gain, qkv_weight) = args
    width = residual.shape[1] // NDP
    hidden = w_gate.shape[2]
    columns = qkv_weight.shape[1]
    slots = NDP * (2 * ROWS * TOP // count)
    group_rows = NDP * ROWS
    all_slots = count * slots
    hbm = pl.BlockSpec(memory_space=pltpu.HBM)
    out = pl.BlockSpec(memory_space=pltpu.VMEM)
    vmem, dma = pltpu.VMEM, pltpu.SemaphoreType.DMA
    pairs = (2, ROWS, HEADS // 2, PAIR)
    return pl.pallas_call(
        layer_kernel,
        out_shape=(
            jax.ShapeDtypeStruct((ROWS, NDP * width), BF16),
            jax.ShapeDtypeStruct((ROWS, NDP * columns), BF16),
        ),
        in_specs=[hbm] * 15,
        out_specs=(out, out),
        scratch_shapes=[
            vmem(kv_pool.shape, BF16),
            vmem((width, HEADS * HD), BF16),
            vmem((NDP, width, hidden), BF16),
            vmem((NDP, width, hidden), BF16),
            vmem((NDP, width, hidden), BF16),
            vmem((NDP, width, columns), BF16),
            pltpu.SMEM((NDP,) + page_table.shape, jnp.int32),
            pltpu.SMEM((NDP, NDP, ROWS), jnp.int32),
            pltpu.SMEM((TOP, ROWS), jnp.int32),
            pltpu.SMEM((TOP, ROWS), F32),
            vmem((1, HEADS), F32),
            vmem((NDP * width,), F32),
            vmem((NDP * width,), F32),
            vmem((2, NDP, 1, width), F32),
            vmem((NDP, ROWS, HEADS * HD), BF16),
            vmem((ROWS * HEADS // 2, PAIR), F32),
            vmem((ROWS, NDP * width), BF16),
            vmem((NDP, ROWS, width), BF16),
            vmem((NDP, ROWS, width), BF16),
            vmem((ROWS, all_slots), F32),
            vmem((NDP, ROWS, all_slots), F32),
            vmem(pairs, F32),
            vmem((2, HEADS, PAIR), F32),
            vmem(pairs, BF16),
            vmem((2, HEADS, PAIR), F32),
            vmem(pairs, BF16),
            vmem((2, HEADS, PAIR), F32),
            vmem(pairs, BF16),
            vmem((HEADS, PAIR), F32),
            vmem(pairs, BF16),
            vmem((HEADS, PAIR), F32),
            vmem((2 * ROWS * HEADS // 2, PAIR), F32),
            vmem((2, 2 * ROWS, HEADS * HD), BF16),
            vmem((2, group_rows, width), BF16),
            vmem((NDP, 8, 128), F32),
            vmem((2, count, slots, width), BF16),
            vmem((2, 2, count, slots, width), BF16),
            vmem((all_slots // BATCHES, hidden), F32),
            vmem((all_slots // BATCHES, hidden), F32),
            vmem((BATCHES, 2, all_slots // BATCHES, width), BF16),
            vmem((BATCHES, 2, all_slots // BATCHES, width), BF16),
            vmem((2, all_slots // BATCHES, width), F32),
            vmem((2, count, slots, width), BF16),
            vmem((2, count, slots, width), BF16),
            vmem((2, group_rows, width), BF16),
            vmem((2, group_rows, width), BF16),
            vmem((2, 2, group_rows, width), BF16),
            vmem((NDP, group_rows, width), F32),
            vmem((NDP, ROWS, columns), BF16),
            dma((15,)),
            dma((N_SEM,)),
            dma((N_SEM,)),
            dma((count,)),
            dma((count,)),
            dma((count,)),
            dma((count,)),
            dma((2, count)),
            dma((2, count)),
            pltpu.SemaphoreType.REGULAR((count.bit_length() - 1,)),
        ],
        compiler_params=pltpu.CompilerParams(collective_id=0, has_side_effects=True, vmem_limit_bytes=44 * 2**20),
        name="layer",
    )(*[pltpu.with_memory_space_constraint(x, pltpu.HBM) for x in (
        queries,
        kv_pool,
        page_table,
        held_tokens.T,
        sinks.reshape(1, HEADS),
        residual,
        route_ids.T,
        route_weights.T,
        moe_gain,
        w_gate.reshape(NDP, width, hidden),
        w_up.reshape(NDP, width, hidden),
        w_down[0].T.reshape(NDP, width, hidden),
        o_weight.T,
        attn_gain,
        qkv_weight.reshape(NDP, width, columns),
    )])


def body(*args):
    return layer_call(args, lax.axis_size("expert"))


def solution(mesh):
    in_specs = (
        P(("dp", "expert"), None),
        P(("dp", "expert"), None, None),
        P(("dp", "expert"), None, None),
        P(("dp", "expert"), None),
        P(),
        P(("dp", "expert"), None),
        P(("dp", "expert"), None),
        P(("dp", "expert"), None),
        P(),
        P("expert", None, "dp"),
        P("expert", None, "dp"),
        P("expert", "dp", None),
        P(None, "dp"),
        P(),
        P(None, "dp"),
    )
    out_specs = (P(("dp", "expert"), None), P(("dp", "expert"), None))
    return jax.shard_map(body, mesh=mesh, in_specs=in_specs, out_specs=out_specs, check_vma=False)
```
